32 devices in a mesh: rep: 4 (over y, x), shard: 8 (over z, core).
Axes of the slice: x: 2, y: 2, z: 4, core: 2. Of those that a mesh axis runs over, the one named last changes fastest.
Arguments:
- tokens: bfloat16 [32, 512, 1024], P(('rep', 'shard')), may hold values from -6 to 6
- cotangent: bfloat16 [32, 512, 1024], P(('rep', 'shard')), may hold values from -6 to 6
- lengths: int32 [32], replicated, may hold values from 1 to 512, 12288 in all
- slot_sequence: int32 [32], P(('rep', 'shard')), may hold values from 0 to 31, each once
- step_count: int32 [1], replicated, may hold values from 1 to 20
- learn_rate: float32 [1], replicated, may hold values from 0.1 to 1
- attention_in: float32 [1024, 3, 1024], P('shard'), may hold values from -0.1875 to 0.1875
- attention_in_first: float32 [1024, 3, 1024], P('shard'), may hold values from -36 to 36
- attention_in_second: float32 [1024, 3, 1024], P('shard'), may hold values from 20 to 400
- attention_out: float32 [1024, 1024], P('shard'), may hold values from -1.5 to 1.5
- attention_out_first: float32 [1024, 1024], P('shard'), may hold values from -36 to 36
- attention_out_second: float32 [1024, 1024], P('shard'), may hold values from 20 to 400
- gate_up_weight: float32 [1024, 2, 2816], P('shard'), may hold values from -0.1875 to 0.1875
- gate_up_first: float32 [1024, 2, 2816], P('shard'), may hold values from -36 to 36
- gate_up_second: float32 [1024, 2, 2816], P('shard'), may hold values from 20 to 400
- down_weight: float32 [2816, 1024], P('shard'), may hold values from -0.109375 to 0.109375
- down_first: float32 [2816, 1024], P('shard'), may hold values from -36 to 36
- down_second: float32 [2816, 1024], P('shard'), may hold values from 20 to 400
Outputs:
- output: bfloat16 [32, 512, 1024], P(('rep', 'shard'))
- input_grad: float32 [32, 512, 1024], P(('rep', 'shard'))
- attention_in_grad: float32 [1024, 3, 1024], P('shard')
- attention_in_new: float32 [1024, 3, 1024], P('shard')
- attention_in_first_new: float32 [1024, 3, 1024], P('shard')
- attention_in_second_new: float32 [1024, 3, 1024], P('shard')
- attention_out_grad: float32 [1024, 1024], P('shard')
- attention_out_new: float32 [1024, 1024], P('shard')
- attention_out_first_new: float32 [1024, 1024], P('shard')
- attention_out_second_new: float32 [1024, 1024], P('shard')
- gate_up_grad: float32 [1024, 2, 2816], P('shard')
- gate_up_new: float32 [1024, 2, 2816], P('shard')
- gate_up_first_new: float32 [1024, 2, 2816], P('shard')
- gate_up_second_new: float32 [1024, 2, 2816], P('shard')
- down_grad: float32 [2816, 1024], P('shard')
- down_new: float32 [2816, 1024], P('shard')
- down_first_new: float32 [2816, 1024], P('shard')
- down_second_new: float32 [2816, 1024], P('shard')
The draws below stay inside these ranges and needn't reach their ends.
Inputs may be any that keep to these rules, and one draw needn't show every extreme that they name: `lengths`: lengths of the sequences by number; they add up to 3 / 4 of 16384, and one is exactly 512. `slot_sequence`: A permutation of the 32 sequence numbers.
All inputs are finite; a program needn't handle non-finite values.
Results may differ from the reference program's by a relative error of at most 0.025.
The reference program's roundings to bfloat16 on the way count: a program that leaves them out, or rounds other values in their place, can miss the bound.
Values may be sent and summed in bfloat16 or wider, within the bound.
A program may use at most 256 MiB of HBM per device.

```python
import math
import jax
import jax.numpy as jnp
import numpy as np
from jax import lax

D = 1024
HD = 64
FF = 2816
LEN = 512
NSEQ = 32


def block_scale(key, extent, cuts, low, high):
    gain, own = 1.0, jax.random.fold_in(key, 6)
    for dim, parts in cuts:
        heights = jnp.exp(jax.random.uniform(jax.random.fold_in(own, dim), (parts,), jnp.float32, low / len(cuts), high / len(cuts)))
        gain = gain * jnp.repeat(heights, extent[dim] // parts).reshape([-1 if axis == dim else 1 for axis in range(len(extent))])
    return gain


def profile(amount, total, most, lean):
    weights = [(1 << 20) // math.isqrt(standing ** lean) + 1 for standing in range(2, amount + 1)]
    spare, holding = total - most - (amount - 1), [1] * (amount - 1)
    while spare > 0:
        free = [i for i in range(amount - 1) if holding[i] < most]
        mass, remaining = sum([weights[i] for i in free]), spare
        for i in free:
            addition = min(most - holding[i], max(1, remaining * weights[i] // mass), spare)
            holding[i] = holding[i] + addition
            spare = spare - addition
    return np.array([most] + holding)


def uneven_parts(key, amount, total, limit, lean):
    if amount == 2:
        one = jax.random.randint(key, (), max(1, total - limit), min(limit, total - 1) + 1)
        return jnp.stack([one, total - one])
    tallies = jnp.asarray(profile(amount, total, limit, lean), jnp.int32)
    couples = (amount - 1) // 2
    source_of, receiver = tallies[1:1 + 2 * couples:2], tallies[2:2 + 2 * couples:2]
    slack = jnp.minimum(source_of - 1, limit - receiver)
    passed = jax.random.randint(jax.random.fold_in(key, 1), (couples,), 0, 1 << 20) % (slack + 1)
    tallies = tallies.at[1:1 + 2 * couples:2].set(source_of - passed).at[2:2 + 2 * couples:2].set(receiver + passed)
    return tallies[jax.random.permutation(jax.random.fold_in(key, 2), amount)]


def bell_draw(own_key, shape, spread, limit, cuts=(), held_as=jnp.bfloat16):
    loudness = block_scale(own_key, shape, cuts, -0.22, 0.18) if cuts else 1.0
    drawn = jax.random.normal(own_key, shape, jnp.float32) * spread * loudness
    return jnp.minimum(jnp.maximum(drawn, -limit), limit).astype(held_as)


def setup_inputs(seed: int = 0) -> dict:
    seeds = jax.random.split(jax.random.key(seed), 19)
    return {
        "tokens": bell_draw(seeds[0], (NSEQ, LEN, D), 1.0, 6.0, ((0, 32),)),
        "cotangent": bell_draw(seeds[1], (NSEQ, LEN, D), 1.0, 6.0, ((0, 32),)),
        "lengths": uneven_parts(seeds[2], NSEQ, NSEQ * LEN * 3 // 4, LEN, 1).astype(jnp.int32),
        "slot_sequence": jax.random.permutation(seeds[3], NSEQ).astype(jnp.int32),
        "step_count": jax.random.randint(seeds[4], (1,), 1, 21).astype(jnp.int32),
        "learn_rate": jnp.clip(jnp.exp(jax.random.uniform(seeds[5], (1,), jnp.float32, math.log(0.1), math.log(1.0))), 0.1, 1.0),
        "attention_in": bell_draw(seeds[6], (D, 3, D), D ** -0.5, 0.1875, ((0, 8),), jnp.float32),
        "attention_in_first": bell_draw(seeds[7], (D, 3, D), 6.0, 36.0, ((0, 8),), jnp.float32),
        "attention_in_second": jnp.clip(jnp.exp(math.log(400.0) - 2.9957323 * jax.random.uniform(seeds[8], (D, 3, D), jnp.float32) ** block_scale(seeds[8], (D, 3, D), ((0, 8),), -0.2, 0.2)), 20.0, 400.0),
        "attention_out": bell_draw(seeds[9], (D, D), (D // 64) ** -0.5, 1.5, ((0, 8),), jnp.float32),
        "attention_out_first": bell_draw(seeds[10], (D, D), 6.0, 36.0, ((0, 8),), jnp.float32),
        "attention_out_second": jnp.clip(jnp.exp(math.log(400.0) - 2.9957323 * jax.random.uniform(seeds[11], (D, D), jnp.float32) ** block_scale(seeds[11], (D, D), ((0, 8),), -0.2, 0.2)), 20.0, 400.0),
        "gate_up_weight": bell_draw(seeds[12], (D, 2, FF), D ** -0.5, 0.1875, ((0, 8),), jnp.float32),
        "gate_up_first": bell_draw(seeds[13], (D, 2, FF), 6.0, 36.0, ((0, 8),), jnp.float32),
        "gate_up_second": jnp.clip(jnp.exp(math.log(400.0) - 2.9957323 * jax.random.uniform(seeds[14], (D, 2, FF), jnp.float32) ** block_scale(seeds[14], (D, 2, FF), ((0, 8),), -0.2, 0.2)), 20.0, 400.0),
        "down_weight": bell_draw(seeds[15], (FF, D), FF ** -0.5, 0.109375, ((0, 8),), jnp.float32),
        "down_first": bell_draw(seeds[16], (FF, D), 6.0, 36.0, ((0, 8),), jnp.float32),
        "down_second": jnp.clip(jnp.exp(math.log(400.0) - 2.9957323 * jax.random.uniform(seeds[17], (FF, D), jnp.float32) ** block_scale(seeds[17], (FF, D), ((0, 8),), -0.2, 0.2)), 20.0, 400.0),
    }


@jax.custom_vjp
def low(v):
    return lax.optimization_barrier(v.astype(jnp.bfloat16)).astype(jnp.float32)

@jax.custom_vjp
def low_back(v):
    return v

def low_keep(v):
    return (low(v), None)

def low_pass(kept, grad):
    return (grad,)

def back_keep(v):
    return (v, None)

def back_low(kept, grad):
    return (low(grad),)
low.defvjp(low_keep, low_pass)
low_back.defvjp(back_keep, back_low)
norm_eps = 1e-05
beta_first = 0.9
beta_second = 0.95
adam_eps = 1e-08
weight_decay = 0.1
rope_base = 10000.0
masked_score = -1e+30
highest = lax.Precision.HIGHEST

def layer_norm(values):
    centered = values - lax.optimization_barrier(jnp.mean(values, axis=-1, keepdims=True))
    inverse = lax.rsqrt(lax.optimization_barrier(jnp.mean(centered * centered, axis=-1, keepdims=True)) + norm_eps)
    return centered * inverse

def rope_tables(position_count, head_size):
    half_size = head_size // 2
    frequency = rope_base ** (-(jnp.arange(half_size, dtype=jnp.float32) * 2.0 / head_size))
    angles = jnp.arange(position_count, dtype=jnp.float32)[:, None] * frequency[None, :]
    angles = jnp.concatenate([angles, angles], axis=1)
    return (jnp.cos(angles)[:, None, :], jnp.sin(angles)[:, None, :])

def rotate(values, cosine_table, sine_table):
    half_size = values.shape[-1] // 2
    turned = jnp.concatenate([-values[..., half_size:], values[..., :half_size]], axis=-1)
    return values * cosine_table + turned * sine_table

def attend_one(pieces):
    queries, rotated_keys, values_low, length = pieces
    position_count, head_size = (queries.shape[0], queries.shape[-1])
    raw_scores = low_back(jnp.einsum('qhd,khd->hqk', queries, rotated_keys, precision=highest))
    position = jnp.arange(position_count)
    allowed = (position[None, :] <= position[:, None]) & (position[None, :] < length)
    scores = jnp.where(allowed[None], raw_scores * head_size ** (-0.5), masked_score)
    probability = jax.nn.softmax(scores, axis=-1)
    return jnp.einsum('hqk,khd->qhd', low(probability), values_low, precision=highest)

def forward(inputs, attention_in, attention_out, gate_up_weight, down_weight, alive_rows, slot_length):
    group_count, position_count, feature_count = inputs.shape
    head_count = feature_count // HD
    in_low = low(attention_in)
    out_low = low(attention_out)
    gate_up_low = low(gate_up_weight)
    down_low = low(down_weight)
    first_input = low(layer_norm(inputs))
    projected = jnp.einsum('gld,dke->glke', first_input, in_low, precision=highest)
    shaped = (group_count, position_count, head_count, HD)
    cosine_table, sine_table = rope_tables(position_count, HD)
    queries = low(rotate(low_back(projected[:, :, 0]).reshape(shaped), cosine_table, sine_table))
    rotated_keys = low(rotate(low_back(projected[:, :, 1]).reshape(shaped), cosine_table, sine_table))
    values_low = low_back(low(projected[:, :, 2])).reshape(shaped)
    mixed_heads = lax.map(jax.checkpoint(attend_one), (queries, rotated_keys, values_low, slot_length))
    mixed_low = low_back(low(mixed_heads.reshape(group_count, position_count, feature_count)))
    residual = inputs + low_back(jnp.einsum('gle,ed->gld', mixed_low, out_low, precision=highest))
    second_input = low(layer_norm(residual))
    gate_up = jnp.einsum('gld,dkf->glkf', second_input, gate_up_low, precision=highest)
    gate_value = low_back(gate_up[:, :, 0])
    up_value = low_back(gate_up[:, :, 1])
    hidden_low = low(jax.nn.silu(gate_value) * up_value)
    result = residual + low_back(jnp.einsum('glf,fd->gld', hidden_low, down_low, precision=highest))
    return result * alive_rows[..., None]

def adam_update(weight, first, second, gradient, step_count, learn_rate):
    steps_taken = step_count[0].astype(jnp.float32)
    first_new = beta_first * first + (1.0 - beta_first) * gradient
    second_new = beta_second * second + (1.0 - beta_second) * gradient * gradient
    first_hat = first_new / (1.0 - beta_first ** steps_taken)
    second_hat = second_new / (1.0 - beta_second ** steps_taken)
    weight_new = weight - learn_rate[0] * (first_hat / (jnp.sqrt(second_hat) + adam_eps) + weight_decay * weight)
    return (gradient, weight_new, first_new, second_new)

def reference(tokens, cotangent, lengths, slot_sequence, step_count, learn_rate, attention_in, attention_in_first, attention_in_second, attention_out, attention_out_first, attention_out_second, gate_up_weight, gate_up_first, gate_up_second, down_weight, down_first, down_second):
    slot_total, position_count, feature_count = tokens.shape
    group_size = math.gcd(slot_total, max(1, 4096 // position_count))
    group_count = slot_total // group_size
    slot_length = lengths[slot_sequence].astype(jnp.int32)
    alive_rows = (jnp.arange(position_count)[None, :] < slot_length[:, None]).astype(jnp.float32)
    shaped = (group_count, group_size, position_count, feature_count)
    inputs = tokens.astype(jnp.float32).reshape(shaped)
    upstream = cotangent.astype(jnp.float32).reshape(shaped)
    alive_groups = alive_rows.reshape(group_count, group_size, position_count)
    length_groups = slot_length.reshape(group_count, group_size)

    def one_group(carry, item):
        group_inputs, group_upstream, group_alive, group_length = item

        def apply_layer(values, w_in, w_out, w_gate_up, w_down):
            return forward(values, w_in, w_out, w_gate_up, w_down, group_alive, group_length)
        result, pull = jax.vjp(apply_layer, group_inputs, attention_in, attention_out, gate_up_weight, down_weight)
        grads = pull(group_upstream)
        carry = (carry[0] + grads[1], carry[1] + grads[2], carry[2] + grads[3], carry[3] + grads[4])
        return (carry, (result.astype(jnp.bfloat16), grads[0]))
    start = (jnp.zeros_like(attention_in), jnp.zeros_like(attention_out), jnp.zeros_like(gate_up_weight), jnp.zeros_like(down_weight))
    totals, stacked = lax.scan(one_group, start, (inputs, upstream, alive_groups, length_groups))
    output = stacked[0].reshape(slot_total, position_count, feature_count)
    input_grad = stacked[1].reshape(slot_total, position_count, feature_count)
    in_grad, in_new, in_first, in_second = adam_update(attention_in, attention_in_first, attention_in_second, totals[0], step_count, learn_rate)
    out_grad, out_new, out_first, out_second = adam_update(attention_out, attention_out_first, attention_out_second, totals[1], step_count, learn_rate)
    gu_grad, gu_new, gu_first, gu_second = adam_update(gate_up_weight, gate_up_first, gate_up_second, totals[2], step_count, learn_rate)
    dn_grad, dn_new, dn_first, dn_second = adam_update(down_weight, down_first, down_second, totals[3], step_count, learn_rate)
    return (output, input_grad, in_grad, in_new, in_first, in_second, out_grad, out_new, out_first, out_second, gu_grad, gu_new, gu_first, gu_second, dn_grad, dn_new, dn_first, dn_second)
```

```python
import jax
import jax.numpy as jnp
from jax import lax
from jax.sharding import PartitionSpec as P

HD = 64


norm_eps = 1e-05
beta_first = 0.9
beta_second = 0.95
adam_eps = 1e-08
weight_decay = 0.1
rope_base = 10000.0
masked_score = -1e30


def layer_norm(values):
    centered = values - jnp.mean(values, axis=-1, keepdims=True)
    inverse = lax.rsqrt(jnp.mean(centered * centered, axis=-1, keepdims=True) + norm_eps)
    return (centered * inverse, inverse)


def norm_back(normed, inverse, upstream):
    mean_grad = jnp.mean(upstream, axis=-1, keepdims=True)
    mean_dot = jnp.mean(upstream * normed, axis=-1, keepdims=True)
    return inverse * (upstream - mean_grad - normed * mean_dot)


def rope_tables(position_count, head_size):
    half_size = head_size // 2
    frequency = rope_base ** (-(jnp.arange(half_size, dtype=jnp.float32) * 2.0 / head_size))
    angles = jnp.arange(position_count, dtype=jnp.float32)[:, None] * frequency[None, :]
    angles = jnp.concatenate([angles, angles], axis=1)
    return (jnp.cos(angles)[:, None, :], jnp.sin(angles)[:, None, :])


def rotate(values, cosine_table, sine_table):
    half_size = values.shape[-1] // 2
    turned = jnp.concatenate([-values[..., half_size:], values[..., :half_size]], axis=-1)
    return values * cosine_table + turned * sine_table


def masked_scores(queries, rotated_keys, length):
    position_count, head_size = (queries.shape[0], queries.shape[-1])
    scores = jnp.einsum(
        "qhd,khd->hqk", queries, rotated_keys, preferred_element_type=jnp.float32
    ) * head_size ** (-0.5)
    position = jnp.arange(position_count)
    allowed = (position[None, :] <= position[:, None]) & (position[None, :] < length)
    return jnp.where(allowed[None], scores, masked_score)


def attend_forward(pieces):
    queries, rotated_keys, values_low, length = pieces
    scores = masked_scores(queries, rotated_keys, length)
    row_max = jnp.max(scores, axis=-1, keepdims=True)
    exponent = jnp.exp(scores - row_max)
    row_sum = jnp.sum(exponent, axis=-1, keepdims=True)
    weights = (exponent / row_sum).astype(jnp.bfloat16)
    mixed_heads = jnp.einsum(
        "hqk,khd->qhd", weights, values_low, preferred_element_type=jnp.float32
    )
    return (mixed_heads, row_max + jnp.log(row_sum))


def attend_backward(pieces):
    queries, rotated_keys, values_low, length, log_total, mixed_grad = pieces
    head_size = queries.shape[-1]
    scores = masked_scores(queries, rotated_keys, length)
    probability = jnp.exp(scores - log_total)
    value_grad = jnp.einsum(
        "hqk,qhd->khd",
        probability.astype(jnp.bfloat16),
        mixed_grad,
        preferred_element_type=jnp.float32,
    )
    probability_grad = jnp.einsum(
        "qhd,khd->hqk", mixed_grad, values_low, preferred_element_type=jnp.float32
    )
    inner_dot = jnp.sum(probability * probability_grad, axis=-1, keepdims=True)
    score_grad = (probability * (probability_grad - inner_dot) * head_size ** (-0.5)).astype(
        jnp.bfloat16
    )
    query_grad = jnp.einsum(
        "hqk,khd->qhd", score_grad, rotated_keys, preferred_element_type=jnp.float32
    )
    key_grad = jnp.einsum("hqk,qhd->khd", score_grad, queries, preferred_element_type=jnp.float32)
    return (query_grad, key_grad, value_grad)


def adam_update(weight, first, second, gradient, step_count, learn_rate):
    steps_taken = step_count[0].astype(jnp.float32)
    first_new = beta_first * first + (1.0 - beta_first) * gradient
    second_new = beta_second * second + (1.0 - beta_second) * gradient * gradient
    first_hat = first_new / (1.0 - beta_first**steps_taken)
    second_hat = second_new / (1.0 - beta_second**steps_taken)
    weight_new = weight - learn_rate[0] * (
        first_hat / (jnp.sqrt(second_hat) + adam_eps) + weight_decay * weight
    )
    return (gradient, weight_new, first_new, second_new)


def gather_full(local, rep_count, rep_index):
    rows = local.shape[0]
    flat = local.reshape(rows, -1)
    width = flat.shape[1] // rep_count
    piece = lax.dynamic_slice_in_dim(flat, rep_index * width, width, axis=1)
    column = lax.all_gather(piece, "shard", axis=0, tiled=True)
    return lax.all_gather(column, "rep", axis=0, tiled=False)


def reduce_full(partial):
    part = lax.psum_scatter(partial, "rep", scatter_dimension=0, tiled=False)
    part = lax.psum_scatter(part, "shard", scatter_dimension=0, tiled=True)
    pieces = lax.all_gather(part, "rep", axis=0, tiled=False)
    rows = pieces.shape[1]
    return jnp.transpose(pieces, (1, 0, 2)).reshape(rows, -1).astype(jnp.float32)


def shards(
    tokens,
    cotangent,
    lengths,
    slot_sequence,
    step_count,
    learn_rate,
    attention_in,
    attention_in_first,
    attention_in_second,
    attention_out,
    attention_out_first,
    attention_out_second,
    gate_up_weight,
    gate_up_first,
    gate_up_second,
    down_weight,
    down_first,
    down_second,
):
    slot_count, position_count, feature_count = tokens.shape
    row_total = slot_count * position_count
    head_count = feature_count // HD
    shaped = (slot_count, position_count, head_count, HD)
    inputs = tokens.astype(jnp.float32).reshape(row_total, feature_count)
    matches = jnp.arange(lengths.shape[0])[None, :] == slot_sequence[:, None]
    slot_length = jnp.sum(jnp.where(matches, lengths[None, :], 0), axis=1)
    alive_rows = (
        (jnp.arange(position_count)[None, :] < slot_length[:, None])
        .astype(jnp.float32)
        .reshape(row_total, 1)
    )
    cosine_table, sine_table = rope_tables(position_count, HD)
    in_local = attention_in.astype(jnp.bfloat16)
    out_local = attention_out.astype(jnp.bfloat16)
    gate_up_local = gate_up_weight.astype(jnp.bfloat16)
    down_local = down_weight.astype(jnp.bfloat16)
    rep_count = lax.axis_size("rep")
    rep_index = lax.axis_index("rep")
    in_full = gather_full(in_local, rep_count, rep_index)
    out_full = gather_full(out_local, rep_count, rep_index)
    gate_up_full = gather_full(gate_up_local, rep_count, rep_index)
    down_full = gather_full(down_local, rep_count, rep_index)
    normed_one, inverse_one = layer_norm(inputs)
    first_input = normed_one.astype(jnp.bfloat16)
    projected = jnp.einsum(
        "rd,qde->rqe", first_input, in_full, preferred_element_type=jnp.float32
    ).reshape(row_total, 3, feature_count)
    queries = rotate(projected[:, 0].reshape(shaped), cosine_table, sine_table).astype(jnp.bfloat16)
    rotated_keys = rotate(projected[:, 1].reshape(shaped), cosine_table, sine_table).astype(
        jnp.bfloat16
    )
    values_low = projected[:, 2].reshape(shaped).astype(jnp.bfloat16)
    mixed_heads, log_total = lax.map(
        attend_forward, (queries, rotated_keys, values_low, slot_length)
    )
    mixed_low = mixed_heads.reshape(row_total, feature_count).astype(jnp.bfloat16)
    residual = inputs + jnp.einsum(
        "rd,qde->rqe", mixed_low, out_full, preferred_element_type=jnp.float32
    ).reshape(row_total, feature_count)
    normed_two, inverse_two = layer_norm(residual)
    second_input = normed_two.astype(jnp.bfloat16)
    gate_up = jnp.einsum(
        "rd,qdf->rqf", second_input, gate_up_full, preferred_element_type=jnp.float32
    ).reshape(row_total, 2, -1)
    gate_value = gate_up[:, 0]
    up_value = gate_up[:, 1]
    sigmoid_gate = jax.nn.sigmoid(gate_value)
    hidden_low = (gate_value * sigmoid_gate * up_value).astype(jnp.bfloat16)
    result = residual + jnp.einsum(
        "rf,qfe->rqe", hidden_low, down_full, preferred_element_type=jnp.float32
    ).reshape(row_total, feature_count)
    output = (result * alive_rows).astype(jnp.bfloat16).reshape(tokens.shape)
    output_grad = cotangent.astype(jnp.float32).reshape(row_total, feature_count) * alive_rows
    result_grad_low = output_grad.astype(jnp.bfloat16)
    hidden_grad = jnp.einsum(
        "rqe,qfe->rf",
        result_grad_low.reshape(row_total, rep_count, -1),
        down_full,
        preferred_element_type=jnp.float32,
    )
    gate_grad = hidden_grad * up_value * sigmoid_gate * (1.0 + gate_value * (1.0 - sigmoid_gate))
    up_grad = hidden_grad * gate_value * sigmoid_gate
    gate_up_grad_low = (
        jnp.concatenate([gate_grad, up_grad], axis=1)
        .astype(jnp.bfloat16)
        .reshape(row_total, rep_count, -1)
    )
    second_input_grad = jnp.einsum(
        "rqf,qdf->rd", gate_up_grad_low, gate_up_full, preferred_element_type=jnp.float32
    )
    residual_grad = output_grad + norm_back(normed_two, inverse_two, second_input_grad)
    down_part = reduce_full(
        jnp.einsum(
            "rc,rqe->qce",
            hidden_low,
            result_grad_low.reshape(row_total, rep_count, -1),
            preferred_element_type=jnp.float32,
        ).astype(jnp.bfloat16)
    )
    gate_up_part = reduce_full(
        jnp.einsum(
            "rc,rqf->qcf", second_input, gate_up_grad_low, preferred_element_type=jnp.float32
        ).astype(jnp.bfloat16)
    ).reshape(gate_up_weight.shape)
    branch_grad = residual_grad.astype(jnp.bfloat16)
    mixed_grad = (
        jnp.einsum(
            "rqe,qde->rd",
            branch_grad.reshape(row_total, rep_count, -1),
            out_full,
            preferred_element_type=jnp.float32,
        )
        .astype(jnp.bfloat16)
        .reshape(shaped)
    )
    query_grad, key_grad, value_grad = lax.map(
        attend_backward, (queries, rotated_keys, values_low, slot_length, log_total, mixed_grad)
    )
    query_back = rotate(query_grad, cosine_table, -sine_table).reshape(row_total, feature_count)
    key_back = rotate(key_grad, cosine_table, -sine_table).reshape(row_total, feature_count)
    projected_grad = (
        jnp.concatenate([query_back, key_back, value_grad.reshape(row_total, feature_count)], axis=1)
        .astype(jnp.bfloat16)
        .reshape(row_total, rep_count, -1)
    )
    first_input_grad = jnp.einsum(
        "rqe,qde->rd", projected_grad, in_full, preferred_element_type=jnp.float32
    )
    input_grad = (residual_grad + norm_back(normed_one, inverse_one, first_input_grad)).reshape(
        tokens.shape
    )
    in_part = reduce_full(
        jnp.einsum(
            "rc,rqe->qce", first_input, projected_grad, preferred_element_type=jnp.float32
        ).astype(jnp.bfloat16)
    ).reshape(attention_in.shape)
    out_part = reduce_full(
        jnp.einsum(
            "rc,rqe->qce",
            mixed_low,
            branch_grad.reshape(row_total, rep_count, -1),
            preferred_element_type=jnp.float32,
        ).astype(jnp.bfloat16)
    )
    in_grad, in_new, in_first, in_second = adam_update(
        attention_in,
        attention_in_first,
        attention_in_second,
        in_part,
        step_count,
        learn_rate,
    )
    out_grad, out_new, out_first, out_second = adam_update(
        attention_out,
        attention_out_first,
        attention_out_second,
        out_part,
        step_count,
        learn_rate,
    )
    gu_grad, gu_new, gu_first, gu_second = adam_update(
        gate_up_weight, gate_up_first, gate_up_second, gate_up_part, step_count, learn_rate
    )
    dn_grad, dn_new, dn_first, dn_second = adam_update(
        down_weight, down_first, down_second, down_part, step_count, learn_rate
    )
    return (
        output,
        input_grad,
        in_grad,
        in_new,
        in_first,
        in_second,
        out_grad,
        out_new,
        out_first,
        out_second,
        gu_grad,
        gu_new,
        gu_first,
        gu_second,
        dn_grad,
        dn_new,
        dn_first,
        dn_second,
    )


def solution(mesh):
    return jax.shard_map(
        shards,
        mesh=mesh,
        in_specs=(
            P(("rep", "shard"), None, None),
            P(("rep", "shard"), None, None),
            P(),
            P(("rep", "shard")),
            P(),
            P(),
            P("shard", None, None),
            P("shard", None, None),
            P("shard", None, None),
            P("shard", None),
            P("shard", None),
            P("shard", None),
            P("shard", None, None),
            P("shard", None, None),
            P("shard", None, None),
            P("shard", None),
            P("shard", None),
            P("shard", None),
        ),
        out_specs=(
            P(("rep", "shard"), None, None),
            P(("rep", "shard"), None, None),
            P("shard", None, None),
            P("shard", None, None),
            P("shard", None, None),
            P("shard", None, None),
            P("shard", None),
            P("shard", None),
            P("shard", None),
            P("shard", None),
            P("shard", None, None),
            P("shard", None, None),
            P("shard", None, None),
            P("shard", None, None),
            P("shard", None),
            P("shard", None),
            P("shard", None),
            P("shard", None),
        ),
        check_vma=False,
    )
```

```python
import functools

import jax
import jax.numpy as jnp
from jax import lax
from jax.experimental import pallas as pl
from jax.experimental.pallas import tpu as pltpu
from jax.sharding import PartitionSpec as P

MESH = pl.DeviceIdType.MESH
DMA = pltpu.SemaphoreType.DMA
RING = 4

HD = 64


norm_eps = 1e-05
beta_first = 0.9
beta_second = 0.95
adam_eps = 1e-08
weight_decay = 0.1
rope_base = 10000.0
masked_score = -1e30


def layer_norm(values):
    centered = values - jnp.mean(values, axis=-1, keepdims=True)
    inverse = lax.rsqrt(jnp.mean(centered * centered, axis=-1, keepdims=True) + norm_eps)
    return (centered * inverse, inverse)


def norm_back(normed, inverse, upstream):
    mean_grad = jnp.mean(upstream, axis=-1, keepdims=True)
    mean_dot = jnp.mean(upstream * normed, axis=-1, keepdims=True)
    return inverse * (upstream - mean_grad - normed * mean_dot)


def rope_tables(position_count, head_size):
    half_size = head_size // 2
    frequency = rope_base ** (-(jnp.arange(half_size, dtype=jnp.float32) * 2.0 / head_size))
    angles = jnp.arange(position_count, dtype=jnp.float32)[:, None] * frequency[None, :]
    angles = jnp.concatenate([angles, angles], axis=1)
    return (jnp.cos(angles)[:, None, :], jnp.sin(angles)[:, None, :])


def rotate(values, cosine_table, sine_table):
    half_size = values.shape[-1] // 2
    turned = jnp.concatenate([-values[..., half_size:], values[..., :half_size]], axis=-1)
    return values * cosine_table + turned * sine_table


def masked_scores(queries, rotated_keys, length):
    position_count, head_size = (queries.shape[0], queries.shape[-1])
    scores = jnp.einsum(
        "qhd,khd->hqk", queries, rotated_keys, preferred_element_type=jnp.float32
    ) * head_size ** (-0.5)
    position = jnp.arange(position_count)
    allowed = (position[None, :] <= position[:, None]) & (position[None, :] < length)
    return jnp.where(allowed[None], scores, masked_score)


def attend_forward(pieces):
    queries, rotated_keys, values_low, length = pieces
    scores = masked_scores(queries, rotated_keys, length)
    row_max = jnp.max(scores, axis=-1, keepdims=True)
    exponent = jnp.exp(scores - row_max)
    row_sum = jnp.sum(exponent, axis=-1, keepdims=True)
    weights = (exponent / row_sum).astype(jnp.bfloat16)
    mixed_heads = jnp.einsum(
        "hqk,khd->qhd", weights, values_low, preferred_element_type=jnp.float32
    )
    return (mixed_heads, row_max + jnp.log(row_sum))


def attend_backward(pieces):
    queries, rotated_keys, values_low, length, log_total, mixed_grad = pieces
    head_size = queries.shape[-1]
    scores = masked_scores(queries, rotated_keys, length)
    probability = jnp.exp(scores - log_total)
    value_grad = jnp.einsum(
        "hqk,qhd->khd",
        probability.astype(jnp.bfloat16),
        mixed_grad,
        preferred_element_type=jnp.float32,
    )
    probability_grad = jnp.einsum(
        "qhd,khd->hqk", mixed_grad, values_low, preferred_element_type=jnp.float32
    )
    inner_dot = jnp.sum(probability * probability_grad, axis=-1, keepdims=True)
    score_grad = (probability * (probability_grad - inner_dot) * head_size ** (-0.5)).astype(
        jnp.bfloat16
    )
    query_grad = jnp.einsum(
        "hqk,khd->qhd", score_grad, rotated_keys, preferred_element_type=jnp.float32
    )
    key_grad = jnp.einsum("hqk,qhd->khd", score_grad, queries, preferred_element_type=jnp.float32)
    return (query_grad, key_grad, value_grad)


def adam_update(weight, first, second, gradient, step_count, learn_rate):
    steps_taken = step_count[0].astype(jnp.float32)
    first_new = beta_first * first + (1.0 - beta_first) * gradient
    second_new = beta_second * second + (1.0 - beta_second) * gradient * gradient
    first_hat = first_new / (1.0 - beta_first**steps_taken)
    second_hat = second_new / (1.0 - beta_second**steps_taken)
    weight_new = weight - learn_rate[0] * (
        first_hat / (jnp.sqrt(second_hat) + adam_eps) + weight_decay * weight
    )
    return (gradient, weight_new, first_new, second_new)


class Gather:
    NSEM = 9
    @staticmethod
    def scratch(nt, nc):
        return [DMA((nt,)), DMA((nc, 4)), DMA((nc, 4)), DMA((nc, 2, 3)), DMA((nc, 2, 3)), DMA((nc, 3, 2)), DMA((nc, 3, 2)), DMA((nc, 3, 2)), DMA((nc, 3, 2))]
    def __init__(self, shapes, chunks, loc, full, sems):
        self.shapes, self.chunks, self.loc, self.full = shapes, chunks, loc, full
        (self.cp, self.sib_s, self.sib_r, self.z_s, self.z_r, self.p_s, self.p_r, self.d_s, self.d_r) = sems
        self.rep = lax.axis_index("rep"); self.shard = lax.axis_index("shard")
        self.z = self.shard // 2; self.core = lax.rem(self.shard, 2)
        self.x = lax.rem(self.rep, 2); self.y = self.rep // 2
        self.sib = (self.rep, self.shard + 1 - 2 * self.core)
        self.nb = ((self.rep + 1 - 2 * self.x, self.shard), (self.rep + 2 - 4 * self.y, self.shard))
        self.diag = self.rep + (1 - 2 * self.x) + (2 - 4 * self.y)
    def barrier(self):
        bar = pltpu.get_barrier_semaphore()
        for dev in (self.sib,) + self.nb + tuple((self.rep, lax.rem(self.shard + 2 * d, 8)) for d in (1, 2, 3)):
            pl.semaphore_signal(bar, inc=1, device_id=dev, device_id_type=MESH)
        pl.semaphore_wait(bar, 6)
    def ref(self, c, s, q=None, half=None):
        t, r0, rows, c0, cols, axis = self.chunks[c]
        R = self.shapes[t][0]
        ro, co, nr, ncl = r0, c0, rows, cols
        base = s * R + r0
        if q is not None:
            parts, i = (4, q) if half is None else (8, 2 * q + half)
            if axis == 0:
                nr = rows // parts; base = base + i * nr
            else:
                ncl = cols // parts; co = pl.multiple_of(c0 + i * ncl, 128)
        base = pl.multiple_of(base, 16 if nr % 16 == 0 else 8)
        return self.full[t].at[pl.ds(base, nr), pl.ds(co, ncl)]
    def loc_ref(self, c, q=None):
        t, r0, rows, c0, cols, axis = self.chunks[c]
        nr, ncl, ro, co = rows, cols, r0, c0
        if q is not None:
            if axis == 0: nr = rows // 4; ro = pl.multiple_of(r0 + q * nr, 16)
            else: ncl = cols // 4; co = pl.multiple_of(c0 + q * ncl, 128)
        return self.loc[t].at[pl.ds(ro, nr), pl.ds(co, ncl)]
    def rc(self, src, dst, ss, rs, dev):
        return pltpu.make_async_remote_copy(src_ref=src, dst_ref=dst, send_sem=ss, recv_sem=rs, device_id=dev, device_id_type=MESH)
    def own(self, t):
        R, C, = self.shapes[t]
        return pltpu.make_async_copy(self.loc[t], self.full[t].at[pl.ds(pl.multiple_of(self.shard * R, R), R), :], self.cp.at[t])
    def other(self, dz): return lax.rem(self.shard + 2 * dz, 8)
    def sibc(self, c, dz):
        r = self.ref(c, self.other(dz))
        return self.rc(self.loc_ref(c) if dz == 0 else r, r, self.sib_s.at[c, dz], self.sib_r.at[c, dz], self.sib)
    def zc(self, c, side, h, first):
        sgn = 1 if side == 0 else -1
        s = self.shard - sgn * 2 * (h - 1)
        src = self.loc_ref(c, self.rep) if first else self.ref(c, s, self.rep)
        return self.rc(src, self.ref(c, s, self.rep), self.z_s.at[c, side, h - 1], self.z_r.at[c, side, h - 1], (self.rep, self.shard + sgn * 2))
    def z_send(self, c, side, h):
        can = (self.z < 3) if side == 0 else (self.z > 0)
        has = (self.z >= h - 1) if side == 0 else (self.z <= 3 - (h - 1))
        return jnp.logical_and(can, has)
    def z_got(self, side, h):
        return (self.z >= h) if side == 0 else (self.z <= 3 - h)
    def zr(self, c, side, h):
        sgn = 1 if side == 0 else -1
        s = self.shard - sgn * 2 * h
        r = self.ref(c, s, self.rep)
        return self.rc(r, r, self.z_s.at[c, side, h - 1], self.z_r.at[c, side, h - 1], (self.rep, self.shard - sgn * 2))
    def pc(self, c, dz, k, q=None):
        q = self.rep if q is None else q
        r = self.ref(c, self.other(dz), q)
        return self.rc(r, r, self.p_s.at[c, dz - 1, k], self.p_r.at[c, dz - 1, k], self.nb[k])
    def dc(self, c, dz, k, q=None):
        q = self.nb[k][0] if q is None else q
        r = self.ref(c, self.other(dz), q, k)
        return self.rc(r, r, self.d_s.at[c, dz - 1, k], self.d_r.at[c, dz - 1, k], self.nb[1 - k])
    def s0(self, c):
        for side in (0, 1):
            @pl.when(self.z_send(c, side, 1))
            def _(): self.zc(c, side, 1, True).start()
        self.sibc(c, 0).start()
    def s1(self, c, h):
        for side in (0, 1):
            @pl.when(self.z_got(side, h))
            def _():
                self.zr(c, side, h).wait_recv()
                if h < 3:
                    @pl.when((self.z < 3) if side == 0 else (self.z > 0))
                    def _(): self.zc(c, side, h + 1, False).start()
                dz = (4 - h) if side == 0 else h
                for k in (0, 1): self.pc(c, dz, k).start()
    def order(self):
        return (1, 3, 2)
    def s2(self, c):
        for dz in self.order():
            for k in (0, 1):
                self.pc(c, dz, k, self.nb[k][0]).wait_recv(); self.dc(c, dz, k).start()
    def s3(self, c):
        for dz in self.order():
            for k in (0, 1): self.dc(c, dz, k, self.diag).wait_recv()
            self.sibc(c, dz).start()
    def done(self, c):
        for dz in range(4): self.sibc(c, dz).wait()
    def drain(self, c):
        for side in (0, 1):
            for h in (1, 2, 3):
                @pl.when(self.z_send(c, side, h))
                def _(): self.zc(c, side, h, h == 1).wait_send()
        for dz in (1, 2, 3):
            for k in (0, 1): self.pc(c, dz, k).wait_send(); self.dc(c, dz, k).wait_send()

def gather_kernel(shapes, chunks, lags, *refs):
    n = len(shapes); nc = len(chunks)
    g = Gather(shapes, chunks, refs[:n], refs[n:2 * n], refs[2 * n:])
    g.barrier()
    for t in range(n): g.own(t).start()
    stages = [g.s0] + [functools.partial(lambda h, c: g.s1(c, h), h) for h in (1, 2, 3)] + [g.s2, g.s3, g.done]
    for i in range(nc + max(lags)):
        for st, lag in zip(stages, lags):
            if 0 <= i - lag < nc: st(i - lag)
    for t in range(n): g.own(t).wait()
    for c in range(nc): g.drain(c)

def gather_call(locs):
    shapes = [l.shape for l in locs]
    rows, qkv = shapes[0]
    gate_up = shapes[2][1] // 2
    chunks = (
        (0, 0, rows, 0, qkv, 1),
        (1, 0, rows, 0, shapes[1][1], 1),
        (2, 0, rows, 0, gate_up, 0),
        (2, 0, rows, gate_up, gate_up, 0),
        (3, 0, shapes[3][0], 0, shapes[3][1], 1),
    )
    lags = (0, 1, 2, 3, 3, 4, 5)
    n, nc = len(shapes), len(chunks)
    return pl.pallas_call(functools.partial(gather_kernel, shapes, chunks, lags),
        out_shape=[jax.ShapeDtypeStruct((8 * r, c), jnp.bfloat16) for r, c in shapes],
        in_specs=[pl.BlockSpec(memory_space=pl.ANY)] * n, out_specs=[pl.BlockSpec(memory_space=pl.ANY)] * n,
        scratch_shapes=Gather.scratch(n, nc),
        compiler_params=pltpu.CompilerParams(collective_id=0, has_side_effects=True))(*locs)

class Reduce:
    def __init__(self, refs):
        (self.mine, self.theirs, self.held, self.got, self.sums, self.one, self.two, self.fin, self.planes, self.total,
         self.a_s, self.a_r, self.o_s, self.o_r, self.t_s, self.t_r, self.c_s, self.c_r, self.d_s, self.d_r, self.f_s, self.f_r) = refs
        self.rep, self.shard = lax.axis_index("rep"), lax.axis_index("shard")
        self.core = lax.rem(self.shard, 2)
        self.x, self.y = lax.rem(self.rep, 2), self.rep // 2
        self.sib = (self.rep, self.shard + 1 - 2 * self.core)
        self.nb = ((self.rep + 1 - 2 * self.x, self.shard), (self.rep + 2 - 4 * self.y, self.shard))

    @staticmethod
    def scratch(chunks, wide):
        v = lambda *s: pltpu.VMEM(s, jnp.bfloat16)
        return [
            v(RING, 8, 16, wide),
            v(RING, 8, 16, wide),
            pltpu.VMEM((2, 8, 16, wide), jnp.float32),
            None, v(RING, 8, 16, wide),
            v(2, RING, 2, 16, wide),
            v(2, RING, 16, wide),
            v(RING, 2, 16, wide),
            v(chunks, 3, 2, 16, wide),
            None,
        ], [DMA((RING,)), DMA((RING,)), DMA((2, RING)), DMA((2, RING)), DMA((2, RING)), DMA((2, RING)), DMA((RING,)), DMA((chunks, 3)),
            DMA((chunks, 2)), DMA((chunks, 2)), DMA((chunks, 2)), DMA((chunks, 2))]

    def copy(self, src, dst, s, r, dev):
        return pltpu.make_async_remote_copy(src_ref=src, dst_ref=dst, send_sem=s, recv_sem=r, device_id=dev, device_id_type=MESH)

    def barrier(self):
        bar = pltpu.get_barrier_semaphore()
        for dev in (self.sib,) + self.nb + tuple((self.rep, lax.rem(self.shard + 2 * d, 8)) for d in (1, 2, 3)):
            pl.semaphore_signal(bar, inc=1, device_id=dev, device_id_type=MESH)
        pl.semaphore_wait(bar, 6)

    def first(self, u, w):
        s = lax.rem(u, RING)
        return self.copy(self.mine.at[s, :, :, pl.ds(0, w)], self.theirs.at[s, :, :, pl.ds(0, w)], self.a_s.at[s], self.a_r.at[s], self.sib)

    def hop_one(self, u, w, k):
        s = lax.rem(u, RING)
        at = 2 - 2 * self.x if k == 0 else 6 - 2 * self.y
        return self.copy(self.sums.at[s, pl.ds(at, 2), :, pl.ds(0, w)], self.one.at[k, s, :, :, pl.ds(0, w)], self.o_s.at[k, s], self.o_r.at[k, s], self.nb[k])

    def hop_two(self, u, w, k):
        s = lax.rem(u, RING)
        at = 2 * self.x + 1 - self.y if k == 0 else 4 + 2 * self.y + 1 - self.x
        return self.copy(self.sums.at[s, at, :, pl.ds(0, w)], self.two.at[k, s, :, pl.ds(0, w)], self.t_s.at[k, s], self.t_r.at[k, s], self.nb[1 - k])

    def across(self, u, w, dz):
        s = lax.rem(u, RING)
        c = u // 4
        return self.copy(self.fin.at[s, :, :, pl.ds(0, w)], self.planes.at[c, 3 - dz, :, :, pl.ds(0, w)], self.c_s.at[s], self.c_r.at[c, 3 - dz], (self.rep, lax.rem(self.shard + 2 * dz, 8)))

    def plane_in(self, c, w, j):
        return self.copy(self.fin.at[0, :, :, pl.ds(0, w)], self.planes.at[c, j, :, :, pl.ds(0, w)], self.c_s.at[0], self.c_r.at[c, j], self.sib)

    def spread(self, c, w, k, own=True):
        q = self.rep if own else self.nb[k][0]
        ref = self.total.at[c, q, :, :, pl.ds(0, w)]
        return self.copy(ref, ref, self.d_s.at[c, k], self.d_r.at[c, k], self.nb[k])

    def spread_on(self, c, w, k, own=True):
        q = self.nb[k][0] if own else self.nb[0][0] + self.nb[1][0] - self.rep
        ref = self.total.at[c, q, k, :, pl.ds(0, w)]
        return self.copy(ref, ref, self.f_s.at[c, k], self.f_r.at[c, k], self.nb[1 - k])

    def stage_two(self, u, w):
        s = lax.rem(u, RING)
        self.first(u, w).wait()
        self.sums[s, :, :, :w] = (self.held[lax.rem(u, 2), :, :, :w] + self.theirs[s, :, :, :w].astype(jnp.float32)).astype(jnp.bfloat16)
        for k in (0, 1):
            self.hop_one(u, w, k).start()

    def stage_three(self, u, w):
        s = lax.rem(u, RING)
        for k in (0, 1):
            self.hop_one(u, w, k).wait()
            at = 2 * self.x if k == 0 else 4 + 2 * self.y
            new = self.sums[s, pl.ds(at, 2), :, :w].astype(jnp.float32) + self.one[k, s, :, :, :w].astype(jnp.float32)
            self.sums[s, pl.ds(at, 2), :, :w] = new.astype(jnp.bfloat16)
            self.hop_two(u, w, k).start()

    def stage_four(self, u, w, start):
        s = lax.rem(u, RING)
        c = u // 4
        dz = lax.rem(lax.rem(u, 4) + 1, 4)

        @pl.when(jnp.logical_and(u >= start + RING, dz > 0))
        def _():
            self.across(u - RING, w, dz).wait_send()

        for k in (0, 1):
            self.hop_two(u, w, k).wait()

        def plane_sum(k):
            at = 2 * self.x + self.y if k == 0 else 4 + 2 * self.y + self.x
            return self.sums[s, at, :, :w].astype(jnp.float32) + self.two[k, s, :, :w].astype(jnp.float32)

        @pl.when(dz > 0)
        def _():
            for k in (0, 1):
                self.fin[s, k, :, :w] = plane_sum(k).astype(jnp.bfloat16)
            self.across(u, w, dz).start()

        @pl.when(dz == 0)
        def _():
            for j in range(3):
                self.plane_in(c, w, j).wait_recv()
            for k in (0, 1):
                out = plane_sum(k)
                for j in range(3):
                    out = out + self.planes[c, j, k, :, :w].astype(jnp.float32)
                self.total[c, self.rep, k, :, :w] = out.astype(jnp.bfloat16)
            for k in (0, 1):
                self.spread(c, w, k).start()

    def stage_five(self, u, w):
        @pl.when(lax.rem(u, 4) == 3)
        def _():
            c = u // 4
            for k in (0, 1):
                self.spread(c, w, k, False).wait_recv()
                self.spread_on(c, w, k).start()

    def drain_across(self, units, w):
        for u in range(units - RING, units):
            if u % 4 != 3:
                self.across(u, w, u % 4 + 1).wait_send()

    def finish(self, units, width):
        self.drain_across(units, width(units - 1))
        for c in range(units // 4):
            w = width(4 * c)
            for k in (0, 1):
                self.spread(c, w, k).wait_send()
                self.spread_on(c, w, k).wait_send()
                self.spread_on(c, w, k, False).wait_recv()


def reduce_kernel(plan, wide, *refs):
    left_ref, at_ref, at_r, gu_l, gu_r, dn_l, dn_r = (None,) + refs[:6]
    total = refs[6]
    s = refs[7:]
    r = Reduce((s[0], s[1], s[2], None, s[3], s[4], s[5], s[6], s[7], total) + tuple(s[8:]))
    units = 4 * sum(n for _, n, _ in plan)
    bounds, u0 = [], 0
    for kind, n, w in plan:
        bounds.append((u0, u0 + 4 * n, kind, w))
        u0 += 4 * n

    def width(u):
        for a, b, _, w in bounds:
            if a <= u < b:
                return w

    def start_of(w):
        return min(a for a, _, _, v in bounds if v == w)

    def plane_of(u):
        return lax.rem(r.shard // 2 + lax.rem(u, 4) + 1, 4)

    def product(u, kind, first, own):
        c = u // 4 - first // 4
        zt = plane_of(u)
        core = r.core if own else 1 - r.core
        dst = (lambda e, lo, n, val: r.held.__setitem__((lax.rem(u, 2), e, slice(None), pl.ds(lo, n)), val)) if own else (
            lambda e, lo, n, val: r.mine.__setitem__((lax.rem(u, RING), e, slice(None), pl.ds(lo, n)), val.astype(jnp.bfloat16)))
        if kind == 0:
            rows = dn_l.shape[0] // 8
            part = rows // 2
            base = pl.multiple_of((2 * zt + core) * rows + c * part, 16)
            left = dn_l[pl.ds(base, part), :]
            for e in range(8):
                if e % 2 == 0:
                    out = jnp.dot(left, dn_r[:, e * 128:e * 128 + 256], preferred_element_type=jnp.float32)
                for j in range(part // 16):
                    dst(e, 128 * j, 128, out[16 * j:16 * j + 16, (e % 2) * 128:(e % 2) * 128 + 128])
        elif kind == 1:
            base = pl.multiple_of((2 * zt + core) * 128, 128)
            left = gu_l[pl.ds(base, 128), :]
            col = pl.multiple_of(c * wide, 128)
            out = jnp.dot(left, gu_r[:, pl.ds(col, wide)], preferred_element_type=jnp.float32)
            dst(slice(None), 0, wide, out.reshape(8, 16, wide))
        else:
            n = 1024
            base = pl.multiple_of((2 * zt + core) * 128 + jnp.where(c == 0, 1024, 0), 128)
            left = at_ref[pl.ds(base, 128), :]
            col = pl.multiple_of(c * n, 128)
            out = jnp.dot(left, at_r[:, pl.ds(col, n)], preferred_element_type=jnp.float32)
            dst(slice(None), 0, n, out.reshape(8, 16, n))

    def step(u, kind, first, ws):
        product(u, kind, first, False)
        r.first(u, ws[0]).start()
        product(u, kind, first, True)
        tail(u, ws)

    def tail(u, ws):
        if ws[1]: r.stage_two(u - 1, ws[1])
        if ws[2]: r.stage_three(u - 2, ws[2])
        if ws[3]: r.stage_four(u - 3, ws[3], start_of(ws[3]))
        if ws[4]: r.stage_five(u - 4, ws[4])

    r.barrier()
    for a, b, kind, w in bounds:
        u = a
        while u < b:
            ws = [width(u - k) if u - k >= 0 else None for k in range(5)]
            if all(x == w for x in ws):
                lax.fori_loop(u, b, lambda i, _: (step(i, kind, a, ws), 0)[1], 0)
                break
            if u >= 4 and ws[3] and u - 4 >= 0 and u - 3 == start_of(ws[3]) and u - 3 > 0:
                r.drain_across(u - 3, width(u - 4))
            step(jnp.int32(u), kind, a, ws)
            u += 1
    for u in range(units, units + 4):
        ws = [width(u - k) if 0 <= u - k < units else None for k in range(5)]
        tail(jnp.int32(u), ws)
    r.finish(units, width)


def reduce_call(attn_left, attn_right, gu_left, gu_right, down_left, down_right):
    wide = gu_right.shape[1] // 4
    plan = ((0, 2, wide), (1, 4, wide), (2, 4, 1024))
    vs, sems = Reduce.scratch(10, wide)
    vm = pl.BlockSpec(memory_space=pltpu.VMEM)
    return pl.pallas_call(
        functools.partial(reduce_kernel, plan, wide),
        out_shape=jax.ShapeDtypeStruct((10, 4, 2, 16, wide), jnp.bfloat16),
        in_specs=[vm] * 6,
        out_specs=vm,
        scratch_shapes=[v for v in vs if v is not None] + sems,
        compiler_params=pltpu.CompilerParams(collective_id=1, has_side_effects=True, vmem_limit_bytes=56 << 20),
    )(attn_left, attn_right, gu_left, gu_right, down_left, down_right)


def pieces(total, c, w):
    t = total[c, :, :, :, :w]
    return jnp.stack([t[0, 0], t[2, 0], t[1, 0], t[3, 0]] + [t[i, 1] for i in range(4)])


def unpack(total, wide):
    down = [pieces(total, c, wide).reshape(8, 16, wide // 128, 128).transpose(2, 1, 0, 3).reshape(-1, 1024) for c in (0, 1)]
    gu = [pieces(total, c, wide).reshape(128, wide) for c in (2, 3, 4, 5)]
    at = [pieces(total, c, 1024).reshape(128, 1024) for c in (6, 7, 8, 9)]
    return jnp.concatenate(down, 0), jnp.concatenate(gu, 1), at[0], jnp.stack(at[1:], 1)


def gather_full(local, rep_count, rep_index):
    rows = local.shape[0]
    flat = local.reshape(rows, -1)
    width = flat.shape[1] // rep_count
    piece = lax.dynamic_slice_in_dim(flat, rep_index * width, width, axis=1)
    column = lax.all_gather(piece, "shard", axis=0, tiled=True)
    return lax.all_gather(column, "rep", axis=0, tiled=False)


def reduce_full(partial):
    part = lax.psum_scatter(partial, "rep", scatter_dimension=0, tiled=False)
    part = lax.psum_scatter(part, "shard", scatter_dimension=0, tiled=True)
    pieces = lax.all_gather(part, "rep", axis=0, tiled=False)
    rows = pieces.shape[1]
    return jnp.transpose(pieces, (1, 0, 2)).reshape(rows, -1).astype(jnp.float32)


def shards_generic(
    tokens,
    cotangent,
    lengths,
    slot_sequence,
    step_count,
    learn_rate,
    attention_in,
    attention_in_first,
    attention_in_second,
    attention_out,
    attention_out_first,
    attention_out_second,
    gate_up_weight,
    gate_up_first,
    gate_up_second,
    down_weight,
    down_first,
    down_second,
):
    slot_count, position_count, feature_count = tokens.shape
    row_total = slot_count * position_count
    head_count = feature_count // HD
    shaped = (slot_count, position_count, head_count, HD)
    inputs = tokens.astype(jnp.float32).reshape(row_total, feature_count)
    matches = jnp.arange(lengths.shape[0])[None, :] == slot_sequence[:, None]
    slot_length = jnp.sum(jnp.where(matches, lengths[None, :], 0), axis=1)
    alive_rows = (
        (jnp.arange(position_count)[None, :] < slot_length[:, None])
        .astype(jnp.float32)
        .reshape(row_total, 1)
    )
    cosine_table, sine_table = rope_tables(position_count, HD)
    in_local = attention_in.astype(jnp.bfloat16)
    out_local = attention_out.astype(jnp.bfloat16)
    gate_up_local = gate_up_weight.astype(jnp.bfloat16)
    down_local = down_weight.astype(jnp.bfloat16)
    rep_count = lax.axis_size("rep")
    rep_index = lax.axis_index("rep")
    in_full = gather_full(in_local, rep_count, rep_index)
    out_full = gather_full(out_local, rep_count, rep_index)
    gate_up_full = gather_full(gate_up_local, rep_count, rep_index)
    down_full = gather_full(down_local, rep_count, rep_index)
    normed_one, inverse_one = layer_norm(inputs)
    first_input = normed_one.astype(jnp.bfloat16)
    projected = jnp.einsum(
        "rd,qde->rqe", first_input, in_full, preferred_element_type=jnp.float32
    ).reshape(row_total, 3, feature_count)
    queries = rotate(projected[:, 0].reshape(shaped), cosine_table, sine_table).astype(jnp.bfloat16)
    rotated_keys = rotate(projected[:, 1].reshape(shaped), cosine_table, sine_table).astype(
        jnp.bfloat16
    )
    values_low = projected[:, 2].reshape(shaped).astype(jnp.bfloat16)
    mixed_heads, log_total = lax.map(
        attend_forward, (queries, rotated_keys, values_low, slot_length)
    )
    mixed_low = mixed_heads.reshape(row_total, feature_count).astype(jnp.bfloat16)
    residual = inputs + jnp.einsum(
        "rd,qde->rqe", mixed_low, out_full, preferred_element_type=jnp.float32
    ).reshape(row_total, feature_count)
    normed_two, inverse_two = layer_norm(residual)
    second_input = normed_two.astype(jnp.bfloat16)
    gate_up = jnp.einsum(
        "rd,qdf->rqf", second_input, gate_up_full, preferred_element_type=jnp.float32
    ).reshape(row_total, 2, -1)
    gate_value = gate_up[:, 0]
    up_value = gate_up[:, 1]
    sigmoid_gate = jax.nn.sigmoid(gate_value)
    hidden_low = (gate_value * sigmoid_gate * up_value).astype(jnp.bfloat16)
    result = residual + jnp.einsum(
        "rf,qfe->rqe", hidden_low, down_full, preferred_element_type=jnp.float32
    ).reshape(row_total, feature_count)
    output = (result * alive_rows).astype(jnp.bfloat16).reshape(tokens.shape)
    output_grad = cotangent.astype(jnp.float32).reshape(row_total, feature_count) * alive_rows
    result_grad_low = output_grad.astype(jnp.bfloat16)
    hidden_grad = jnp.einsum(
        "rqe,qfe->rf",
        result_grad_low.reshape(row_total, rep_count, -1),
        down_full,
        preferred_element_type=jnp.float32,
    )
    gate_grad = hidden_grad * up_value * sigmoid_gate * (1.0 + gate_value * (1.0 - sigmoid_gate))
    up_grad = hidden_grad * gate_value * sigmoid_gate
    gate_up_grad_low = (
        jnp.concatenate([gate_grad, up_grad], axis=1)
        .astype(jnp.bfloat16)
        .reshape(row_total, rep_count, -1)
    )
    second_input_grad = jnp.einsum(
        "rqf,qdf->rd", gate_up_grad_low, gate_up_full, preferred_element_type=jnp.float32
    )
    residual_grad = output_grad + norm_back(normed_two, inverse_two, second_input_grad)
    down_part = reduce_full(
        jnp.einsum(
            "rc,rqe->qce",
            hidden_low,
            result_grad_low.reshape(row_total, rep_count, -1),
            preferred_element_type=jnp.float32,
        ).astype(jnp.bfloat16)
    )
    gate_up_part = reduce_full(
        jnp.einsum(
            "rc,rqf->qcf", second_input, gate_up_grad_low, preferred_element_type=jnp.float32
        ).astype(jnp.bfloat16)
    ).reshape(gate_up_weight.shape)
    branch_grad = residual_grad.astype(jnp.bfloat16)
    mixed_grad = (
        jnp.einsum(
            "rqe,qde->rd",
            branch_grad.reshape(row_total, rep_count, -1),
            out_full,
            preferred_element_type=jnp.float32,
        )
        .astype(jnp.bfloat16)
        .reshape(shaped)
    )
    query_grad, key_grad, value_grad = lax.map(
        attend_backward, (queries, rotated_keys, values_low, slot_length, log_total, mixed_grad)
    )
    query_back = rotate(query_grad, cosine_table, -sine_table).reshape(row_total, feature_count)
    key_back = rotate(key_grad, cosine_table, -sine_table).reshape(row_total, feature_count)
    projected_grad = (
        jnp.concatenate([query_back, key_back, value_grad.reshape(row_total, feature_count)], axis=1)
        .astype(jnp.bfloat16)
        .reshape(row_total, rep_count, -1)
    )
    first_input_grad = jnp.einsum(
        "rqe,qde->rd", projected_grad, in_full, preferred_element_type=jnp.float32
    )
    input_grad = (residual_grad + norm_back(normed_one, inverse_one, first_input_grad)).reshape(
        tokens.shape
    )
    in_part = reduce_full(
        jnp.einsum(
            "rc,rqe->qce", first_input, projected_grad, preferred_element_type=jnp.float32
        ).astype(jnp.bfloat16)
    ).reshape(attention_in.shape)
    out_part = reduce_full(
        jnp.einsum(
            "rc,rqe->qce",
            mixed_low,
            branch_grad.reshape(row_total, rep_count, -1),
            preferred_element_type=jnp.float32,
        ).astype(jnp.bfloat16)
    )
    in_grad, in_new, in_first, in_second = adam_update(
        attention_in,
        attention_in_first,
        attention_in_second,
        in_part,
        step_count,
        learn_rate,
    )
    out_grad, out_new, out_first, out_second = adam_update(
        attention_out,
        attention_out_first,
        attention_out_second,
        out_part,
        step_count,
        learn_rate,
    )
    gu_grad, gu_new, gu_first, gu_second = adam_update(
        gate_up_weight, gate_up_first, gate_up_second, gate_up_part, step_count, learn_rate
    )
    dn_grad, dn_new, dn_first, dn_second = adam_update(
        down_weight, down_first, down_second, down_part, step_count, learn_rate
    )
    return (
        output,
        input_grad,
        in_grad,
        in_new,
        in_first,
        in_second,
        out_grad,
        out_new,
        out_first,
        out_second,
        gu_grad,
        gu_new,
        gu_first,
        gu_second,
        dn_grad,
        dn_new,
        dn_first,
        dn_second,
    )


def shards_fast(
    tokens,
    cotangent,
    lengths,
    slot_sequence,
    step_count,
    learn_rate,
    attention_in,
    attention_in_first,
    attention_in_second,
    attention_out,
    attention_out_first,
    attention_out_second,
    gate_up_weight,
    gate_up_first,
    gate_up_second,
    down_weight,
    down_first,
    down_second,
):
    slot_count, position_count, feature_count = tokens.shape
    row_total = slot_count * position_count
    head_count = feature_count // HD
    shaped = (slot_count, position_count, head_count, HD)
    inputs = tokens.astype(jnp.float32).reshape(row_total, feature_count)
    matches = jnp.arange(lengths.shape[0])[None, :] == slot_sequence[:, None]
    slot_length = jnp.sum(jnp.where(matches, lengths[None, :], 0), axis=1)
    alive_rows = (
        (jnp.arange(position_count)[None, :] < slot_length[:, None])
        .astype(jnp.float32)
        .reshape(row_total, 1)
    )
    cosine_table, sine_table = rope_tables(position_count, HD)
    in_local = attention_in.astype(jnp.bfloat16)
    out_local = attention_out.astype(jnp.bfloat16)
    gate_up_local = gate_up_weight.astype(jnp.bfloat16)
    down_local = down_weight.astype(jnp.bfloat16)
    locs = [
        in_local.reshape(in_local.shape[0], -1),
        out_local,
        gate_up_local.reshape(gate_up_local.shape[0], -1),
        down_local,
    ]
    in_full, out_full, gate_up_full, down_full = gather_call(locs)
    normed_one, inverse_one = layer_norm(inputs)
    first_input = normed_one.astype(jnp.bfloat16)
    projected = jnp.dot(first_input, in_full, preferred_element_type=jnp.float32).reshape(
        row_total, 3, feature_count
    )
    queries = rotate(projected[:, 0].reshape(shaped), cosine_table, sine_table).astype(jnp.bfloat16)
    rotated_keys = rotate(projected[:, 1].reshape(shaped), cosine_table, sine_table).astype(
        jnp.bfloat16
    )
    values_low = projected[:, 2].reshape(shaped).astype(jnp.bfloat16)
    mixed_heads, log_total = lax.map(
        attend_forward, (queries, rotated_keys, values_low, slot_length)
    )
    mixed_low = mixed_heads.reshape(row_total, feature_count).astype(jnp.bfloat16)
    residual = inputs + jnp.dot(mixed_low, out_full, preferred_element_type=jnp.float32)
    normed_two, inverse_two = layer_norm(residual)
    second_input = normed_two.astype(jnp.bfloat16)
    gate_up = jnp.dot(second_input, gate_up_full, preferred_element_type=jnp.float32)
    hidden_count = down_full.shape[0]
    gate_value = gate_up[:, :hidden_count]
    up_value = gate_up[:, hidden_count:]
    sigmoid_gate = jax.nn.sigmoid(gate_value)
    hidden_low = (gate_value * sigmoid_gate * up_value).astype(jnp.bfloat16)
    result = residual + jnp.dot(hidden_low, down_full, preferred_element_type=jnp.float32)
    output = (result * alive_rows).astype(jnp.bfloat16).reshape(tokens.shape)
    output_grad = cotangent.astype(jnp.float32).reshape(row_total, feature_count) * alive_rows
    result_grad_low = output_grad.astype(jnp.bfloat16)
    hidden_grad = jnp.einsum(
        "re,fe->rf", result_grad_low, down_full, preferred_element_type=jnp.float32
    )
    gate_grad = hidden_grad * up_value * sigmoid_gate * (1.0 + gate_value * (1.0 - sigmoid_gate))
    up_grad = hidden_grad * gate_value * sigmoid_gate
    gate_up_grad_low = jnp.concatenate([gate_grad, up_grad], axis=1).astype(jnp.bfloat16)
    second_input_grad = jnp.einsum(
        "rf,df->rd", gate_up_grad_low, gate_up_full, preferred_element_type=jnp.float32
    )
    residual_grad = output_grad + norm_back(normed_two, inverse_two, second_input_grad)
    branch_grad = residual_grad.astype(jnp.bfloat16)
    mixed_grad = (
        jnp.einsum("re,de->rd", branch_grad, out_full, preferred_element_type=jnp.float32)
        .astype(jnp.bfloat16)
        .reshape(shaped)
    )
    query_grad, key_grad, value_grad = lax.map(
        attend_backward, (queries, rotated_keys, values_low, slot_length, log_total, mixed_grad)
    )
    query_back = rotate(query_grad, cosine_table, -sine_table).reshape(row_total, feature_count)
    key_back = rotate(key_grad, cosine_table, -sine_table).reshape(row_total, feature_count)
    projected_grad = (
        jnp.concatenate([query_back, key_back, value_grad.reshape(row_total, feature_count)], axis=1)
        .astype(jnp.bfloat16)
    )
    first_input_grad = jnp.einsum(
        "re,de->rd", projected_grad, in_full, preferred_element_type=jnp.float32
    )
    input_grad = (residual_grad + norm_back(normed_one, inverse_one, first_input_grad)).reshape(
        tokens.shape
    )
    total = reduce_call(
        jnp.concatenate([first_input.T, mixed_low.T], axis=0),
        jnp.concatenate([branch_grad, projected_grad], axis=1),
        second_input.T,
        gate_up_grad_low,
        hidden_low.T,
        result_grad_low,
    )
    down_part, gate_up_part, out_part, in_part = [
        part.astype(jnp.float32) for part in unpack(total, 2 * hidden_count // 4)
    ]
    gate_up_part = gate_up_part.reshape(gate_up_weight.shape)
    in_grad, in_new, in_first, in_second = adam_update(
        attention_in,
        attention_in_first,
        attention_in_second,
        in_part,
        step_count,
        learn_rate,
    )
    out_grad, out_new, out_first, out_second = adam_update(
        attention_out,
        attention_out_first,
        attention_out_second,
        out_part,
        step_count,
        learn_rate,
    )
    gu_grad, gu_new, gu_first, gu_second = adam_update(
        gate_up_weight, gate_up_first, gate_up_second, gate_up_part, step_count, learn_rate
    )
    dn_grad, dn_new, dn_first, dn_second = adam_update(
        down_weight, down_first, down_second, down_part, step_count, learn_rate
    )
    return (
        output,
        input_grad,
        in_grad,
        in_new,
        in_first,
        in_second,
        out_grad,
        out_new,
        out_first,
        out_second,
        gu_grad,
        gu_new,
        gu_first,
        gu_second,
        dn_grad,
        dn_new,
        dn_first,
        dn_second,
    )


def solution(mesh):
    fast = mesh.shape["rep"] == 4 and mesh.shape["shard"] == 8
    return jax.shard_map(
        shards_fast if fast else shards_generic,
        mesh=mesh,
        in_specs=(
            P(("rep", "shard"), None, None),
            P(("rep", "shard"), None, None),
            P(),
            P(("rep", "shard")),
            P(),
            P(),
            P("shard", None, None),
            P("shard", None, None),
            P("shard", None, None),
            P("shard", None),
            P("shard", None),
            P("shard", None),
            P("shard", None, None),
            P("shard", None, None),
            P("shard", None, None),
            P("shard", None),
            P("shard", None),
            P("shard", None),
        ),
        out_specs=(
            P(("rep", "shard"), None, None),
            P(("rep", "shard"), None, None),
            P("shard", None, None),
            P("shard", None, None),
            P("shard", None, None),
            P("shard", None, None),
            P("shard", None),
            P("shard", None),
            P("shard", None),
            P("shard", None),
            P("shard", None, None),
            P("shard", None, None),
            P("shard", None, None),
            P("shard", None, None),
            P("shard", None),
            P("shard", None),
            P("shard", None),
            P("shard", None),
        ),
        check_vma=False,
    )
```

```python
import functools

import jax
import jax.numpy as jnp
from jax import lax
from jax.experimental import pallas as pl
from jax.experimental.pallas import tpu as pltpu
from jax.sharding import PartitionSpec as P

MESH = pl.DeviceIdType.MESH
DMA = pltpu.SemaphoreType.DMA
RING = 4
F32, BF16 = jnp.float32, jnp.bfloat16

HD = 64


norm_eps = 1e-05
beta_first = 0.9
beta_second = 0.95
adam_eps = 1e-08
weight_decay = 0.1
rope_base = 10000.0
masked_score = -1e30


def layer_norm(values):
    centered = values - jnp.mean(values, axis=-1, keepdims=True)
    inverse = lax.rsqrt(jnp.mean(centered * centered, axis=-1, keepdims=True) + norm_eps)
    return (centered * inverse, inverse)


def norm_back(normed, inverse, upstream):
    mean_grad = jnp.mean(upstream, axis=-1, keepdims=True)
    mean_dot = jnp.mean(upstream * normed, axis=-1, keepdims=True)
    return inverse * (upstream - mean_grad - normed * mean_dot)


def rope_tables(position_count, head_size):
    half_size = head_size // 2
    frequency = rope_base ** (-(jnp.arange(half_size, dtype=jnp.float32) * 2.0 / head_size))
    angles = jnp.arange(position_count, dtype=jnp.float32)[:, None] * frequency[None, :]
    angles = jnp.concatenate([angles, angles], axis=1)
    return (jnp.cos(angles)[:, None, :], jnp.sin(angles)[:, None, :])


def rotate(values, cosine_table, sine_table):
    half_size = values.shape[-1] // 2
    turned = jnp.concatenate([-values[..., half_size:], values[..., :half_size]], axis=-1)
    return values * cosine_table + turned * sine_table


def masked_scores(queries, rotated_keys, length):
    position_count, head_size = (queries.shape[0], queries.shape[-1])
    scores = jnp.einsum(
        "qhd,khd->hqk", queries, rotated_keys, preferred_element_type=jnp.float32
    ) * head_size ** (-0.5)
    position = jnp.arange(position_count)
    allowed = (position[None, :] <= position[:, None]) & (position[None, :] < length)
    return jnp.where(allowed[None], scores, masked_score)


def attend_forward(pieces):
    queries, rotated_keys, values_low, length = pieces
    scores = masked_scores(queries, rotated_keys, length)
    row_max = jnp.max(scores, axis=-1, keepdims=True)
    exponent = jnp.exp(scores - row_max)
    row_sum = jnp.sum(exponent, axis=-1, keepdims=True)
    weights = (exponent / row_sum).astype(jnp.bfloat16)
    mixed_heads = jnp.einsum(
        "hqk,khd->qhd", weights, values_low, preferred_element_type=jnp.float32
    )
    return (mixed_heads, row_max + jnp.log(row_sum))


def attend_backward(pieces):
    queries, rotated_keys, values_low, length, log_total, mixed_grad = pieces
    head_size = queries.shape[-1]
    scores = masked_scores(queries, rotated_keys, length)
    probability = jnp.exp(scores - log_total)
    value_grad = jnp.einsum(
        "hqk,qhd->khd",
        probability.astype(jnp.bfloat16),
        mixed_grad,
        preferred_element_type=jnp.float32,
    )
    probability_grad = jnp.einsum(
        "qhd,khd->hqk", mixed_grad, values_low, preferred_element_type=jnp.float32
    )
    inner_dot = jnp.sum(probability * probability_grad, axis=-1, keepdims=True)
    score_grad = (probability * (probability_grad - inner_dot) * head_size ** (-0.5)).astype(
        jnp.bfloat16
    )
    query_grad = jnp.einsum(
        "hqk,khd->qhd", score_grad, rotated_keys, preferred_element_type=jnp.float32
    )
    key_grad = jnp.einsum("hqk,qhd->khd", score_grad, queries, preferred_element_type=jnp.float32)
    return (query_grad, key_grad, value_grad)


def adam_update(weight, first, second, gradient, step_count, learn_rate):
    steps_taken = step_count[0].astype(jnp.float32)
    first_new = beta_first * first + (1.0 - beta_first) * gradient
    second_new = beta_second * second + (1.0 - beta_second) * gradient * gradient
    first_hat = first_new / (1.0 - beta_first**steps_taken)
    second_hat = second_new / (1.0 - beta_second**steps_taken)
    weight_new = weight - learn_rate[0] * (
        first_hat / (jnp.sqrt(second_hat) + adam_eps) + weight_decay * weight
    )
    return (gradient, weight_new, first_new, second_new)


class Gather:
    @staticmethod
    def scratch(tensors, chunks):
        return [DMA((tensors,)), DMA((chunks, 4)), DMA((chunks, 4)), DMA((chunks, 2, 3)), DMA((chunks, 2, 3))] + [DMA((chunks, 3, 2))] * 4

    def __init__(self, shapes, chunks, loc, full, sems):
        self.shapes, self.chunks, self.loc, self.full = shapes, chunks, loc, full
        (self.own_s, self.sib_s, self.sib_r, self.z_s, self.z_r, self.p_s, self.p_r, self.d_s, self.d_r) = sems
        self.rep, self.shard = lax.axis_index("rep"), lax.axis_index("shard")
        self.z, core = self.shard // 2, lax.rem(self.shard, 2)
        x, y = lax.rem(self.rep, 2), self.rep // 2
        self.sib = (self.rep, self.shard + 1 - 2 * core)
        self.nb = ((self.rep + 1 - 2 * x, self.shard), (self.rep + 2 - 4 * y, self.shard))
        self.diag = self.rep + (1 - 2 * x) + (2 - 4 * y)

    def barrier(self):
        bar = pltpu.get_barrier_semaphore()
        for dev in (self.sib,) + self.nb + tuple((self.rep, self.other(d)) for d in (1, 2, 3)):
            pl.semaphore_signal(bar, inc=1, device_id=dev, device_id_type=MESH)
        pl.semaphore_wait(bar, 6)

    def ref(self, c, s, q=None, half=None):
        t, r0, rows, c0, cols, axis = self.chunks[c]
        base, col, nr, nc = s * self.shapes[t][0] + r0, c0, rows, cols
        if q is not None:
            parts, i = (4, q) if half is None else (8, 2 * q + half)
            if axis == 0:
                nr = rows // parts
                base = base + i * nr
            else:
                nc = cols // parts
                col = pl.multiple_of(c0 + i * nc, 128)
        return self.full[t].at[pl.ds(pl.multiple_of(base, 16), nr), pl.ds(col, nc)]

    def loc_ref(self, c, q=None):
        t, r0, rows, c0, cols, axis = self.chunks[c]
        row, col, nr, nc = r0, c0, rows, cols
        if q is not None and axis == 0:
            nr = rows // 4
            row = pl.multiple_of(r0 + q * nr, 16)
        elif q is not None:
            nc = cols // 4
            col = pl.multiple_of(c0 + q * nc, 128)
        return self.loc[t].at[pl.ds(row, nr), pl.ds(col, nc)]

    def copy(self, src, dst, s, r, dev):
        return pltpu.make_async_remote_copy(src_ref=src, dst_ref=dst, send_sem=s, recv_sem=r, device_id=dev, device_id_type=MESH)

    def own(self, t):
        rows = self.shapes[t][0]
        return pltpu.make_async_copy(self.loc[t], self.full[t].at[pl.ds(pl.multiple_of(self.shard * rows, rows), rows), :], self.own_s.at[t])

    def other(self, dz):
        return lax.rem(self.shard + 2 * dz, 8)

    def sibling(self, c, dz):
        r = self.ref(c, self.other(dz))
        return self.copy(self.loc_ref(c) if dz == 0 else r, r, self.sib_s.at[c, dz], self.sib_r.at[c, dz], self.sib)

    def chain(self, c, side, h):
        sgn = 1 if side == 0 else -1
        s = self.shard - sgn * 2 * (h - 1)
        src = self.loc_ref(c, self.rep) if h == 1 else self.ref(c, s, self.rep)
        return self.copy(src, self.ref(c, s, self.rep), self.z_s.at[c, side, h - 1], self.z_r.at[c, side, h - 1], (self.rep, self.shard + sgn * 2))

    def chain_in(self, c, side, h):
        sgn = 1 if side == 0 else -1
        r = self.ref(c, self.shard - sgn * 2 * h, self.rep)
        return self.copy(r, r, self.z_s.at[c, side, h - 1], self.z_r.at[c, side, h - 1], (self.rep, self.shard - sgn * 2))

    def chain_sends(self, side, h):
        if side == 0:
            return jnp.logical_and(self.z < 3, self.z >= h - 1)
        return jnp.logical_and(self.z > 0, self.z <= 4 - h)

    def plane(self, c, dz, k, theirs=False):
        r = self.ref(c, self.other(dz), self.nb[k][0] if theirs else self.rep)
        return self.copy(r, r, self.p_s.at[c, dz - 1, k], self.p_r.at[c, dz - 1, k], self.nb[k])

    def corner(self, c, dz, k, theirs=False):
        r = self.ref(c, self.other(dz), self.diag if theirs else self.nb[k][0], k)
        return self.copy(r, r, self.d_s.at[c, dz - 1, k], self.d_r.at[c, dz - 1, k], self.nb[1 - k])

    def s0(self, c):
        for side in (0, 1):
            @pl.when(self.chain_sends(side, 1))
            def _():
                self.chain(c, side, 1).start()
        self.sibling(c, 0).start()

    def s1(self, c, h):
        for side in (0, 1):
            @pl.when((self.z >= h) if side == 0 else (self.z <= 3 - h))
            def _():
                self.chain_in(c, side, h).wait_recv()
                if h < 3:
                    @pl.when((self.z < 3) if side == 0 else (self.z > 0))
                    def _():
                        self.chain(c, side, h + 1).start()
                for k in (0, 1):
                    self.plane(c, (4 - h) if side == 0 else h, k).start()

    def s2(self, c):
        for dz in (1, 3, 2):
            for k in (0, 1):
                self.plane(c, dz, k, True).wait_recv()
                self.corner(c, dz, k).start()

    def s3(self, c):
        for dz in (1, 3, 2):
            for k in (0, 1):
                self.corner(c, dz, k, True).wait_recv()
            self.sibling(c, dz).start()

    def s4(self, c):
        for dz in range(4):
            self.sibling(c, dz).wait()

    def drain(self, c):
        for side in (0, 1):
            for h in (1, 2, 3):
                @pl.when(self.chain_sends(side, h))
                def _():
                    self.chain(c, side, h).wait_send()
        for dz in (1, 2, 3):
            for k in (0, 1):
                self.plane(c, dz, k).wait_send()
                self.corner(c, dz, k).wait_send()


def normed(v):
    c = v - jnp.mean(v, axis=-1, keepdims=True)
    inv = lax.rsqrt(jnp.mean(c * c, axis=-1, keepdims=True) + norm_eps)
    return c * inv, inv


def turn(w):
    lane = lax.broadcasted_iota(jnp.int32, w.shape, 1)
    return jnp.where(lax.rem(lane, 64) < 32, pltpu.roll(w, 96, 1), pltpu.roll(w, 32, 1))


def two_heads(w):
    lane = lax.broadcasted_iota(jnp.int32, w.shape, 1)
    zero = jnp.zeros_like(w)
    return jnp.concatenate([jnp.where(lane < 64, w, zero), jnp.where(lane < 64, zero, w)], axis=0)


def join_heads(w):
    n = w.shape[0] // 2
    lane = lax.broadcasted_iota(jnp.int32, (n, w.shape[1]), 1)
    return jnp.where(lane < 64, w[:n], w[n:])


def dot(a, b, da=1, db=0):
    return lax.dot_general(a, b, (((da,), (db,)), ((), ())), preferred_element_type=F32)


def probabilities(q2, keys, bias):
    n, width = q2.shape[0] // 2, keys.shape[0]
    s = dot(q2, keys, 1, 1) * 0.125 + bias
    row = lax.broadcasted_iota(jnp.int32, (n, 128), 0)
    col = lax.broadcasted_iota(jnp.int32, (n, 128), 1)
    causal = jnp.where(col <= row, 0.0, -1e30)
    last = s[:, width - 128:] + jnp.concatenate([causal, causal], axis=0)
    s = last if width == 128 else jnp.concatenate([s[:, :width - 128], last], axis=1)
    e = jnp.exp(s - jnp.max(s, axis=-1, keepdims=True))
    return e * (1.0 / jnp.sum(e, axis=-1, keepdims=True))


def forward_kernel(
    shapes, chunks,
    x_ref, bias_ref, cos_ref, sin_ref, win_h, wout_h, wgu_h, wdn_h,
    fin_h, fout_h, fgu_h, fdn_h, at_h, ot_h, bt_h, mt_h, qkv_h, slopes_h, h_h,
    win, wout, wgu, wdn, lin, lout, lgu, ldn, bin_, bout, bgu,
    a, at, qkv, o, ot, h, b, bt, mt, slopes, in_s, load_s, out_s, *sems,
):
    g = Gather(shapes, chunks, (lin, lout, lgu, ldn), (fin_h, fout_h, fgu_h, fdn_h), sems)
    rows = x_ref.shape[0]
    loads = [pltpu.make_async_copy(s, d, in_s.at[i]) for i, (s, d) in enumerate(((win_h, win), (wout_h, wout), (wgu_h, wgu), (wdn_h, wdn)))]
    for cp in loads:
        cp.start()
    outs = [pltpu.make_async_copy(s, d, out_s.at[i]) for i, (s, d) in enumerate(
        ((at, at_h), (ot, ot_h), (bt, bt_h), (mt, mt_h), (qkv, qkv_h), (slopes, slopes_h), (h, h_h)))]
    AT, OT, BT, MT, QKV, SL, H = range(7)
    g.barrier()

    def weight_in(t):
        loads[t].wait()
        if t == 0:
            for p in range(3):
                lin[:, 1024 * p:1024 * p + 1024] = win[p].astype(BF16)
        elif t == 1:
            lout[...] = wout[...].astype(BF16)
        elif t == 3:
            ldn[...] = wdn[...].astype(BF16)
        else:
            tiles = lgu.shape[1] // 128
            for c in range(tiles):
                lgu[:, 128 * c:128 * c + 128] = wgu[pl.ds(c, lgu.shape[0], stride=tiles), :].astype(BF16)
        g.own(t).start()

    def ln_one():
        for r in range(0, rows, 128):
            n, _ = normed(x_ref[r:r + 128, :].astype(F32))
            a[r:r + 128, :] = n.astype(BF16)
        for c in range(0, 1024, 128):
            at[c:c + 128, :] = a[:, c:c + 128].T
        outs[AT].start()

    def load(t, c0, n, dst):
        return pltpu.make_async_copy(g.full[t].at[:, pl.ds(c0, n)], dst.at[:, pl.ds(c0, n)], load_s.at[t])

    def project(p, j):
        c = 1024 * p + 256 * j
        w = dot(a[...], bin_[:, c:c + 256])
        for i in (0, 128):
            t = w[:, i:i + 128]
            if p < 2:
                t = t * cos_ref[...] + turn(t) * sin_ref[...]
            qkv[:, c + i:c + i + 128] = t.astype(BF16)

    def attend(pair):
        for qt in range(rows // 128):
            width = 128 * (qt + 1)
            lo = pl.multiple_of(pair * 128, 128)
            q2 = two_heads(qkv[128 * qt:width, pl.ds(lo, 128)])
            p = probabilities(q2, qkv[:width, pl.ds(pl.multiple_of(1024 + lo, 128), 128)], bias_ref[:, :width])
            mixed = join_heads(dot(p.astype(BF16), qkv[:width, pl.ds(pl.multiple_of(2048 + lo, 128), 128)]))
            o[128 * qt:width, pl.ds(lo, 128)] = mixed.astype(BF16)
        ot[pl.ds(lo, 128), :] = o[:, pl.ds(lo, 128)].T

    def out_and_norm():
        for r in range(0, rows, 256):
            v = x_ref[r:r + 256, :].astype(F32) + dot(o[r:r + 256, :], bout[...])
            h[r:r + 256, :] = v
            n, _ = normed(v)
            b[r:r + 256, :] = n.astype(BF16)
        outs[H].start()
        for c in range(0, 1024, 128):
            bt[c:c + 128, :] = b[:, c:c + 128].T
        outs[BT].start()

    def gate(ct):
        lo = pl.multiple_of(ct * 256, 256)
        w = dot(b[...], bgu[:, pl.ds(lo, 256)])
        gv, uv = w[:, :128], w[:, 128:]
        sig = jax.nn.sigmoid(gv)
        silu = gv * sig
        mt[pl.ds(pl.multiple_of(ct * 128, 128), 128), :] = (silu * uv).astype(BF16).T
        slopes[:, pl.ds(lo, 128)] = (uv * sig * (1.0 + gv * (1.0 - sig))).astype(BF16)
        slopes[:, pl.ds(pl.multiple_of(lo + 128, 128), 128)] = silu.astype(BF16)

    Q, O, G1, G2, D = range(5)
    half = chunks[G1][4]
    tiles = half // 256
    weight_in(0)
    g.s0(Q)
    weight_in(1)
    g.s0(O)
    ln_one()
    g.s1(Q, 1)
    weight_in(2)
    g.s1(Q, 2)
    g.s0(G1)
    g.s1(O, 1)
    g.s1(O, 2)
    g.s1(Q, 3)
    g.s2(Q)
    g.s0(G2)
    weight_in(3)
    g.s1(G1, 1)
    g.s1(G1, 2)
    g.s1(O, 3)
    g.s2(O)
    g.s3(Q)
    g.s0(D)
    g.s1(G2, 1)
    g.s4(Q)
    g.own(0).wait()
    ld = load(0, 0, chunks[Q][4], bin_)
    ld.start()
    g.s1(G2, 2)
    g.s1(G1, 3)
    ld.wait()
    between = {
        (0, 1): lambda: g.s2(G1), (1, 3): lambda: g.s3(O), (2, 3): lambda: g.s1(D, 1),
    }
    for p in range(3):
        for j in range(4):
            project(p, j)
            if (p, j) in between:
                between[p, j]()
    outs[QKV].start()
    steps = [lambda: g.s1(D, 2), lambda: g.s1(G2, 3), lambda: g.s2(G2), lambda: g.s3(G1)]
    for i in range(4):
        lax.fori_loop(2 * i, 2 * i + 2, lambda k, _: (attend(k), 0)[1], 0)
        steps[i]()
        if i == 1:
            g.s4(O)
            g.own(1).wait()
            ld = load(1, 0, 1024, bout)
            ld.start()
    outs[OT].start()
    ld.wait()
    out_and_norm()
    g.s1(D, 3)
    g.s2(D)
    g.own(2).wait()
    g.s4(G1)
    ld = load(2, 0, half, bgu)
    ld.start()
    g.s3(G2)
    ld.wait()
    mid = tiles // 2
    lax.fori_loop(0, mid, lambda k, _: (gate(k), 0)[1], 0)
    g.s4(G2)
    ld = load(2, half, half, bgu)
    ld.start()
    lax.fori_loop(mid, tiles, lambda k, _: (gate(k), 0)[1], 0)
    g.s3(D)
    ld.wait()
    lax.fori_loop(tiles, 2 * tiles, lambda k, _: (gate(k), 0)[1], 0)
    outs[MT].start()
    outs[SL].start()
    g.s4(D)
    g.own(3).wait()
    for c in range(len(chunks)):
        g.drain(c)
    for cp in outs:
        cp.wait()


def forward_call(x, bias, cos, sin, win, wout, wgu, wdn):
    rows, d = x.shape
    r = wout.shape[0]
    ff2 = wgu.shape[0] * 128 // r
    ff = ff2 // 2
    shapes = ((r, 3 * d), (r, d), (r, ff2), wdn.shape)
    chunks = ((0, 0, r, 0, 3 * d, 1), (1, 0, r, 0, d, 1), (2, 0, r, 0, ff, 0), (2, 0, r, ff, ff, 0), (3, 0, wdn.shape[0], 0, d, 1))
    vm, an = pl.BlockSpec(memory_space=pltpu.VMEM), pl.BlockSpec(memory_space=pl.ANY)
    sd = lambda s, t=BF16: jax.ShapeDtypeStruct(s, t)
    v = lambda s, t=BF16: pltpu.VMEM(s, t)
    outs = [sd((8 * s[0], s[1])) for s in shapes] + [sd((d, rows)), sd((d, rows)), sd((d, rows)), sd((ff, rows)), sd((rows, 3 * d)), sd((rows, ff2)), sd((rows, d), F32)]
    scratch = [v(win.shape, F32), v(wout.shape, F32), v(wgu.shape, F32), v(wdn.shape, F32)] + [v(s) for s in shapes]
    scratch += [v((8 * r, 3 * d)), v((8 * r, d)), v((8 * r, ff2))]
    scratch += [v((rows, d)), v((d, rows)), v((rows, 3 * d)), v((rows, d)), v((d, rows)), v((rows, d), F32), v((rows, d)), v((d, rows)), v((ff, rows)), v((rows, ff2))]
    scratch += [DMA((4,)), DMA((4,)), DMA((7,))] + Gather.scratch(4, len(chunks))
    return pl.pallas_call(
        functools.partial(forward_kernel, shapes, chunks),
        out_shape=outs, in_specs=[vm] * 4 + [an] * 4, out_specs=[an] * len(outs), scratch_shapes=scratch,
        compiler_params=pltpu.CompilerParams(collective_id=0, has_side_effects=True, vmem_limit_bytes=60 << 20),
    )(x, bias, cos, sin, win, wout, wgu, wdn)


class Reduce:
    def __init__(self, refs):
        (self.mine, self.theirs, self.held, self.sums, self.one, self.two, self.fin, self.planes, self.total,
         self.a_s, self.a_r, self.o_s, self.o_r, self.t_s, self.t_r, self.c_s, self.c_r, self.d_s, self.d_r, self.f_s, self.f_r) = refs
        self.rep, self.shard = lax.axis_index("rep"), lax.axis_index("shard")
        self.core = lax.rem(self.shard, 2)
        self.x, self.y = lax.rem(self.rep, 2), self.rep // 2
        self.sib = (self.rep, self.shard + 1 - 2 * self.core)
        self.nb = ((self.rep + 1 - 2 * self.x, self.shard), (self.rep + 2 - 4 * self.y, self.shard))

    @staticmethod
    def scratch(chunks, wide):
        v = lambda *s: pltpu.VMEM(s, BF16)
        return [
            v(RING, 8, 16, wide),
            v(RING, 8, 16, wide),
            pltpu.VMEM((2, 8, 16, wide), F32),
            v(RING, 8, 16, wide),
            v(2, RING, 2, 16, wide),
            v(2, RING, 16, wide),
            v(RING, 2, 16, wide),
            v(chunks, 3, 2, 16, wide),
        ], [DMA((RING,)), DMA((RING,)), DMA((2, RING)), DMA((2, RING)), DMA((2, RING)), DMA((2, RING)), DMA((RING,)), DMA((chunks, 3)),
            DMA((chunks, 2)), DMA((chunks, 2)), DMA((chunks, 2)), DMA((chunks, 2))]

    def copy(self, src, dst, s, r, dev):
        return pltpu.make_async_remote_copy(src_ref=src, dst_ref=dst, send_sem=s, recv_sem=r, device_id=dev, device_id_type=MESH)

    def barrier(self):
        bar = pltpu.get_barrier_semaphore()
        for dev in (self.sib,) + self.nb + tuple((self.rep, lax.rem(self.shard + 2 * d, 8)) for d in (1, 2, 3)):
            pl.semaphore_signal(bar, inc=1, device_id=dev, device_id_type=MESH)
        pl.semaphore_wait(bar, 6)

    def first(self, u, w):
        s = lax.rem(u, RING)
        return self.copy(self.mine.at[s, :, :, pl.ds(0, w)], self.theirs.at[s, :, :, pl.ds(0, w)], self.a_s.at[s], self.a_r.at[s], self.sib)

    def hop_one(self, u, w, k):
        s = lax.rem(u, RING)
        at = 2 - 2 * self.x if k == 0 else 6 - 2 * self.y
        return self.copy(self.sums.at[s, pl.ds(at, 2), :, pl.ds(0, w)], self.one.at[k, s, :, :, pl.ds(0, w)], self.o_s.at[k, s], self.o_r.at[k, s], self.nb[k])

    def hop_two(self, u, w, k):
        s = lax.rem(u, RING)
        at = 2 * self.x + 1 - self.y if k == 0 else 4 + 2 * self.y + 1 - self.x
        return self.copy(self.sums.at[s, at, :, pl.ds(0, w)], self.two.at[k, s, :, pl.ds(0, w)], self.t_s.at[k, s], self.t_r.at[k, s], self.nb[1 - k])

    def across(self, u, w, dz):
        s = lax.rem(u, RING)
        c = u // 4
        return self.copy(self.fin.at[s, :, :, pl.ds(0, w)], self.planes.at[c, 3 - dz, :, :, pl.ds(0, w)], self.c_s.at[s], self.c_r.at[c, 3 - dz], (self.rep, lax.rem(self.shard + 2 * dz, 8)))

    def plane_in(self, c, w, j):
        return self.copy(self.fin.at[0, :, :, pl.ds(0, w)], self.planes.at[c, j, :, :, pl.ds(0, w)], self.c_s.at[0], self.c_r.at[c, j], self.sib)

    def spread(self, c, w, k, own=True):
        q = self.rep if own else self.nb[k][0]
        ref = self.total.at[c, q, :, :, pl.ds(0, w)]
        return self.copy(ref, ref, self.d_s.at[c, k], self.d_r.at[c, k], self.nb[k])

    def spread_on(self, c, w, k, own=True):
        q = self.nb[k][0] if own else self.nb[0][0] + self.nb[1][0] - self.rep
        ref = self.total.at[c, q, k, :, pl.ds(0, w)]
        return self.copy(ref, ref, self.f_s.at[c, k], self.f_r.at[c, k], self.nb[1 - k])

    def stage_two(self, u, w):
        s = lax.rem(u, RING)
        self.first(u, w).wait()
        self.sums[s, :, :, :w] = (self.held[lax.rem(u, 2), :, :, :w] + self.theirs[s, :, :, :w].astype(F32)).astype(BF16)
        for k in (0, 1):
            self.hop_one(u, w, k).start()

    def stage_three(self, u, w):
        s = lax.rem(u, RING)
        for k in (0, 1):
            self.hop_one(u, w, k).wait()
            at = 2 * self.x if k == 0 else 4 + 2 * self.y
            new = self.sums[s, pl.ds(at, 2), :, :w].astype(F32) + self.one[k, s, :, :, :w].astype(F32)
            self.sums[s, pl.ds(at, 2), :, :w] = new.astype(BF16)
            self.hop_two(u, w, k).start()

    def stage_four(self, u, w, start):
        s = lax.rem(u, RING)
        c = u // 4
        dz = lax.rem(lax.rem(u, 4) + 1, 4)

        @pl.when(jnp.logical_and(u >= start + RING, dz > 0))
        def _():
            self.across(u - RING, w, dz).wait_send()

        for k in (0, 1):
            self.hop_two(u, w, k).wait()

        def plane_sum(k):
            at = 2 * self.x + self.y if k == 0 else 4 + 2 * self.y + self.x
            return self.sums[s, at, :, :w].astype(F32) + self.two[k, s, :, :w].astype(F32)

        @pl.when(dz > 0)
        def _():
            for k in (0, 1):
                self.fin[s, k, :, :w] = plane_sum(k).astype(BF16)
            self.across(u, w, dz).start()

        @pl.when(dz == 0)
        def _():
            for j in range(3):
                self.plane_in(c, w, j).wait_recv()
            for k in (0, 1):
                out = plane_sum(k)
                for j in range(3):
                    out = out + self.planes[c, j, k, :, :w].astype(F32)
                self.total[c, self.rep, k, :, :w] = out.astype(BF16)
            for k in (0, 1):
                self.spread(c, w, k).start()

    def stage_five(self, u, w):
        @pl.when(lax.rem(u, 4) == 3)
        def _():
            c = u // 4
            for k in (0, 1):
                self.spread(c, w, k, False).wait_recv()
                self.spread_on(c, w, k).start()

    def drain_across(self, units, w):
        for u in range(units - RING, units):
            if u % 4 != 3:
                self.across(u, w, u % 4 + 1).wait_send()

    def finish(self, units, width):
        self.drain_across(units, width(units - 1))
        for c in range(units // 4):
            w = width(4 * c)
            for k in (0, 1):
                self.spread(c, w, k).wait_send()
                self.spread_on(c, w, k).wait_send()
                self.spread_on(c, w, k, False).wait_recv()


def norm_back_rows(v, d):
    n, inv = normed(v)
    return inv * (d - jnp.mean(d, axis=-1, keepdims=True) - n * jnp.mean(d * n, axis=-1, keepdims=True))


def backward_kernel(
    wide,
    x_ref, dy, live, bias_ref, cos_ref, sin_ref, at_h, ot_h, bt_h, mt_h, qkv_h, slopes_h, h_h, fin_h, fout_h, fgu_h, fdn_h,
    total, out_h, grad_h,
    atl, bt, mt, qkv, dgu, h, wd, wb, wo, atr, do, acc, dh, dk, dv, ld_s, wb_s, st_s, *rs,
):
    r = Reduce(rs[:8] + (total,) + rs[8:])
    rows, d = x_ref.shape
    chunk_plan = ((0, 2, wide), (1, 4, wide), (2, 4, d))
    bounds, u0 = [], 0
    for kind, n, w in chunk_plan:
        bounds.append((u0, u0 + 4 * n, kind, w))
        u0 += 4 * n
    units = u0
    names = ("mt", "wd", "gu", "bt", "qkv", "h", "wo", "ot", "at")
    pairs = ((mt_h, mt), (fdn_h, wd), (slopes_h, dgu), (bt_h, bt), (qkv_h, qkv), (h_h, h), (fout_h, wo),
             (ot_h, atl.at[pl.ds(d, d), :]), (at_h, atl.at[pl.ds(0, d), :]))
    loads = {n: pltpu.make_async_copy(s, t, ld_s.at[i]) for i, (n, (s, t)) in enumerate(zip(names, pairs))}
    for n in names:
        loads[n].start()

    def weights(j):
        src = fgu_h.at[:, pl.ds(wide * j, wide)] if j < 4 else fin_h.at[:, pl.ds(d * (j - 4), d)]
        dst = wb.at[j % 2] if j < 4 else wb.at[j % 2, :, pl.ds(0, d)]
        return pltpu.make_async_copy(src, dst, wb_s.at[j % 2])

    def width(u):
        for a, b, _, w in bounds:
            if a <= u < b:
                return w

    def start_of(w):
        return min(a for a, _, _, v in bounds if v == w)

    def product(u, kind, first, own):
        c = u // 4 - first // 4
        zt = lax.rem(r.shard // 2 + lax.rem(u, 4) + 1, 4)
        core = r.core if own else 1 - r.core

        def put(e, lo, n, val):
            if own:
                r.held[lax.rem(u, 2), e, :, lo:lo + n] = val
            else:
                r.mine[lax.rem(u, RING), e, :, lo:lo + n] = val.astype(BF16)

        if kind == 0:
            part = mt.shape[0] // 16
            left = mt[pl.ds(pl.multiple_of((2 * zt + core) * 2 * part + c * part, 16), part), :]
            for e in range(0, 8, 2):
                val = dot(left, dy[:, e * 128:e * 128 + 256])
                for i in (0, 1):
                    for j in range(part // 16):
                        put(e + i, 128 * j, 128, val[16 * j:16 * j + 16, i * 128:i * 128 + 128])
            return
        base = (2 * zt + core) * 128
        if kind == 1:
            left = bt[pl.ds(pl.multiple_of(base, 128), 128), :]
            right, n = dgu[:, pl.ds(pl.multiple_of(c * wide, 128), wide)], wide
        else:
            left = atl[pl.ds(pl.multiple_of(base + jnp.where(c == 0, d, 0), 128), 128), :]
            right, n = atr[:, pl.ds(pl.multiple_of(c * d, 128), d)], d
        put(slice(None), 0, n, dot(left, right).reshape(8, 16, n))

    def tail(u, ws):
        if ws[1]:
            r.stage_two(u - 1, ws[1])
        if ws[2]:
            r.stage_three(u - 2, ws[2])
        if ws[3]:
            r.stage_four(u - 3, ws[3], start_of(ws[3]))
        if ws[4]:
            r.stage_five(u - 4, ws[4])

    def widths(u):
        return [width(u - k) if 0 <= u - k < units else None for k in range(5)]

    def step(u, kind, first, ws):
        product(u, kind, first, False)
        r.first(u, ws[0]).start()
        product(u, kind, first, True)
        tail(u, ws)

    def hidden(t):
        val = dot(dy[...], wd[pl.ds(pl.multiple_of(256 * t, 256), 256), :], 1, 1)
        for i in (0, 1):
            part = val[:, 128 * i:128 * i + 128]
            for j in (0, 1):
                at = pl.ds(pl.multiple_of(512 * t + 256 * i + 128 * j, 128), 128)
                dgu[:, at] = (part * dgu[:, at].astype(F32)).astype(BF16)

    def hidden_unit(u):
        hidden(u)
        tiles = mt.shape[0] // 256

        @pl.when(u + 8 < tiles)
        def _():
            hidden(u + 8)

    def input_two(j):
        weights(j).wait()
        val = dot(dgu[:, wide * j:wide * j + wide], wb[j % 2], 1, 1)
        acc[...] = val if j == 0 else acc[...] + val
        weights(j + 2).start()

    def norm_two():
        loads["h"].wait()
        for i in range(0, rows, 128):
            s = slice(i, i + 128)
            v = dy[s, :].astype(F32) + norm_back_rows(h[s, :], acc[s, :])
            dh[s, :] = v
            atr[s, :d] = v.astype(BF16)

    def mixed_grad():
        loads["wo"].wait()
        loads["qkv"].wait()
        do[...] = dot(atr[:, :d], wo[...], 1, 1).astype(BF16)

    def turn_back(t, s):
        return t * cos_ref[s, :] - turn(t) * sin_ref[s, :]

    def attend_back(pair):
        lo = pl.multiple_of(pair * 128, 128)
        lanes = [pl.ds(pl.multiple_of(lo + d * i, 128), 128) for i in range(4)]
        for qt in reversed(range(rows // 128)):
            n = 128 * (qt + 1)
            s = slice(128 * qt, n)
            keys = qkv[:n, lanes[1]]
            q2, g2 = two_heads(qkv[s, lanes[0]]), two_heads(do[s, lanes[0]])
            p = probabilities(q2, keys, bias_ref[:, :n])
            dp = dot(g2, qkv[:n, lanes[2]], 1, 1)
            ds = (p * (dp - jnp.sum(p * dp, axis=-1, keepdims=True)) * 0.125).astype(BF16)
            new_v, new_k = dot(p.astype(BF16), g2, 0, 0), dot(ds, q2, 0, 0)
            if n == rows:
                dv[...] = new_v
                dk[...] = new_k
            else:
                dv[:n, :] = dv[:n, :] + new_v
                dk[:n, :] = dk[:n, :] + new_k
            atr[s, lanes[1]] = turn_back(join_heads(dot(ds, keys)), s).astype(BF16)
        every = slice(0, rows)
        atr[:, lanes[2]] = turn_back(dk[...], every).astype(BF16)
        atr[:, lanes[3]] = dv[...].astype(BF16)

    def input_one(j):
        weights(4 + j).wait()
        val = dot(atr[:, d * (j + 1):d * (j + 2)], wb[j % 2, :, :d], 1, 1)
        acc[...] = val if j == 0 else acc[...] + val
        if j == 0:
            weights(6).start()

    grad_out = pltpu.make_async_copy(dh, grad_h, st_s.at[0])
    result_out = pltpu.make_async_copy(do, out_h, st_s.at[1])

    def norm_one():
        for i in range(0, rows, 128):
            s = slice(i, i + 128)
            dh[s, :] = dh[s, :] + norm_back_rows(x_ref[s, :].astype(F32), acc[s, :])
        grad_out.start()

    def result(i):
        s = slice(256 * i, 256 * i + 256)
        do[s, :] = ((h[s, :] + dot(mt[:, s], wd[...], 0, 0)) * live[s, :]).astype(BF16)

    before = {0: lambda: loads["mt"].wait(), 8: lambda: loads["bt"].wait(), 24: lambda: loads["ot"].wait(), 28: lambda: loads["at"].wait()}
    fill = {8 + j: functools.partial(input_two, j) for j in range(4)}
    fill[12] = norm_two
    fill[13] = mixed_grad
    fill.update({29 + 2 * j: functools.partial(input_one, j) for j in range(3)})
    fill[35] = norm_one
    fill[36] = lambda: result(0)
    fill[37] = lambda: (result(1), result_out.start())
    ranged = [(0, 8, hidden_unit), (14, 22, lambda u: attend_back(u - 14))]

    weights(0).start()
    weights(1).start()
    r.barrier()
    edges = sorted({a for a, _, _, _ in bounds} | {e for a, b, _ in ranged for e in (a, b)} | {units} | set(before))
    u = 0
    while u < units:
        if u in before:
            before[u]()
        if u == 0:
            ready = False
        ws = widths(u)
        first, _, kind, w = next(b for b in bounds if b[0] <= u < b[1])
        in_range = next((f for a, b, f in ranged if a <= u < b), None)
        end = min(e for e in edges if e > u)
        plain = all(x == w for x in ws) and u not in fill
        stop = u
        while plain and stop < end and stop not in fill:
            stop += 1
        if plain and stop - u > 1:
            def body(i, _, kind=kind, first=first, ws=ws, f=in_range):
                step(i, kind, first, ws)
                if f:
                    f(i)
                return 0
            lax.fori_loop(u, stop, body, 0)
            u = stop
            continue
        if ws[3] and u - 3 == start_of(ws[3]) and u > 3:
            r.drain_across(u - 3, width(u - 4))
        step(jnp.int32(u), kind, first, ws)
        if in_range:
            if u == 0:
                loads["wd"].wait()
                loads["gu"].wait()
            in_range(jnp.int32(u))
        if u in fill:
            fill[u]()
        u += 1
    for u in range(units, units + 4):
        tail(jnp.int32(u), widths(u))
    r.finish(units, width)
    grad_out.wait()
    result_out.wait()


def backward_call(x, dy, live, bias, cos, sin, saved, full):
    rows, d = x.shape
    ff = saved[3].shape[0]
    wide = 2 * ff // 4
    chunks = 10
    vm, an = pl.BlockSpec(memory_space=pltpu.VMEM), pl.BlockSpec(memory_space=pl.ANY)
    v = lambda s, t=BF16: pltpu.VMEM(s, t)
    bufs, sems = Reduce.scratch(chunks, wide)
    scratch = [v((2 * d, rows)), v((d, rows)), v((ff, rows)), v((rows, 3 * d)), v((rows, 2 * ff)), v((rows, d), F32), v((ff, d)), v((2, d, wide)), v((d, d)),
               v((rows, 4 * d)), v((rows, d)), v((rows, d), F32), v((rows, d), F32), v((rows, 128), F32), v((rows, 128), F32), DMA((9,)), DMA((2,)), DMA((2,))]
    return pl.pallas_call(
        functools.partial(backward_kernel, wide),
        out_shape=[jax.ShapeDtypeStruct((chunks, 4, 2, 16, wide), BF16), jax.ShapeDtypeStruct((rows, d), BF16), jax.ShapeDtypeStruct((rows, d), F32)],
        in_specs=[vm] * 6 + [an] * 11, out_specs=[vm, an, an], scratch_shapes=scratch + bufs + sems,
        compiler_params=pltpu.CompilerParams(collective_id=1, has_side_effects=True, vmem_limit_bytes=63 << 20),
    )(x, dy, live, bias, cos, sin, *saved, *full)


def pieces(total, c, w):
    t = total[c, :, :, :, :w]
    return jnp.stack([t[0, 0], t[2, 0], t[1, 0], t[3, 0]] + [t[i, 1] for i in range(4)])


def unpack(total, wide, d):
    down = [pieces(total, c, wide).reshape(8, 16, wide // 128, 128).transpose(2, 1, 0, 3).reshape(-1, d) for c in (0, 1)]
    gate_up = [pieces(total, c, wide).reshape(128, wide) for c in (2, 3, 4, 5)]
    attention = [pieces(total, c, d).reshape(128, d) for c in (6, 7, 8, 9)]
    return jnp.concatenate(down, 0), jnp.concatenate(gate_up, 1), attention[0], jnp.stack(attention[1:], 1)


def gather_full(local, rep_count, rep_index):
    rows = local.shape[0]
    flat = local.reshape(rows, -1)
    width = flat.shape[1] // rep_count
    piece = lax.dynamic_slice_in_dim(flat, rep_index * width, width, axis=1)
    column = lax.all_gather(piece, "shard", axis=0, tiled=True)
    return lax.all_gather(column, "rep", axis=0, tiled=False)


def reduce_full(partial):
    part = lax.psum_scatter(partial, "rep", scatter_dimension=0, tiled=False)
    part = lax.psum_scatter(part, "shard", scatter_dimension=0, tiled=True)
    pieces = lax.all_gather(part, "rep", axis=0, tiled=False)
    rows = pieces.shape[1]
    return jnp.transpose(pieces, (1, 0, 2)).reshape(rows, -1).astype(jnp.float32)


def shards_generic(
    tokens,
    cotangent,
    lengths,
    slot_sequence,
    step_count,
    learn_rate,
    attention_in,
    attention_in_first,
    attention_in_second,
    attention_out,
    attention_out_first,
    attention_out_second,
    gate_up_weight,
    gate_up_first,
    gate_up_second,
    down_weight,
    down_first,
    down_second,
):
    slot_count, position_count, feature_count = tokens.shape
    row_total = slot_count * position_count
    head_count = feature_count // HD
    shaped = (slot_count, position_count, head_count, HD)
    inputs = tokens.astype(jnp.float32).reshape(row_total, feature_count)
    matches = jnp.arange(lengths.shape[0])[None, :] == slot_sequence[:, None]
    slot_length = jnp.sum(jnp.where(matches, lengths[None, :], 0), axis=1)
    alive_rows = (
        (jnp.arange(position_count)[None, :] < slot_length[:, None])
        .astype(jnp.float32)
        .reshape(row_total, 1)
    )
    cosine_table, sine_table = rope_tables(position_count, HD)
    in_local = attention_in.astype(jnp.bfloat16)
    out_local = attention_out.astype(jnp.bfloat16)
    gate_up_local = gate_up_weight.astype(jnp.bfloat16)
    down_local = down_weight.astype(jnp.bfloat16)
    rep_count = lax.axis_size("rep")
    rep_index = lax.axis_index("rep")
    in_full = gather_full(in_local, rep_count, rep_index)
    out_full = gather_full(out_local, rep_count, rep_index)
    gate_up_full = gather_full(gate_up_local, rep_count, rep_index)
    down_full = gather_full(down_local, rep_count, rep_index)
    normed_one, inverse_one = layer_norm(inputs)
    first_input = normed_one.astype(jnp.bfloat16)
    projected = jnp.einsum(
        "rd,qde->rqe", first_input, in_full, preferred_element_type=jnp.float32
    ).reshape(row_total, 3, feature_count)
    queries = rotate(projected[:, 0].reshape(shaped), cosine_table, sine_table).astype(jnp.bfloat16)
    rotated_keys = rotate(projected[:, 1].reshape(shaped), cosine_table, sine_table).astype(
        jnp.bfloat16
    )
    values_low = projected[:, 2].reshape(shaped).astype(jnp.bfloat16)
    mixed_heads, log_total = lax.map(
        attend_forward, (queries, rotated_keys, values_low, slot_length)
    )
    mixed_low = mixed_heads.reshape(row_total, feature_count).astype(jnp.bfloat16)
    residual = inputs + jnp.einsum(
        "rd,qde->rqe", mixed_low, out_full, preferred_element_type=jnp.float32
    ).reshape(row_total, feature_count)
    normed_two, inverse_two = layer_norm(residual)
    second_input = normed_two.astype(jnp.bfloat16)
    gate_up = jnp.einsum(
        "rd,qdf->rqf", second_input, gate_up_full, preferred_element_type=jnp.float32
    ).reshape(row_total, 2, -1)
    gate_value = gate_up[:, 0]
    up_value = gate_up[:, 1]
    sigmoid_gate = jax.nn.sigmoid(gate_value)
    hidden_low = (gate_value * sigmoid_gate * up_value).astype(jnp.bfloat16)
    result = residual + jnp.einsum(
        "rf,qfe->rqe", hidden_low, down_full, preferred_element_type=jnp.float32
    ).reshape(row_total, feature_count)
    output = (result * alive_rows).astype(jnp.bfloat16).reshape(tokens.shape)
    output_grad = cotangent.astype(jnp.float32).reshape(row_total, feature_count) * alive_rows
    result_grad_low = output_grad.astype(jnp.bfloat16)
    hidden_grad = jnp.einsum(
        "rqe,qfe->rf",
        result_grad_low.reshape(row_total, rep_count, -1),
        down_full,
        preferred_element_type=jnp.float32,
    )
    gate_grad = hidden_grad * up_value * sigmoid_gate * (1.0 + gate_value * (1.0 - sigmoid_gate))
    up_grad = hidden_grad * gate_value * sigmoid_gate
    gate_up_grad_low = (
        jnp.concatenate([gate_grad, up_grad], axis=1)
        .astype(jnp.bfloat16)
        .reshape(row_total, rep_count, -1)
    )
    second_input_grad = jnp.einsum(
        "rqf,qdf->rd", gate_up_grad_low, gate_up_full, preferred_element_type=jnp.float32
    )
    residual_grad = output_grad + norm_back(normed_two, inverse_two, second_input_grad)
    down_part = reduce_full(
        jnp.einsum(
            "rc,rqe->qce",
            hidden_low,
            result_grad_low.reshape(row_total, rep_count, -1),
            preferred_element_type=jnp.float32,
        ).astype(jnp.bfloat16)
    )
    gate_up_part = reduce_full(
        jnp.einsum(
            "rc,rqf->qcf", second_input, gate_up_grad_low, preferred_element_type=jnp.float32
        ).astype(jnp.bfloat16)
    ).reshape(gate_up_weight.shape)
    branch_grad = residual_grad.astype(jnp.bfloat16)
    mixed_grad = (
        jnp.einsum(
            "rqe,qde->rd",
            branch_grad.reshape(row_total, rep_count, -1),
            out_full,
            preferred_element_type=jnp.float32,
        )
        .astype(jnp.bfloat16)
        .reshape(shaped)
    )
    query_grad, key_grad, value_grad = lax.map(
        attend_backward, (queries, rotated_keys, values_low, slot_length, log_total, mixed_grad)
    )
    query_back = rotate(query_grad, cosine_table, -sine_table).reshape(row_total, feature_count)
    key_back = rotate(key_grad, cosine_table, -sine_table).reshape(row_total, feature_count)
    projected_grad = (
        jnp.concatenate([query_back, key_back, value_grad.reshape(row_total, feature_count)], axis=1)
        .astype(jnp.bfloat16)
        .reshape(row_total, rep_count, -1)
    )
    first_input_grad = jnp.einsum(
        "rqe,qde->rd", projected_grad, in_full, preferred_element_type=jnp.float32
    )
    input_grad = (residual_grad + norm_back(normed_one, inverse_one, first_input_grad)).reshape(
        tokens.shape
    )
    in_part = reduce_full(
        jnp.einsum(
            "rc,rqe->qce", first_input, projected_grad, preferred_element_type=jnp.float32
        ).astype(jnp.bfloat16)
    ).reshape(attention_in.shape)
    out_part = reduce_full(
        jnp.einsum(
            "rc,rqe->qce",
            mixed_low,
            branch_grad.reshape(row_total, rep_count, -1),
            preferred_element_type=jnp.float32,
        ).astype(jnp.bfloat16)
    )
    in_grad, in_new, in_first, in_second = adam_update(
        attention_in,
        attention_in_first,
        attention_in_second,
        in_part,
        step_count,
        learn_rate,
    )
    out_grad, out_new, out_first, out_second = adam_update(
        attention_out,
        attention_out_first,
        attention_out_second,
        out_part,
        step_count,
        learn_rate,
    )
    gu_grad, gu_new, gu_first, gu_second = adam_update(
        gate_up_weight, gate_up_first, gate_up_second, gate_up_part, step_count, learn_rate
    )
    dn_grad, dn_new, dn_first, dn_second = adam_update(
        down_weight, down_first, down_second, down_part, step_count, learn_rate
    )
    return (
        output,
        input_grad,
        in_grad,
        in_new,
        in_first,
        in_second,
        out_grad,
        out_new,
        out_first,
        out_second,
        gu_grad,
        gu_new,
        gu_first,
        gu_second,
        dn_grad,
        dn_new,
        dn_first,
        dn_second,
    )


def shards_fast(
    tokens,
    cotangent,
    lengths,
    slot_sequence,
    step_count,
    learn_rate,
    attention_in,
    attention_in_first,
    attention_in_second,
    attention_out,
    attention_out_first,
    attention_out_second,
    gate_up_weight,
    gate_up_first,
    gate_up_second,
    down_weight,
    down_first,
    down_second,
):
    _, rows, d = tokens.shape
    x = tokens.reshape(rows, d)
    matches = jnp.arange(lengths.shape[0]) == slot_sequence[0]
    length = jnp.sum(jnp.where(matches, lengths, 0))
    alive = jnp.arange(rows) < length
    live = alive.astype(F32)[:, None]
    bias = jnp.where(alive, 0.0, masked_score)[None].astype(F32)
    dy = jnp.where(alive[:, None], cotangent.reshape(rows, d), jnp.zeros((), BF16))
    cosine, sine = rope_tables(rows, HD)
    sign = jnp.where(jnp.arange(HD) < HD // 2, -1.0, 1.0)
    cosine = jnp.tile(cosine[:, 0], (1, 2))
    sine = jnp.tile(sine[:, 0] * sign, (1, 2))
    owned, _, ff = gate_up_weight.shape
    tiled = gate_up_weight.reshape(owned, 2, ff // 128, 128).transpose(0, 2, 1, 3).reshape(-1, 128)
    results = forward_call(x, bias, cosine, sine, attention_in.transpose(1, 0, 2), attention_out, tiled, down_weight)
    full, saved = results[:4], results[4:]
    total, output, input_grad = backward_call(x, dy, live, bias, cosine, sine, saved, full)
    output = output.reshape(tokens.shape)
    input_grad = input_grad.reshape(tokens.shape)
    down_part, gate_up_part, out_part, in_part = [part.astype(F32) for part in unpack(total, ff // 2, d)]
    gate_up_part = gate_up_part.reshape(owned, ff // 128, 2, 128).transpose(0, 2, 1, 3).reshape(owned, 2, ff)
    in_grad, in_new, in_first, in_second = adam_update(
        attention_in,
        attention_in_first,
        attention_in_second,
        in_part,
        step_count,
        learn_rate,
    )
    out_grad, out_new, out_first, out_second = adam_update(
        attention_out,
        attention_out_first,
        attention_out_second,
        out_part,
        step_count,
        learn_rate,
    )
    gu_grad, gu_new, gu_first, gu_second = adam_update(
        gate_up_weight, gate_up_first, gate_up_second, gate_up_part, step_count, learn_rate
    )
    dn_grad, dn_new, dn_first, dn_second = adam_update(
        down_weight, down_first, down_second, down_part, step_count, learn_rate
    )
    return (
        output,
        input_grad,
        in_grad,
        in_new,
        in_first,
        in_second,
        out_grad,
        out_new,
        out_first,
        out_second,
        gu_grad,
        gu_new,
        gu_first,
        gu_second,
        dn_grad,
        dn_new,
        dn_first,
        dn_second,
    )


def solution(mesh):
    fast = mesh.shape["rep"] == 4 and mesh.shape["shard"] == 8
    return jax.shard_map(
        shards_fast if fast else shards_generic,
        mesh=mesh,
        in_specs=(
            P(("rep", "shard"), None, None),
            P(("rep", "shard"), None, None),
            P(),
            P(("rep", "shard")),
            P(),
            P(),
            P("shard", None, None),
            P("shard", None, None),
            P("shard", None, None),
            P("shard", None),
            P("shard", None),
            P("shard", None),
            P("shard", None, None),
            P("shard", None, None),
            P("shard", None, None),
            P("shard", None),
            P("shard", None),
            P("shard", None),
        ),
        out_specs=(
            P(("rep", "shard"), None, None),
            P(("rep", "shard"), None, None),
            P("shard", None, None),
            P("shard", None, None),
            P("shard", None, None),
            P("shard", None, None),
            P("shard", None),
            P("shard", None),
            P("shard", None),
            P("shard", None),
            P("shard", None, None),
            P("shard", None, None),
            P("shard", None, None),
            P("shard", None, None),
            P("shard", None),
            P("shard", None),
            P("shard", None),
            P("shard", None),
        ),
        check_vma=False,
    )
```

```python
import functools

import jax
import jax.numpy as jnp
import numpy as np
from jax import lax
from jax.experimental import pallas as pl
from jax.experimental.layout import Layout, with_layout_constraint
from jax.experimental.pallas import tpu as pltpu
from jax.sharding import PartitionSpec as P

MESH = pl.DeviceIdType.MESH
DMA = pltpu.SemaphoreType.DMA
RING = 4
rowwise = Layout(major_to_minor=(0, 1, 2, 3))
F32, BF16 = jnp.float32, jnp.bfloat16

HD = 64


norm_eps = 1e-05
beta_first = 0.9
beta_second = 0.95
adam_eps = 1e-08
weight_decay = 0.1
rope_base = 10000.0
masked_score = -1e30


def layer_norm(values):
    centered = values - jnp.mean(values, axis=-1, keepdims=True)
    inverse = lax.rsqrt(jnp.mean(centered * centered, axis=-1, keepdims=True) + norm_eps)
    return (centered * inverse, inverse)


def norm_back(normed, inverse, upstream):
    mean_grad = jnp.mean(upstream, axis=-1, keepdims=True)
    mean_dot = jnp.mean(upstream * normed, axis=-1, keepdims=True)
    return inverse * (upstream - mean_grad - normed * mean_dot)


def rope_tables(position_count, head_size):
    half_size = head_size // 2
    frequency = rope_base ** (-(jnp.arange(half_size, dtype=jnp.float32) * 2.0 / head_size))
    angles = jnp.arange(position_count, dtype=jnp.float32)[:, None] * frequency[None, :]
    angles = jnp.concatenate([angles, angles], axis=1)
    return (jnp.cos(angles)[:, None, :], jnp.sin(angles)[:, None, :])


def half_turns(position_count, head_size):
    half_size = head_size // 2
    frequency = np.float32(rope_base) ** (-(np.arange(half_size, dtype=np.float32) * np.float32(2.0) / np.float32(head_size)))
    angles = np.arange(position_count, dtype=np.float32)[:, None] * frequency[None, :]
    cosine, sine = np.cos(angles), np.sin(angles)
    return (
        jnp.asarray(np.concatenate([cosine] * 4, axis=1), jnp.float32),
        jnp.asarray(np.concatenate([-sine, sine] * 2, axis=1), jnp.float32),
    )


def rotate(values, cosine_table, sine_table):
    half_size = values.shape[-1] // 2
    turned = jnp.concatenate([-values[..., half_size:], values[..., :half_size]], axis=-1)
    return values * cosine_table + turned * sine_table


def masked_scores(queries, rotated_keys, length):
    position_count, head_size = (queries.shape[0], queries.shape[-1])
    scores = jnp.einsum(
        "qhd,khd->hqk", queries, rotated_keys, preferred_element_type=jnp.float32
    ) * head_size ** (-0.5)
    position = jnp.arange(position_count)
    allowed = (position[None, :] <= position[:, None]) & (position[None, :] < length)
    return jnp.where(allowed[None], scores, masked_score)


def attend_forward(pieces):
    queries, rotated_keys, values_low, length = pieces
    scores = masked_scores(queries, rotated_keys, length)
    row_max = jnp.max(scores, axis=-1, keepdims=True)
    exponent = jnp.exp(scores - row_max)
    row_sum = jnp.sum(exponent, axis=-1, keepdims=True)
    weights = (exponent / row_sum).astype(jnp.bfloat16)
    mixed_heads = jnp.einsum(
        "hqk,khd->qhd", weights, values_low, preferred_element_type=jnp.float32
    )
    return (mixed_heads, row_max + jnp.log(row_sum))


def attend_backward(pieces):
    queries, rotated_keys, values_low, length, log_total, mixed_grad = pieces
    head_size = queries.shape[-1]
    scores = masked_scores(queries, rotated_keys, length)
    probability = jnp.exp(scores - log_total)
    value_grad = jnp.einsum(
        "hqk,qhd->khd",
        probability.astype(jnp.bfloat16),
        mixed_grad,
        preferred_element_type=jnp.float32,
    )
    probability_grad = jnp.einsum(
        "qhd,khd->hqk", mixed_grad, values_low, preferred_element_type=jnp.float32
    )
    inner_dot = jnp.sum(probability * probability_grad, axis=-1, keepdims=True)
    score_grad = (probability * (probability_grad - inner_dot) * head_size ** (-0.5)).astype(
        jnp.bfloat16
    )
    query_grad = jnp.einsum(
        "hqk,khd->qhd", score_grad, rotated_keys, preferred_element_type=jnp.float32
    )
    key_grad = jnp.einsum("hqk,qhd->khd", score_grad, queries, preferred_element_type=jnp.float32)
    return (query_grad, key_grad, value_grad)


def adam_update(weight, first, second, gradient, step_count, learn_rate):
    steps_taken = step_count[0].astype(jnp.float32)
    first_new = beta_first * first + (1.0 - beta_first) * gradient
    second_new = beta_second * second + (1.0 - beta_second) * gradient * gradient
    first_hat = first_new / (1.0 - beta_first**steps_taken)
    second_hat = second_new / (1.0 - beta_second**steps_taken)
    weight_new = weight - learn_rate[0] * (
        first_hat / (jnp.sqrt(second_hat) + adam_eps) + weight_decay * weight
    )
    return (gradient, weight_new, first_new, second_new)


class Gather:
    @staticmethod
    def scratch(tensors, chunks):
        return [DMA((tensors,)), DMA((chunks, 4)), DMA((chunks, 4)), DMA((chunks, 2, 3)), DMA((chunks, 2, 3))] + [DMA((chunks, 3, 2))] * 4

    def __init__(self, shapes, chunks, loc, full, sems):
        self.shapes, self.chunks, self.loc, self.full = shapes, chunks, loc, full
        (self.own_s, self.sib_s, self.sib_r, self.z_s, self.z_r, self.p_s, self.p_r, self.d_s, self.d_r) = sems
        self.rep, self.shard = lax.axis_index("rep"), lax.axis_index("shard")
        self.z, core = self.shard // 2, lax.rem(self.shard, 2)
        x, y = lax.rem(self.rep, 2), self.rep // 2
        self.sib = (self.rep, self.shard + 1 - 2 * core)
        self.nb = ((self.rep + 1 - 2 * x, self.shard), (self.rep + 2 - 4 * y, self.shard))
        self.diag = self.rep + (1 - 2 * x) + (2 - 4 * y)

    def barrier(self):
        bar = pltpu.get_barrier_semaphore()
        for dev in (self.sib,) + self.nb + tuple((self.rep, self.other(d)) for d in (1, 2, 3)):
            pl.semaphore_signal(bar, inc=1, device_id=dev, device_id_type=MESH)
        pl.semaphore_wait(bar, 6)

    def ref(self, c, s, q=None, half=None):
        t, r0, rows, c0, cols, axis = self.chunks[c]
        base, col, nr, nc = s * self.shapes[t][0] + r0, c0, rows, cols
        if q is not None:
            parts, i = (4, q) if half is None else (8, 2 * q + half)
            if axis == 0:
                nr = rows // parts
                base = base + i * nr
            else:
                nc = cols // parts
                col = pl.multiple_of(c0 + i * nc, 128)
        return self.full[t].at[pl.ds(pl.multiple_of(base, 16), nr), pl.ds(col, nc)]

    def loc_ref(self, c, q=None):
        t, r0, rows, c0, cols, axis = self.chunks[c]
        row, col, nr, nc = r0, c0, rows, cols
        if q is not None and axis == 0:
            nr = rows // 4
            row = pl.multiple_of(r0 + q * nr, 16)
        elif q is not None:
            nc = cols // 4
            col = pl.multiple_of(c0 + q * nc, 128)
        return self.loc[t].at[pl.ds(row, nr), pl.ds(col, nc)]

    def copy(self, src, dst, s, r, dev):
        return pltpu.make_async_remote_copy(src_ref=src, dst_ref=dst, send_sem=s, recv_sem=r, device_id=dev, device_id_type=MESH)

    def own(self, t):
        rows = self.shapes[t][0]
        return pltpu.make_async_copy(self.loc[t], self.full[t].at[pl.ds(pl.multiple_of(self.shard * rows, rows), rows), :], self.own_s.at[t])

    def other(self, dz):
        return lax.rem(self.shard + 2 * dz, 8)

    def sibling(self, c, dz):
        r = self.ref(c, self.other(dz))
        return self.copy(self.loc_ref(c) if dz == 0 else r, r, self.sib_s.at[c, dz], self.sib_r.at[c, dz], self.sib)

    def chain(self, c, side, h):
        sgn = 1 if side == 0 else -1
        s = self.shard - sgn * 2 * (h - 1)
        src = self.loc_ref(c, self.rep) if h == 1 else self.ref(c, s, self.rep)
        return self.copy(src, self.ref(c, s, self.rep), self.z_s.at[c, side, h - 1], self.z_r.at[c, side, h - 1], (self.rep, self.shard + sgn * 2))

    def chain_in(self, c, side, h):
        sgn = 1 if side == 0 else -1
        r = self.ref(c, self.shard - sgn * 2 * h, self.rep)
        return self.copy(r, r, self.z_s.at[c, side, h - 1], self.z_r.at[c, side, h - 1], (self.rep, self.shard - sgn * 2))

    def chain_sends(self, side, h):
        if side == 0:
            return jnp.logical_and(self.z < 3, self.z >= h - 1)
        return jnp.logical_and(self.z > 0, self.z <= 4 - h)

    def plane(self, c, dz, k, theirs=False):
        r = self.ref(c, self.other(dz), self.nb[k][0] if theirs else self.rep)
        return self.copy(r, r, self.p_s.at[c, dz - 1, k], self.p_r.at[c, dz - 1, k], self.nb[k])

    def corner(self, c, dz, k, theirs=False):
        r = self.ref(c, self.other(dz), self.diag if theirs else self.nb[k][0], k)
        return self.copy(r, r, self.d_s.at[c, dz - 1, k], self.d_r.at[c, dz - 1, k], self.nb[1 - k])

    def s0(self, c):
        for side in (0, 1):
            @pl.when(self.chain_sends(side, 1))
            def _():
                self.chain(c, side, 1).start()
        self.sibling(c, 0).start()

    def s1(self, c, h):
        for side in (0, 1):
            @pl.when((self.z >= h) if side == 0 else (self.z <= 3 - h))
            def _():
                self.chain_in(c, side, h).wait_recv()
                if h < 3:
                    @pl.when((self.z < 3) if side == 0 else (self.z > 0))
                    def _():
                        self.chain(c, side, h + 1).start()
                for k in (0, 1):
                    self.plane(c, (4 - h) if side == 0 else h, k).start()

    def s2(self, c):
        for dz in (1, 3, 2):
            for k in (0, 1):
                self.plane(c, dz, k, True).wait_recv()
                self.corner(c, dz, k).start()

    def s3(self, c):
        for dz in (1, 3, 2):
            for k in (0, 1):
                self.corner(c, dz, k, True).wait_recv()
            self.sibling(c, dz).start()

    def s4(self, c):
        for dz in range(4):
            self.sibling(c, dz).wait()

    def drain(self, c):
        for side in (0, 1):
            for h in (1, 2, 3):
                @pl.when(self.chain_sends(side, h))
                def _():
                    self.chain(c, side, h).wait_send()
        for dz in (1, 2, 3):
            for k in (0, 1):
                self.plane(c, dz, k).wait_send()
                self.corner(c, dz, k).wait_send()


def normed(v):
    c = v - jnp.mean(v, axis=-1, keepdims=True)
    inv = lax.rsqrt(jnp.mean(c * c, axis=-1, keepdims=True) + norm_eps)
    return c * inv, inv


def turn(w):
    lane = lax.broadcasted_iota(jnp.int32, w.shape, 1)
    return jnp.where(lax.rem(lane, 64) < 32, pltpu.roll(w, 96, 1), pltpu.roll(w, 32, 1))


def two_heads(w):
    lane = lax.broadcasted_iota(jnp.int32, w.shape, 1)
    zero = jnp.zeros_like(w)
    return jnp.concatenate([jnp.where(lane < 64, w, zero), jnp.where(lane < 64, zero, w)], axis=0)


def join_heads(w):
    n = w.shape[0] // 2
    lane = lax.broadcasted_iota(jnp.int32, (n, w.shape[1]), 1)
    return jnp.where(lane < 64, w[:n], w[n:])


def dot(a, b, da=1, db=0):
    return lax.dot_general(a, b, (((da,), (db,)), ((), ())), preferred_element_type=F32)


def key_bias(ref, length):
    ref[...] = jnp.where(lax.broadcasted_iota(jnp.int32, ref.shape, 1) < length, 0.0, -1e30)


def probabilities(q2, keys, bias):
    n, width = q2.shape[0] // 2, keys.shape[0]
    s = dot(q2, keys, 1, 1) * 0.125 + bias
    row = lax.broadcasted_iota(jnp.int32, (n, 128), 0)
    col = lax.broadcasted_iota(jnp.int32, (n, 128), 1)
    causal = jnp.where(col <= row, 0.0, -1e30)
    last = s[:, width - 128:] + jnp.concatenate([causal, causal], axis=0)
    s = last if width == 128 else jnp.concatenate([s[:, :width - 128], last], axis=1)
    e = jnp.exp(s - jnp.max(s, axis=-1, keepdims=True))
    return e * (1.0 / jnp.sum(e, axis=-1, keepdims=True))


def forward_kernel(
    shapes, chunks,
    x_ref, cos_ref, sin_ref, lengths, slot, win_h, wout_h, wgu_h, wdn_h,
    fin_h, fout_h, fgu_h, fdn_h, at_h, ot_h, bt_h, mt_h, qkv_h, slopes_h, h_h,
    win, wout, wgu, wdn, lin, lout, lgu, ldn, bin_, bout, bgu,
    a, at, qkv, o, ot, h, b, bt, mt, slopes, bias_ref, in_s, load_s, out_s, *sems,
):
    g = Gather(shapes, chunks, (lin, lout, lgu, ldn), (fin_h, fout_h, fgu_h, fdn_h), sems)
    rows = x_ref.shape[0]
    loads = [pltpu.make_async_copy(s, d, in_s.at[i]) for i, (s, d) in enumerate(((win_h, win), (wout_h, wout), (wgu_h, wgu), (wdn_h, wdn)))]
    for cp in loads:
        cp.start()
    outs = [pltpu.make_async_copy(s, d, out_s.at[i]) for i, (s, d) in enumerate(
        ((at, at_h), (ot, ot_h), (bt, bt_h), (mt, mt_h), (qkv, qkv_h), (slopes, slopes_h), (h, h_h)))]
    AT, OT, BT, MT, QKV, SL, H = range(7)
    g.barrier()
    key_bias(bias_ref, lengths[slot[0]])

    def weight_in(t):
        loads[t].wait()
        if t == 0:
            for p in range(3):
                lin[:, 1024 * p:1024 * p + 1024] = win[p].astype(BF16)
        elif t == 1:
            lout[...] = wout[...].astype(BF16)
        elif t == 3:
            ldn[...] = wdn[...].astype(BF16)
        else:
            tiles = lgu.shape[1] // 128
            for c in range(tiles):
                lgu[:, 128 * c:128 * c + 128] = wgu[pl.ds(c, lgu.shape[0], stride=tiles), :].astype(BF16)
        g.own(t).start()

    def ln_one():
        for r in range(0, rows, 128):
            n, _ = normed(x_ref[r:r + 128, :].astype(F32))
            a[r:r + 128, :] = n.astype(BF16)
        for c in range(0, 1024, 128):
            at[c:c + 128, :] = a[:, c:c + 128].T
        outs[AT].start()

    def load(t, c0, n, dst):
        return pltpu.make_async_copy(g.full[t].at[:, pl.ds(c0, n)], dst.at[:, pl.ds(c0, n)], load_s.at[t])

    def project(p, j):
        c = 1024 * p + 256 * j
        w = dot(a[...], bin_[:, c:c + 256])
        for i in (0, 128):
            t = w[:, i:i + 128]
            if p < 2:
                t = t * cos_ref[...] + turn(t) * sin_ref[...]
            qkv[:, c + i:c + i + 128] = t.astype(BF16)

    def attend(pair):
        for qt in range(rows // 128):
            width = 128 * (qt + 1)
            lo = pl.multiple_of(pair * 128, 128)
            q2 = two_heads(qkv[128 * qt:width, pl.ds(lo, 128)])
            p = probabilities(q2, qkv[:width, pl.ds(pl.multiple_of(1024 + lo, 128), 128)], bias_ref[:, :width])
            mixed = join_heads(dot(p.astype(BF16), qkv[:width, pl.ds(pl.multiple_of(2048 + lo, 128), 128)]))
            o[128 * qt:width, pl.ds(lo, 128)] = mixed.astype(BF16)
        ot[pl.ds(lo, 128), :] = o[:, pl.ds(lo, 128)].T

    def out_and_norm():
        for r in range(0, rows, 256):
            v = x_ref[r:r + 256, :].astype(F32) + dot(o[r:r + 256, :], bout[...])
            h[r:r + 256, :] = v
            n, _ = normed(v)
            b[r:r + 256, :] = n.astype(BF16)
        outs[H].start()
        for c in range(0, 1024, 128):
            bt[c:c + 128, :] = b[:, c:c + 128].T
        outs[BT].start()

    def gate(ct):
        lo = pl.multiple_of(ct * 256, 256)
        w = dot(b[...], bgu[:, pl.ds(lo, 256)])
        gv, uv = w[:, :128], w[:, 128:]
        sig = jax.nn.sigmoid(gv)
        silu = gv * sig
        mt[pl.ds(pl.multiple_of(ct * 128, 128), 128), :] = (silu * uv).astype(BF16).T
        slopes[:, pl.ds(lo, 128)] = (uv * sig * (1.0 + gv * (1.0 - sig))).astype(BF16)
        slopes[:, pl.ds(pl.multiple_of(lo + 128, 128), 128)] = silu.astype(BF16)

    Q, O, G1, G2, D = range(5)
    half = chunks[G1][4]
    tiles = half // 256
    weight_in(0)
    g.s0(Q)
    weight_in(1)
    g.s0(O)
    ln_one()
    g.s1(Q, 1)
    weight_in(2)
    g.s1(Q, 2)
    g.s0(G1)
    g.s1(O, 1)
    g.s1(O, 2)
    g.s1(Q, 3)
    g.s2(Q)
    g.s0(G2)
    weight_in(3)
    g.s1(G1, 1)
    g.s1(G1, 2)
    g.s1(O, 3)
    g.s2(O)
    g.s3(Q)
    g.s0(D)
    g.s1(G2, 1)
    g.s4(Q)
    g.own(0).wait()
    ld = load(0, 0, chunks[Q][4], bin_)
    ld.start()
    g.s1(G2, 2)
    g.s1(G1, 3)
    ld.wait()
    between = {
        (0, 1): lambda: g.s2(G1), (1, 3): lambda: g.s3(O), (2, 3): lambda: g.s1(D, 1),
    }
    for p in range(3):
        for j in range(4):
            project(p, j)
            if (p, j) in between:
                between[p, j]()
    outs[QKV].start()
    steps = [lambda: g.s1(D, 2), lambda: g.s1(G2, 3), lambda: g.s2(G2), lambda: g.s3(G1)]
    for i in range(4):
        lax.fori_loop(2 * i, 2 * i + 2, lambda k, _: (attend(k), 0)[1], 0)
        steps[i]()
        if i == 1:
            g.s4(O)
            g.own(1).wait()
            ld = load(1, 0, 1024, bout)
            ld.start()
    outs[OT].start()
    ld.wait()
    out_and_norm()
    g.s1(D, 3)
    g.s2(D)
    g.own(2).wait()
    g.s4(G1)
    ld = load(2, 0, half, bgu)
    ld.start()
    g.s3(G2)
    ld.wait()
    mid = tiles // 2
    lax.fori_loop(0, mid, lambda k, _: (gate(k), 0)[1], 0)
    g.s4(G2)
    ld = load(2, half, half, bgu)
    ld.start()
    lax.fori_loop(mid, tiles, lambda k, _: (gate(k), 0)[1], 0)
    g.s3(D)
    ld.wait()
    lax.fori_loop(tiles, 2 * tiles, lambda k, _: (gate(k), 0)[1], 0)
    outs[MT].start()
    outs[SL].start()
    g.s4(D)
    g.own(3).wait()
    for c in range(len(chunks)):
        g.drain(c)
    for cp in outs:
        cp.wait()


def forward_call(x, cos, sin, lengths, slot, win, wout, wgu, wdn):
    rows, d = x.shape
    r = wout.shape[0]
    ff2 = wgu.shape[0] * 128 // r
    ff = ff2 // 2
    shapes = ((r, 3 * d), (r, d), (r, ff2), wdn.shape)
    chunks = ((0, 0, r, 0, 3 * d, 1), (1, 0, r, 0, d, 1), (2, 0, r, 0, ff, 0), (2, 0, r, ff, ff, 0), (3, 0, wdn.shape[0], 0, d, 1))
    vm, an, sm = (pl.BlockSpec(memory_space=m) for m in (pltpu.VMEM, pl.ANY, pltpu.SMEM))
    sd = lambda s, t=BF16: jax.ShapeDtypeStruct(s, t)
    v = lambda s, t=BF16: pltpu.VMEM(s, t)
    outs = [sd((8 * s[0], s[1])) for s in shapes] + [sd((d, rows)), sd((d, rows)), sd((d, rows)), sd((ff, rows)), sd((rows, 3 * d)), sd((rows, ff2)), sd((rows, d), F32)]
    scratch = [v(win.shape, F32), v(wout.shape, F32), v(wgu.shape, F32), v(wdn.shape, F32)] + [v(s) for s in shapes]
    scratch += [v((8 * r, 3 * d)), v((8 * r, d)), v((8 * r, ff2))]
    scratch += [v((rows, d)), v((d, rows)), v((rows, 3 * d)), v((rows, d)), v((d, rows)), v((rows, d), F32), v((rows, d)), v((d, rows)), v((ff, rows)), v((rows, ff2)), v((1, rows), F32)]
    scratch += [DMA((4,)), DMA((4,)), DMA((7,))] + Gather.scratch(4, len(chunks))
    return pl.pallas_call(
        functools.partial(forward_kernel, shapes, chunks),
        out_shape=outs, in_specs=[vm] * 3 + [sm] * 2 + [an] * 4, out_specs=[an] * len(outs), scratch_shapes=scratch,
        compiler_params=pltpu.CompilerParams(collective_id=0, has_side_effects=True, vmem_limit_bytes=60 << 20),
    )(x, cos, sin, lengths, slot, win, wout, wgu, wdn)


class Reduce:
    def __init__(self, refs):
        (self.mine, self.theirs, self.held, self.sums, self.one, self.two, self.fin, self.planes, self.total,
         self.a_s, self.a_r, self.o_s, self.o_r, self.t_s, self.t_r, self.c_s, self.c_r, self.d_s, self.d_r, self.f_s, self.f_r) = refs
        self.rep, self.shard = lax.axis_index("rep"), lax.axis_index("shard")
        self.core = lax.rem(self.shard, 2)
        self.x, self.y = lax.rem(self.rep, 2), self.rep // 2
        self.sib = (self.rep, self.shard + 1 - 2 * self.core)
        self.nb = ((self.rep + 1 - 2 * self.x, self.shard), (self.rep + 2 - 4 * self.y, self.shard))

    @staticmethod
    def scratch(chunks, wide):
        v = lambda *s: pltpu.VMEM(s, BF16)
        return [
            v(RING, 8, 16, wide),
            v(RING, 8, 16, wide),
            pltpu.VMEM((2, 8, 16, wide), F32),
            v(RING, 8, 16, wide),
            v(2, RING, 2, 16, wide),
            v(2, RING, 16, wide),
            v(RING, 2, 16, wide),
            v(chunks, 3, 2, 16, wide),
        ], [DMA((RING,)), DMA((RING,)), DMA((2, RING)), DMA((2, RING)), DMA((2, RING)), DMA((2, RING)), DMA((RING,)), DMA((chunks, 3)),
            DMA((chunks, 2)), DMA((chunks, 2)), DMA((chunks, 2)), DMA((chunks, 2))]

    def copy(self, src, dst, s, r, dev):
        return pltpu.make_async_remote_copy(src_ref=src, dst_ref=dst, send_sem=s, recv_sem=r, device_id=dev, device_id_type=MESH)

    def barrier(self):
        bar = pltpu.get_barrier_semaphore()
        for dev in (self.sib,) + self.nb + tuple((self.rep, lax.rem(self.shard + 2 * d, 8)) for d in (1, 2, 3)):
            pl.semaphore_signal(bar, inc=1, device_id=dev, device_id_type=MESH)
        pl.semaphore_wait(bar, 6)

    def first(self, u, w):
        s = lax.rem(u, RING)
        return self.copy(self.mine.at[s, :, :, pl.ds(0, w)], self.theirs.at[s, :, :, pl.ds(0, w)], self.a_s.at[s], self.a_r.at[s], self.sib)

    def hop_one(self, u, w, k):
        s = lax.rem(u, RING)
        at = 2 - 2 * self.x if k == 0 else 6 - 2 * self.y
        return self.copy(self.sums.at[s, pl.ds(at, 2), :, pl.ds(0, w)], self.one.at[k, s, :, :, pl.ds(0, w)], self.o_s.at[k, s], self.o_r.at[k, s], self.nb[k])

    def hop_two(self, u, w, k):
        s = lax.rem(u, RING)
        at = 2 * self.x + 1 - self.y if k == 0 else 4 + 2 * self.y + 1 - self.x
        return self.copy(self.sums.at[s, at, :, pl.ds(0, w)], self.two.at[k, s, :, pl.ds(0, w)], self.t_s.at[k, s], self.t_r.at[k, s], self.nb[1 - k])

    def across(self, u, w, dz):
        s = lax.rem(u, RING)
        c = u // 4
        return self.copy(self.fin.at[s, :, :, pl.ds(0, w)], self.planes.at[c, 3 - dz, :, :, pl.ds(0, w)], self.c_s.at[s], self.c_r.at[c, 3 - dz], (self.rep, lax.rem(self.shard + 2 * dz, 8)))

    def plane_in(self, c, w, j):
        return self.copy(self.fin.at[0, :, :, pl.ds(0, w)], self.planes.at[c, j, :, :, pl.ds(0, w)], self.c_s.at[0], self.c_r.at[c, j], self.sib)

    def spread(self, c, w, k, own=True):
        q = self.rep if own else self.nb[k][0]
        ref = self.total.at[c, q, :, :, pl.ds(0, w)]
        return self.copy(ref, ref, self.d_s.at[c, k], self.d_r.at[c, k], self.nb[k])

    def spread_on(self, c, w, k, own=True):
        q = self.nb[k][0] if own else self.nb[0][0] + self.nb[1][0] - self.rep
        ref = self.total.at[c, q, k, :, pl.ds(0, w)]
        return self.copy(ref, ref, self.f_s.at[c, k], self.f_r.at[c, k], self.nb[1 - k])

    def stage_two(self, u, w):
        s = lax.rem(u, RING)
        self.first(u, w).wait()
        self.sums[s, :, :, :w] = (self.held[lax.rem(u, 2), :, :, :w] + self.theirs[s, :, :, :w].astype(F32)).astype(BF16)
        for k in (0, 1):
            self.hop_one(u, w, k).start()

    def stage_three(self, u, w):
        s = lax.rem(u, RING)
        for k in (0, 1):
            self.hop_one(u, w, k).wait()
            at = 2 * self.x if k == 0 else 4 + 2 * self.y
            new = self.sums[s, pl.ds(at, 2), :, :w].astype(F32) + self.one[k, s, :, :, :w].astype(F32)
            self.sums[s, pl.ds(at, 2), :, :w] = new.astype(BF16)
            self.hop_two(u, w, k).start()

    def stage_four(self, u, w, start):
        s = lax.rem(u, RING)
        c = u // 4
        dz = lax.rem(lax.rem(u, 4) + 1, 4)

        @pl.when(jnp.logical_and(u >= start + RING, dz > 0))
        def _():
            self.across(u - RING, w, dz).wait_send()

        for k in (0, 1):
            self.hop_two(u, w, k).wait()

        def plane_sum(k):
            at = 2 * self.x + self.y if k == 0 else 4 + 2 * self.y + self.x
            return self.sums[s, at, :, :w].astype(F32) + self.two[k, s, :, :w].astype(F32)

        @pl.when(dz > 0)
        def _():
            for k in (0, 1):
                self.fin[s, k, :, :w] = plane_sum(k).astype(BF16)
            self.across(u, w, dz).start()

        @pl.when(dz == 0)
        def _():
            for j in range(3):
                self.plane_in(c, w, j).wait_recv()
            for k in (0, 1):
                out = plane_sum(k)
                for j in range(3):
                    out = out + self.planes[c, j, k, :, :w].astype(F32)
                self.total[c, self.rep, k, :, :w] = out.astype(BF16)
            for k in (0, 1):
                self.spread(c, w, k).start()

    def stage_five(self, u, w):
        @pl.when(lax.rem(u, 4) == 3)
        def _():
            c = u // 4
            for k in (0, 1):
                self.spread(c, w, k, False).wait_recv()
                self.spread_on(c, w, k).start()

    def drain_across(self, units, w):
        for u in range(units - RING, units):
            if u % 4 != 3:
                self.across(u, w, u % 4 + 1).wait_send()

    def finish(self, units, width):
        self.drain_across(units, width(units - 1))
        for c in range(units // 4):
            w = width(4 * c)
            for k in (0, 1):
                self.spread(c, w, k).wait_send()
                self.spread_on(c, w, k).wait_send()
                self.spread_on(c, w, k, False).wait_recv()


def norm_back_rows(v, d):
    n, inv = normed(v)
    return inv * (d - jnp.mean(d, axis=-1, keepdims=True) - n * jnp.mean(d * n, axis=-1, keepdims=True))


def backward_kernel(
    wide,
    x_ref, cot_ref, cos_ref, sin_ref, lengths, slot, at_h, ot_h, bt_h, mt_h, qkv_h, slopes_h, h_h, fin_h, fout_h, fgu_h, fdn_h,
    total, out_h, grad_h,
    atl, bt, mt, qkv, dgu, h, wd, wb, wo, atr, do, acc, dh, dk, dv, dy, bias_ref, ld_s, wb_s, st_s, *rs,
):
    r = Reduce(rs[:8] + (total,) + rs[8:])
    rows, d = x_ref.shape
    chunk_plan = ((0, 2, wide), (1, 4, wide), (2, 4, d))
    bounds, u0 = [], 0
    for kind, n, w in chunk_plan:
        bounds.append((u0, u0 + 4 * n, kind, w))
        u0 += 4 * n
    units = u0
    names = ("mt", "wd", "gu", "bt", "qkv", "h", "wo", "ot", "at")
    pairs = ((mt_h, mt), (fdn_h, wd), (slopes_h, dgu), (bt_h, bt), (qkv_h, qkv), (h_h, h), (fout_h, wo),
             (ot_h, atl.at[pl.ds(d, d), :]), (at_h, atl.at[pl.ds(0, d), :]))
    loads = {n: pltpu.make_async_copy(s, t, ld_s.at[i]) for i, (n, (s, t)) in enumerate(zip(names, pairs))}
    for n in names:
        loads[n].start()

    def weights(j):
        src = fgu_h.at[:, pl.ds(wide * j, wide)] if j < 4 else fin_h.at[:, pl.ds(d * (j - 4), d)]
        dst = wb.at[j % 2] if j < 4 else wb.at[j % 2, :, pl.ds(0, d)]
        return pltpu.make_async_copy(src, dst, wb_s.at[j % 2])

    def width(u):
        for a, b, _, w in bounds:
            if a <= u < b:
                return w

    def start_of(w):
        return min(a for a, _, _, v in bounds if v == w)

    def product(u, kind, first, own):
        c = u // 4 - first // 4
        zt = lax.rem(r.shard // 2 + lax.rem(u, 4) + 1, 4)
        core = r.core if own else 1 - r.core

        def put(e, lo, n, val):
            if own:
                r.held[lax.rem(u, 2), e, :, lo:lo + n] = val
            else:
                r.mine[lax.rem(u, RING), e, :, lo:lo + n] = val.astype(BF16)

        if kind == 0:
            part = mt.shape[0] // 16
            left = mt[pl.ds(pl.multiple_of((2 * zt + core) * 2 * part + c * part, 16), part), :]
            for e in range(0, 8, 2):
                val = dot(left, dy[:, e * 128:e * 128 + 256])
                for i in (0, 1):
                    for j in range(part // 16):
                        put(e + i, 128 * j, 128, val[16 * j:16 * j + 16, i * 128:i * 128 + 128])
            return
        base = (2 * zt + core) * 128
        if kind == 1:
            left = bt[pl.ds(pl.multiple_of(base, 128), 128), :]
            right, n = dgu[:, pl.ds(pl.multiple_of(c * wide, 128), wide)], wide
        else:
            left = atl[pl.ds(pl.multiple_of(base + jnp.where(c == 0, d, 0), 128), 128), :]
            right, n = atr[:, pl.ds(pl.multiple_of(c * d, 128), d)], d
        put(slice(None), 0, n, dot(left, right).reshape(8, 16, n))

    def tail(u, ws):
        if ws[1]:
            r.stage_two(u - 1, ws[1])
        if ws[2]:
            r.stage_three(u - 2, ws[2])
        if ws[3]:
            r.stage_four(u - 3, ws[3], start_of(ws[3]))
        if ws[4]:
            r.stage_five(u - 4, ws[4])

    def widths(u):
        return [width(u - k) if 0 <= u - k < units else None for k in range(5)]

    def step(u, kind, first, ws):
        product(u, kind, first, False)
        r.first(u, ws[0]).start()
        product(u, kind, first, True)
        tail(u, ws)

    def hidden(t):
        val = dot(dy[...], wd[pl.ds(pl.multiple_of(256 * t, 256), 256), :], 1, 1)
        for i in (0, 1):
            part = val[:, 128 * i:128 * i + 128]
            for j in (0, 1):
                at = pl.ds(pl.multiple_of(512 * t + 256 * i + 128 * j, 128), 128)
                dgu[:, at] = (part * dgu[:, at].astype(F32)).astype(BF16)

    def hidden_unit(u):
        hidden(u)
        tiles = mt.shape[0] // 256

        @pl.when(u + 8 < tiles)
        def _():
            hidden(u + 8)

    def input_two(j):
        weights(j).wait()
        val = dot(dgu[:, wide * j:wide * j + wide], wb[j % 2], 1, 1)
        acc[...] = val if j == 0 else acc[...] + val
        weights(j + 2).start()

    def norm_two():
        loads["h"].wait()
        for i in range(0, rows, 128):
            s = slice(i, i + 128)
            v = dy[s, :].astype(F32) + norm_back_rows(h[s, :], acc[s, :])
            dh[s, :] = v
            atr[s, :d] = v.astype(BF16)

    def mixed_grad():
        loads["wo"].wait()
        loads["qkv"].wait()
        do[...] = dot(atr[:, :d], wo[...], 1, 1).astype(BF16)

    def turn_back(t, s):
        return t * cos_ref[s, :] - turn(t) * sin_ref[s, :]

    def attend_back(pair):
        lo = pl.multiple_of(pair * 128, 128)
        lanes = [pl.ds(pl.multiple_of(lo + d * i, 128), 128) for i in range(4)]
        for qt in reversed(range(rows // 128)):
            n = 128 * (qt + 1)
            s = slice(128 * qt, n)
            keys = qkv[:n, lanes[1]]
            q2, g2 = two_heads(qkv[s, lanes[0]]), two_heads(do[s, lanes[0]])
            p = probabilities(q2, keys, bias_ref[:, :n])
            dp = dot(g2, qkv[:n, lanes[2]], 1, 1)
            ds = (p * (dp - jnp.sum(p * dp, axis=-1, keepdims=True)) * 0.125).astype(BF16)
            new_v, new_k = dot(p.astype(BF16), g2, 0, 0), dot(ds, q2, 0, 0)
            if n == rows:
                dv[...] = new_v
                dk[...] = new_k
            else:
                dv[:n, :] = dv[:n, :] + new_v
                dk[:n, :] = dk[:n, :] + new_k
            atr[s, lanes[1]] = turn_back(join_heads(dot(ds, keys)), s).astype(BF16)
        every = slice(0, rows)
        atr[:, lanes[2]] = turn_back(dk[...], every).astype(BF16)
        atr[:, lanes[3]] = dv[...].astype(BF16)

    def input_one(j):
        weights(4 + j).wait()
        val = dot(atr[:, d * (j + 1):d * (j + 2)], wb[j % 2, :, :d], 1, 1)
        acc[...] = val if j == 0 else acc[...] + val
        if j == 0:
            weights(6).start()

    grad_out = pltpu.make_async_copy(dh, grad_h, st_s.at[0])
    result_out = pltpu.make_async_copy(do, out_h, st_s.at[1])

    def norm_one():
        for i in range(0, rows, 128):
            s = slice(i, i + 128)
            dh[s, :] = dh[s, :] + norm_back_rows(x_ref[s, :].astype(F32), acc[s, :])
        grad_out.start()

    def result(i):
        s = slice(256 * i, 256 * i + 256)
        do[s, :] = jnp.where(alive(256 * i, 256), h[s, :] + dot(mt[:, s], wd[...], 0, 0), 0.0).astype(BF16)

    before = {0: lambda: loads["mt"].wait(), 8: lambda: loads["bt"].wait(), 24: lambda: loads["ot"].wait(), 28: lambda: loads["at"].wait()}
    fill = {8 + j: functools.partial(input_two, j) for j in range(4)}
    fill[12] = norm_two
    fill[13] = mixed_grad
    fill.update({29 + 2 * j: functools.partial(input_one, j) for j in range(3)})
    fill[35] = norm_one
    fill[36] = lambda: result(0)
    fill[37] = lambda: (result(1), result_out.start())
    ranged = [(0, 8, hidden_unit), (14, 22, lambda u: attend_back(u - 14))]

    weights(0).start()
    weights(1).start()
    length = lengths[slot[0]]

    def alive(first, n):
        return lax.broadcasted_iota(jnp.int32, (n, d), 0) + first < length

    for i in range(0, rows, 128):
        s = slice(i, i + 128)
        dy[s, :] = jnp.where(alive(i, 128), cot_ref[s, :].astype(F32), 0.0).astype(BF16)
    key_bias(bias_ref, length)
    r.barrier()
    edges = sorted({a for a, _, _, _ in bounds} | {e for a, b, _ in ranged for e in (a, b)} | {units} | set(before))
    u = 0
    while u < units:
        if u in before:
            before[u]()
        if u == 0:
            ready = False
        ws = widths(u)
        first, _, kind, w = next(b for b in bounds if b[0] <= u < b[1])
        in_range = next((f for a, b, f in ranged if a <= u < b), None)
        end = min(e for e in edges if e > u)
        plain = all(x == w for x in ws) and u not in fill
        stop = u
        while plain and stop < end and stop not in fill:
            stop += 1
        if plain and stop - u > 1:
            def body(i, _, kind=kind, first=first, ws=ws, f=in_range):
                step(i, kind, first, ws)
                if f:
                    f(i)
                return 0
            lax.fori_loop(u, stop, body, 0)
            u = stop
            continue
        if ws[3] and u - 3 == start_of(ws[3]) and u > 3:
            r.drain_across(u - 3, width(u - 4))
        step(jnp.int32(u), kind, first, ws)
        if in_range:
            if u == 0:
                loads["wd"].wait()
                loads["gu"].wait()
            in_range(jnp.int32(u))
        if u in fill:
            fill[u]()
        u += 1
    for u in range(units, units + 4):
        tail(jnp.int32(u), widths(u))
    r.finish(units, width)
    grad_out.wait()
    result_out.wait()


def backward_call(x, cot, cos, sin, lengths, slot, saved, full):
    rows, d = x.shape
    ff = saved[3].shape[0]
    wide = 2 * ff // 4
    chunks = 10
    vm, an, sm = (pl.BlockSpec(memory_space=m) for m in (pltpu.VMEM, pl.ANY, pltpu.SMEM))
    v = lambda s, t=BF16: pltpu.VMEM(s, t)
    bufs, sems = Reduce.scratch(chunks, wide)
    scratch = [v((2 * d, rows)), v((d, rows)), v((ff, rows)), v((rows, 3 * d)), v((rows, 2 * ff)), v((rows, d), F32), v((ff, d)), v((2, d, wide)), v((d, d)),
               v((rows, 4 * d)), v((rows, d)), v((rows, d), F32), v((rows, d), F32), v((rows, 128), F32), v((rows, 128), F32), v((rows, d)), v((1, rows), F32), DMA((9,)), DMA((2,)), DMA((2,))]
    return pl.pallas_call(
        functools.partial(backward_kernel, wide),
        out_shape=[jax.ShapeDtypeStruct((chunks, 4, 2, 16, wide), BF16), jax.ShapeDtypeStruct((rows, d), BF16), jax.ShapeDtypeStruct((rows, d), F32)],
        in_specs=[vm] * 4 + [sm] * 2 + [an] * 11, out_specs=[vm, an, an], scratch_shapes=scratch + bufs + sems,
        compiler_params=pltpu.CompilerParams(collective_id=1, has_side_effects=True, vmem_limit_bytes=63 << 20),
    )(x, cot, cos, sin, lengths, slot, *saved, *full)


def adam_kernel(scalars, total, *refs):
    masters, outs, spread = refs[:12], refs[12:28], refs[28]
    first_scale, second_scale, rate = scalars[0], scalars[1], scalars[2]
    wide = total.shape[-1]
    cols = wide // 128
    d = masters[3].shape[1]

    def update(k, at, grad):
        w, m, v = (masters[3 * k + j][at] for j in range(3))
        m = beta_first * m + (1.0 - beta_first) * grad
        v = beta_second * v + (1.0 - beta_second) * grad * grad
        outs[4 * k][at] = grad
        outs[4 * k + 1][at] = w - rate * (m * first_scale / (jnp.sqrt(v * second_scale) + adam_eps) + weight_decay * w)
        outs[4 * k + 2][at] = m
        outs[4 * k + 3][at] = v

    def piece(c, lo, n):
        return total[c, 0, 0, :, lo:lo + n].astype(F32)

    for p in range(3):
        update(0, (p,), piece(7 + p, 0, d))
    update(1, (slice(None),), piece(6, 0, d))
    stride = 4 * cols
    for c in range(4):
        for j in range(cols):
            spread[pl.ds(c * cols + j, 16, stride=stride), :] = piece(2 + c, 128 * j, 128)
    for i in range(0, 16 * stride, 176):
        s = (slice(i, i + 176),)
        update(2, s, spread[s])
    half = 16 * cols
    for c in (0, 1):
        for j in range(cols):
            update(3, (slice(c * half + 16 * j, c * half + 16 * j + 16),), piece(c, 128 * j, 128))


def adam_call(scalars, total, masters):
    chunks, _, _, _, wide = total.shape
    blocks = []
    for k, shape in enumerate((masters[0].shape, masters[3].shape, masters[6].shape, masters[9].shape)):
        if k == 0:
            blocks.append(pl.BlockSpec((3, shape[1] // 8, shape[2]), lambda i: (0, i, 0)))
        elif k < 3:
            blocks.append(pl.BlockSpec((shape[0] // 8, shape[1]), lambda i: (i, 0)))
        else:
            blocks.append(pl.BlockSpec((shape[0], shape[1] // 8), lambda i: (0, i)))

    def part(i):
        low = lax.rem(i, 2) * 2 + i // 2
        return (0, jnp.where(i < 4, low, i - 4), i // 4, 0, 0)

    shapes = [masters[3 * k].shape for k in range(4) for _ in range(4)]
    return pl.pallas_call(
        adam_kernel,
        grid=(8,),
        out_shape=[jax.ShapeDtypeStruct(s, F32) for s in shapes],
        in_specs=[pl.BlockSpec(memory_space=pltpu.SMEM), pl.BlockSpec((chunks, 1, 1, 16, wide), part)] + [blocks[k] for k in range(4) for _ in range(3)],
        out_specs=[blocks[k] for k in range(4) for _ in range(4)],
        scratch_shapes=[pltpu.VMEM((masters[6].shape[0] // 8, 128), F32)],
        compiler_params=pltpu.CompilerParams(vmem_limit_bytes=60 << 20),
    )(scalars, total, *masters)


def gather_full(local, rep_count, rep_index):
    rows = local.shape[0]
    flat = local.reshape(rows, -1)
    width = flat.shape[1] // rep_count
    piece = lax.dynamic_slice_in_dim(flat, rep_index * width, width, axis=1)
    column = lax.all_gather(piece, "shard", axis=0, tiled=True)
    return lax.all_gather(column, "rep", axis=0, tiled=False)


def reduce_full(partial):
    part = lax.psum_scatter(partial, "rep", scatter_dimension=0, tiled=False)
    part = lax.psum_scatter(part, "shard", scatter_dimension=0, tiled=True)
    pieces = lax.all_gather(part, "rep", axis=0, tiled=False)
    rows = pieces.shape[1]
    return jnp.transpose(pieces, (1, 0, 2)).reshape(rows, -1).astype(jnp.float32)


def shards_generic(
    tokens,
    cotangent,
    lengths,
    slot_sequence,
    step_count,
    learn_rate,
    attention_in,
    attention_in_first,
    attention_in_second,
    attention_out,
    attention_out_first,
    attention_out_second,
    gate_up_weight,
    gate_up_first,
    gate_up_second,
    down_weight,
    down_first,
    down_second,
):
    slot_count, position_count, feature_count = tokens.shape
    row_total = slot_count * position_count
    head_count = feature_count // HD
    shaped = (slot_count, position_count, head_count, HD)
    inputs = tokens.astype(jnp.float32).reshape(row_total, feature_count)
    matches = jnp.arange(lengths.shape[0])[None, :] == slot_sequence[:, None]
    slot_length = jnp.sum(jnp.where(matches, lengths[None, :], 0), axis=1)
    alive_rows = (
        (jnp.arange(position_count)[None, :] < slot_length[:, None])
        .astype(jnp.float32)
        .reshape(row_total, 1)
    )
    cosine_table, sine_table = rope_tables(position_count, HD)
    in_local = attention_in.astype(jnp.bfloat16)
    out_local = attention_out.astype(jnp.bfloat16)
    gate_up_local = gate_up_weight.astype(jnp.bfloat16)
    down_local = down_weight.astype(jnp.bfloat16)
    rep_count = lax.axis_size("rep")
    rep_index = lax.axis_index("rep")
    in_full = gather_full(in_local, rep_count, rep_index)
    out_full = gather_full(out_local, rep_count, rep_index)
    gate_up_full = gather_full(gate_up_local, rep_count, rep_index)
    down_full = gather_full(down_local, rep_count, rep_index)
    normed_one, inverse_one = layer_norm(inputs)
    first_input = normed_one.astype(jnp.bfloat16)
    projected = jnp.einsum(
        "rd,qde->rqe", first_input, in_full, preferred_element_type=jnp.float32
    ).reshape(row_total, 3, feature_count)
    queries = rotate(projected[:, 0].reshape(shaped), cosine_table, sine_table).astype(jnp.bfloat16)
    rotated_keys = rotate(projected[:, 1].reshape(shaped), cosine_table, sine_table).astype(
        jnp.bfloat16
    )
    values_low = projected[:, 2].reshape(shaped).astype(jnp.bfloat16)
    mixed_heads, log_total = lax.map(
        attend_forward, (queries, rotated_keys, values_low, slot_length)
    )
    mixed_low = mixed_heads.reshape(row_total, feature_count).astype(jnp.bfloat16)
    residual = inputs + jnp.einsum(
        "rd,qde->rqe", mixed_low, out_full, preferred_element_type=jnp.float32
    ).reshape(row_total, feature_count)
    normed_two, inverse_two = layer_norm(residual)
    second_input = normed_two.astype(jnp.bfloat16)
    gate_up = jnp.einsum(
        "rd,qdf->rqf", second_input, gate_up_full, preferred_element_type=jnp.float32
    ).reshape(row_total, 2, -1)
    gate_value = gate_up[:, 0]
    up_value = gate_up[:, 1]
    sigmoid_gate = jax.nn.sigmoid(gate_value)
    hidden_low = (gate_value * sigmoid_gate * up_value).astype(jnp.bfloat16)
    result = residual + jnp.einsum(
        "rf,qfe->rqe", hidden_low, down_full, preferred_element_type=jnp.float32
    ).reshape(row_total, feature_count)
    output = (result * alive_rows).astype(jnp.bfloat16).reshape(tokens.shape)
    output_grad = cotangent.astype(jnp.float32).reshape(row_total, feature_count) * alive_rows
    result_grad_low = output_grad.astype(jnp.bfloat16)
    hidden_grad = jnp.einsum(
        "rqe,qfe->rf",
        result_grad_low.reshape(row_total, rep_count, -1),
        down_full,
        preferred_element_type=jnp.float32,
    )
    gate_grad = hidden_grad * up_value * sigmoid_gate * (1.0 + gate_value * (1.0 - sigmoid_gate))
    up_grad = hidden_grad * gate_value * sigmoid_gate
    gate_up_grad_low = (
        jnp.concatenate([gate_grad, up_grad], axis=1)
        .astype(jnp.bfloat16)
        .reshape(row_total, rep_count, -1)
    )
    second_input_grad = jnp.einsum(
        "rqf,qdf->rd", gate_up_grad_low, gate_up_full, preferred_element_type=jnp.float32
    )
    residual_grad = output_grad + norm_back(normed_two, inverse_two, second_input_grad)
    down_part = reduce_full(
        jnp.einsum(
            "rc,rqe->qce",
            hidden_low,
            result_grad_low.reshape(row_total, rep_count, -1),
            preferred_element_type=jnp.float32,
        ).astype(jnp.bfloat16)
    )
    gate_up_part = reduce_full(
        jnp.einsum(
            "rc,rqf->qcf", second_input, gate_up_grad_low, preferred_element_type=jnp.float32
        ).astype(jnp.bfloat16)
    ).reshape(gate_up_weight.shape)
    branch_grad = residual_grad.astype(jnp.bfloat16)
    mixed_grad = (
        jnp.einsum(
            "rqe,qde->rd",
            branch_grad.reshape(row_total, rep_count, -1),
            out_full,
            preferred_element_type=jnp.float32,
        )
        .astype(jnp.bfloat16)
        .reshape(shaped)
    )
    query_grad, key_grad, value_grad = lax.map(
        attend_backward, (queries, rotated_keys, values_low, slot_length, log_total, mixed_grad)
    )
    query_back = rotate(query_grad, cosine_table, -sine_table).reshape(row_total, feature_count)
    key_back = rotate(key_grad, cosine_table, -sine_table).reshape(row_total, feature_count)
    projected_grad = (
        jnp.concatenate([query_back, key_back, value_grad.reshape(row_total, feature_count)], axis=1)
        .astype(jnp.bfloat16)
        .reshape(row_total, rep_count, -1)
    )
    first_input_grad = jnp.einsum(
        "rqe,qde->rd", projected_grad, in_full, preferred_element_type=jnp.float32
    )
    input_grad = (residual_grad + norm_back(normed_one, inverse_one, first_input_grad)).reshape(
        tokens.shape
    )
    in_part = reduce_full(
        jnp.einsum(
            "rc,rqe->qce", first_input, projected_grad, preferred_element_type=jnp.float32
        ).astype(jnp.bfloat16)
    ).reshape(attention_in.shape)
    out_part = reduce_full(
        jnp.einsum(
            "rc,rqe->qce",
            mixed_low,
            branch_grad.reshape(row_total, rep_count, -1),
            preferred_element_type=jnp.float32,
        ).astype(jnp.bfloat16)
    )
    in_grad, in_new, in_first, in_second = adam_update(
        attention_in,
        attention_in_first,
        attention_in_second,
        in_part,
        step_count,
        learn_rate,
    )
    out_grad, out_new, out_first, out_second = adam_update(
        attention_out,
        attention_out_first,
        attention_out_second,
        out_part,
        step_count,
        learn_rate,
    )
    gu_grad, gu_new, gu_first, gu_second = adam_update(
        gate_up_weight, gate_up_first, gate_up_second, gate_up_part, step_count, learn_rate
    )
    dn_grad, dn_new, dn_first, dn_second = adam_update(
        down_weight, down_first, down_second, down_part, step_count, learn_rate
    )
    return (
        output,
        input_grad,
        in_grad,
        in_new,
        in_first,
        in_second,
        out_grad,
        out_new,
        out_first,
        out_second,
        gu_grad,
        gu_new,
        gu_first,
        gu_second,
        dn_grad,
        dn_new,
        dn_first,
        dn_second,
    )


def shards_fast(
    tokens,
    cotangent,
    lengths,
    slot_sequence,
    step_count,
    learn_rate,
    attention_in,
    attention_in_first,
    attention_in_second,
    attention_out,
    attention_out_first,
    attention_out_second,
    gate_up_weight,
    gate_up_first,
    gate_up_second,
    down_weight,
    down_first,
    down_second,
):
    _, rows, d = tokens.shape
    x = tokens.reshape(rows, d)
    cosine, sine = half_turns(rows, HD)
    owned, _, ff = gate_up_weight.shape
    tiles = ff // 128

    def tiled(value):
        value = value.reshape(owned, 2, tiles, 128).transpose(0, 2, 1, 3)
        return with_layout_constraint(value, rowwise).reshape(-1, 128)

    def untiled(value):
        value = with_layout_constraint(value.reshape(owned, tiles, 2, 128), rowwise)
        return value.transpose(0, 2, 1, 3).reshape(owned, 2, ff)

    heads = [value.transpose(1, 0, 2) for value in (attention_in, attention_in_first, attention_in_second)]
    gates = [tiled(value) for value in (gate_up_weight, gate_up_first, gate_up_second)]
    results = forward_call(x, cosine, sine, lengths, slot_sequence, heads[0], attention_out, gates[0], down_weight)
    full, saved = results[:4], results[4:]
    total, output, input_grad = backward_call(x, cotangent.reshape(rows, d), cosine, sine, lengths, slot_sequence, saved, full)
    steps_taken = step_count[0].astype(F32)
    scalars = jnp.stack([1.0 / (1.0 - beta_first**steps_taken), 1.0 / (1.0 - beta_second**steps_taken), learn_rate[0]])
    masters = heads + [attention_out, attention_out_first, attention_out_second] + gates + [down_weight, down_first, down_second]
    new = adam_call(scalars, total, masters)
    return (
        output.reshape(tokens.shape),
        input_grad.reshape(tokens.shape),
        *[value.transpose(1, 0, 2) for value in new[:4]],
        *new[4:8],
        *[untiled(value) for value in new[8:12]],
        *new[12:],
    )


def solution(mesh):
    fast = mesh.shape["rep"] == 4 and mesh.shape["shard"] == 8
    return jax.shard_map(
        shards_fast if fast else shards_generic,
        mesh=mesh,
        in_specs=(
            P(("rep", "shard"), None, None),
            P(("rep", "shard"), None, None),
            P(),
            P(("rep", "shard")),
            P(),
            P(),
            P("shard", None, None),
            P("shard", None, None),
            P("shard", None, None),
            P("shard", None),
            P("shard", None),
            P("shard", None),
            P("shard", None, None),
            P("shard", None, None),
            P("shard", None, None),
            P("shard", None),
            P("shard", None),
            P("shard", None),
        ),
        out_specs=(
            P(("rep", "shard"), None, None),
            P(("rep", "shard"), None, None),
            P("shard", None, None),
            P("shard", None, None),
            P("shard", None, None),
            P("shard", None, None),
            P("shard", None),
            P("shard", None),
            P("shard", None),
            P("shard", None),
            P("shard", None, None),
            P("shard", None, None),
            P("shard", None, None),
            P("shard", None, None),
            P("shard", None),
            P("shard", None),
            P("shard", None),
            P("shard", None),
        ),
        check_vma=False,
    )
```

```python
import functools

import jax
import jax.numpy as jnp
import numpy as np
from jax import lax
from jax.experimental import pallas as pl
from jax.experimental.layout import Layout, with_layout_constraint
from jax.experimental.pallas import tpu as pltpu
from jax.sharding import PartitionSpec as P

MESH = pl.DeviceIdType.MESH
DMA = pltpu.SemaphoreType.DMA
RING, RING_ONE, RING_SUMS, RING_TWO = 4, 6, 5, 6
LAG_TWO, LAG_THREE, LAG_FOUR, LAG_FIVE = 1, 3, 5, 7
F32, BF16 = jnp.float32, jnp.bfloat16
rowwise = Layout(major_to_minor=(0, 1, 2, 3))

HD = 64


norm_eps = 1e-05
beta_first = 0.9
beta_second = 0.95
adam_eps = 1e-08
weight_decay = 0.1
rope_base = 10000.0
masked_score = -1e30


def layer_norm(values):
    centered = values - jnp.mean(values, axis=-1, keepdims=True)
    inverse = lax.rsqrt(jnp.mean(centered * centered, axis=-1, keepdims=True) + norm_eps)
    return (centered * inverse, inverse)


def norm_back(normed, inverse, upstream):
    mean_grad = jnp.mean(upstream, axis=-1, keepdims=True)
    mean_dot = jnp.mean(upstream * normed, axis=-1, keepdims=True)
    return inverse * (upstream - mean_grad - normed * mean_dot)


def rope_tables(position_count, head_size):
    half_size = head_size // 2
    frequency = rope_base ** (-(jnp.arange(half_size, dtype=jnp.float32) * 2.0 / head_size))
    angles = jnp.arange(position_count, dtype=jnp.float32)[:, None] * frequency[None, :]
    angles = jnp.concatenate([angles, angles], axis=1)
    return (jnp.cos(angles)[:, None, :], jnp.sin(angles)[:, None, :])


def half_turns(position_count, head_size):
    half_size = head_size // 2
    frequency = np.float32(rope_base) ** (-(np.arange(half_size, dtype=np.float32) * np.float32(2.0) / np.float32(head_size)))
    angles = np.arange(position_count, dtype=np.float32)[:, None] * frequency[None, :]
    cosine, sine = np.cos(angles), np.sin(angles)
    return (
        jnp.asarray(np.concatenate([cosine] * 4, axis=1), jnp.float32),
        jnp.asarray(np.concatenate([-sine, sine] * 2, axis=1), jnp.float32),
    )


def rotate(values, cosine_table, sine_table):
    half_size = values.shape[-1] // 2
    turned = jnp.concatenate([-values[..., half_size:], values[..., :half_size]], axis=-1)
    return values * cosine_table + turned * sine_table


def masked_scores(queries, rotated_keys, length):
    position_count, head_size = (queries.shape[0], queries.shape[-1])
    scores = jnp.einsum(
        "qhd,khd->hqk", queries, rotated_keys, preferred_element_type=jnp.float32
    ) * head_size ** (-0.5)
    position = jnp.arange(position_count)
    allowed = (position[None, :] <= position[:, None]) & (position[None, :] < length)
    return jnp.where(allowed[None], scores, masked_score)


def attend_forward(pieces):
    queries, rotated_keys, values_low, length = pieces
    scores = masked_scores(queries, rotated_keys, length)
    row_max = jnp.max(scores, axis=-1, keepdims=True)
    exponent = jnp.exp(scores - row_max)
    row_sum = jnp.sum(exponent, axis=-1, keepdims=True)
    weights = (exponent / row_sum).astype(jnp.bfloat16)
    mixed_heads = jnp.einsum(
        "hqk,khd->qhd", weights, values_low, preferred_element_type=jnp.float32
    )
    return (mixed_heads, row_max + jnp.log(row_sum))


def attend_backward(pieces):
    queries, rotated_keys, values_low, length, log_total, mixed_grad = pieces
    head_size = queries.shape[-1]
    scores = masked_scores(queries, rotated_keys, length)
    probability = jnp.exp(scores - log_total)
    value_grad = jnp.einsum(
        "hqk,qhd->khd",
        probability.astype(jnp.bfloat16),
        mixed_grad,
        preferred_element_type=jnp.float32,
    )
    probability_grad = jnp.einsum(
        "qhd,khd->hqk", mixed_grad, values_low, preferred_element_type=jnp.float32
    )
    inner_dot = jnp.sum(probability * probability_grad, axis=-1, keepdims=True)
    score_grad = (probability * (probability_grad - inner_dot) * head_size ** (-0.5)).astype(
        jnp.bfloat16
    )
    query_grad = jnp.einsum(
        "hqk,khd->qhd", score_grad, rotated_keys, preferred_element_type=jnp.float32
    )
    key_grad = jnp.einsum("hqk,qhd->khd", score_grad, queries, preferred_element_type=jnp.float32)
    return (query_grad, key_grad, value_grad)


def adam_update(weight, first, second, gradient, step_count, learn_rate):
    steps_taken = step_count[0].astype(jnp.float32)
    first_new = beta_first * first + (1.0 - beta_first) * gradient
    second_new = beta_second * second + (1.0 - beta_second) * gradient * gradient
    first_hat = first_new / (1.0 - beta_first**steps_taken)
    second_hat = second_new / (1.0 - beta_second**steps_taken)
    weight_new = weight - learn_rate[0] * (
        first_hat / (jnp.sqrt(second_hat) + adam_eps) + weight_decay * weight
    )
    return (gradient, weight_new, first_new, second_new)


class Gather:
    @staticmethod
    def scratch(tensors, chunks):
        return [DMA((tensors,)), DMA((chunks, 4)), DMA((chunks, 4)), DMA((chunks, 2, 3)), DMA((chunks, 2, 3))] + [DMA((chunks, 3, 2))] * 4

    def __init__(self, shapes, chunks, loc, full, sems):
        self.shapes, self.chunks, self.loc, self.full = shapes, chunks, loc, full
        (self.own_s, self.sib_s, self.sib_r, self.z_s, self.z_r, self.p_s, self.p_r, self.d_s, self.d_r) = sems
        self.rep, self.shard = lax.axis_index("rep"), lax.axis_index("shard")
        self.z, core = self.shard // 2, lax.rem(self.shard, 2)
        x, y = lax.rem(self.rep, 2), self.rep // 2
        self.sib = (self.rep, self.shard + 1 - 2 * core)
        self.nb = ((self.rep + 1 - 2 * x, self.shard), (self.rep + 2 - 4 * y, self.shard))
        self.diag = self.rep + (1 - 2 * x) + (2 - 4 * y)

    def barrier(self):
        bar = pltpu.get_barrier_semaphore()
        for dev in (self.sib,) + self.nb + tuple((self.rep, self.other(d)) for d in (1, 2, 3)):
            pl.semaphore_signal(bar, inc=1, device_id=dev, device_id_type=MESH)
        pl.semaphore_wait(bar, 6)

    def ref(self, c, s, q=None, half=None):
        t, r0, rows, c0, cols, axis = self.chunks[c]
        base, col, nr, nc = s * self.shapes[t][0] + r0, c0, rows, cols
        if q is not None:
            parts, i = (4, q) if half is None else (8, 2 * q + half)
            if axis == 0:
                nr = rows // parts
                base = base + i * nr
            else:
                nc = cols // parts
                col = pl.multiple_of(c0 + i * nc, 128)
        return self.full[t].at[pl.ds(pl.multiple_of(base, 16), nr), pl.ds(col, nc)]

    def loc_ref(self, c, q=None):
        t, r0, rows, c0, cols, axis = self.chunks[c]
        row, col, nr, nc = r0, c0, rows, cols
        if q is not None and axis == 0:
            nr = rows // 4
            row = pl.multiple_of(r0 + q * nr, 16)
        elif q is not None:
            nc = cols // 4
            col = pl.multiple_of(c0 + q * nc, 128)
        return self.loc[t].at[pl.ds(row, nr), pl.ds(col, nc)]

    def copy(self, src, dst, s, r, dev):
        return pltpu.make_async_remote_copy(src_ref=src, dst_ref=dst, send_sem=s, recv_sem=r, device_id=dev, device_id_type=MESH)

    def own(self, t):
        rows = self.shapes[t][0]
        return pltpu.make_async_copy(self.loc[t], self.full[t].at[pl.ds(pl.multiple_of(self.shard * rows, rows), rows), :], self.own_s.at[t])

    def other(self, dz):
        return lax.rem(self.shard + 2 * dz, 8)

    def sibling(self, c, dz):
        r = self.ref(c, self.other(dz))
        return self.copy(self.loc_ref(c) if dz == 0 else r, r, self.sib_s.at[c, dz], self.sib_r.at[c, dz], self.sib)

    def quarter(self, c):
        return None if self.chunks[c][5] is None else self.rep

    def chain(self, c, side, h):
        sgn = 1 if side == 0 else -1
        s = self.shard - sgn * 2 * (h - 1)
        q = self.quarter(c)
        src = self.loc_ref(c, q) if h == 1 else self.ref(c, s, q)
        return self.copy(src, self.ref(c, s, q), self.z_s.at[c, side, h - 1], self.z_r.at[c, side, h - 1], (self.rep, self.shard + sgn * 2))

    def chain_in(self, c, side, h):
        sgn = 1 if side == 0 else -1
        r = self.ref(c, self.shard - sgn * 2 * h, self.quarter(c))
        return self.copy(r, r, self.z_s.at[c, side, h - 1], self.z_r.at[c, side, h - 1], (self.rep, self.shard - sgn * 2))

    def chain_sends(self, side, h):
        if side == 0:
            return jnp.logical_and(self.z < 3, self.z >= h - 1)
        return jnp.logical_and(self.z > 0, self.z <= 4 - h)

    def plane(self, c, dz, k, theirs=False):
        r = self.ref(c, self.other(dz), self.nb[k][0] if theirs else self.rep)
        return self.copy(r, r, self.p_s.at[c, dz - 1, k], self.p_r.at[c, dz - 1, k], self.nb[k])

    def corner(self, c, dz, k, theirs=False):
        r = self.ref(c, self.other(dz), self.diag if theirs else self.nb[k][0], k)
        return self.copy(r, r, self.d_s.at[c, dz - 1, k], self.d_r.at[c, dz - 1, k], self.nb[1 - k])

    def s0(self, c):
        for side in (0, 1):
            @pl.when(self.chain_sends(side, 1))
            def _():
                self.chain(c, side, 1).start()
        self.sibling(c, 0).start()

    def s1(self, c, h):
        for side in (0, 1):
            @pl.when((self.z >= h) if side == 0 else (self.z <= 3 - h))
            def _():
                self.chain_in(c, side, h).wait_recv()
                if h < 3:
                    @pl.when((self.z < 3) if side == 0 else (self.z > 0))
                    def _():
                        self.chain(c, side, h + 1).start()
                dz = (4 - h) if side == 0 else h
                if self.quarter(c) is None:
                    self.sibling(c, dz).start()
                else:
                    for k in (0, 1):
                        self.plane(c, dz, k).start()

    def s2(self, c):
        for dz in (1, 3, 2):
            for k in (0, 1):
                self.plane(c, dz, k, True).wait_recv()
                self.corner(c, dz, k).start()

    def s3(self, c):
        for dz in (1, 3, 2):
            for k in (0, 1):
                self.corner(c, dz, k, True).wait_recv()
            self.sibling(c, dz).start()

    def s4(self, c):
        for dz in range(4):
            self.sibling(c, dz).wait()

    def drain(self, c):
        for side in (0, 1):
            for h in (1, 2, 3):
                @pl.when(self.chain_sends(side, h))
                def _():
                    self.chain(c, side, h).wait_send()
        for dz in (1, 2, 3) if self.quarter(c) is not None else ():
            for k in (0, 1):
                self.plane(c, dz, k).wait_send()
                self.corner(c, dz, k).wait_send()


def normed(v):
    c = v - jnp.mean(v, axis=-1, keepdims=True)
    inv = lax.rsqrt(jnp.mean(c * c, axis=-1, keepdims=True) + norm_eps)
    return c * inv, inv


def turn(w):
    lane = lax.broadcasted_iota(jnp.int32, w.shape, 1)
    return jnp.where(lax.rem(lane, 64) < 32, pltpu.roll(w, 96, 1), pltpu.roll(w, 32, 1))


def two_heads(w):
    lane = lax.broadcasted_iota(jnp.int32, w.shape, 1)
    zero = jnp.zeros_like(w)
    return jnp.concatenate([jnp.where(lane < 64, w, zero), jnp.where(lane < 64, zero, w)], axis=0)


def join_heads(w):
    n = w.shape[0] // 2
    lane = lax.broadcasted_iota(jnp.int32, (n, w.shape[1]), 1)
    return jnp.where(lane < 64, w[:n], w[n:])


def dot(a, b, da=1, db=0):
    return lax.dot_general(a, b, (((da,), (db,)), ((), ())), preferred_element_type=F32)


def key_bias(ref, length):
    ref[...] = jnp.where(lax.broadcasted_iota(jnp.int32, ref.shape, 1) < length, 0.0, -1e30)


def probabilities(q2, keys, bias):
    n, width = q2.shape[0] // 2, keys.shape[0]
    s = dot(q2, keys, 1, 1) * 0.125 + bias
    row = lax.broadcasted_iota(jnp.int32, (n, 128), 0)
    col = lax.broadcasted_iota(jnp.int32, (n, 128), 1)
    causal = jnp.where(col <= row, 0.0, -1e30)
    last = s[:, width - 128:] + jnp.concatenate([causal, causal], axis=0)
    s = last if width == 128 else jnp.concatenate([s[:, :width - 128], last], axis=1)
    e = jnp.exp(s - jnp.max(s, axis=-1, keepdims=True))
    return e * (1.0 / jnp.sum(e, axis=-1, keepdims=True))


def forward_kernel(
    shapes, chunks,
    x_ref, cos_ref, sin_ref, lengths, slot, win_h, wout_h, wgu_h, wdn_h,
    fin_h, fout_h, fgu_h, fdn_h, at_h, ot_h, bt_h, mt_h, qkv_h, slopes_h, h_h,
    win, wout, wgu, wdn, lin, lout, lgu, ldn, bin_, bout, bgu,
    a, at, qkv, o, ot, h, b, bt, mt, slopes, bias_ref, in_s, load_s, out_s, *sems,
):
    g = Gather(shapes, chunks, (lin, lout, lgu, ldn), (fin_h, fout_h, fgu_h, fdn_h), sems)
    rows = x_ref.shape[0]
    loads = [pltpu.make_async_copy(s, d, in_s.at[i]) for i, (s, d) in enumerate(((win_h, win), (wout_h, wout), (wgu_h, wgu), (wdn_h, wdn)))]
    loads[0].start()
    ffh, half = mt.shape[0] // 2, slopes.shape[1] // 2
    stores = [(at, at_h), (ot, ot_h), (bt, bt_h), (qkv, qkv_h), (h, h_h)]
    stores += [(m.at[pl.ds(i * ffh, ffh), :], n.at[pl.ds(i * ffh, ffh), :]) for m, n in ((mt, mt_h),) for i in (0, 1)]
    stores += [(m.at[:, pl.ds(i * half, half)], n.at[:, pl.ds(i * half, half)]) for m, n in ((slopes, slopes_h),) for i in (0, 1)]
    outs = [pltpu.make_async_copy(s, d, out_s.at[i]) for i, (s, d) in enumerate(stores)]
    AT, OT, BT, QKV, H, MT, SL = 0, 1, 2, 3, 4, 5, 7
    g.barrier()
    key_bias(bias_ref, lengths[slot[0]])

    def weight_in(t, part=0):
        if part == 0:
            loads[t].wait()
        if t == 0:
            for p in (0,) if part == 0 else (1, 2):
                lin[:, 1024 * p:1024 * p + 1024] = win[p].astype(BF16)
        elif t == 1:
            lout[...] = wout[...].astype(BF16)
        elif t == 3:
            ldn[...] = wdn[...].astype(BF16)
        else:
            tiles = lgu.shape[1] // 128
            for c in range(part * tiles // 2, (part + 1) * tiles // 2):
                lgu[:, 128 * c:128 * c + 128] = wgu[pl.ds(c, lgu.shape[0], stride=tiles), :].astype(BF16)
        if t in (1, 3) or part == 1:
            g.own(t).start()

    def ln_one(first, last):
        for r in range(first, last, 128):
            n, _ = normed(x_ref[r:r + 128, :].astype(F32))
            a[r:r + 128, :] = n.astype(BF16)

    def transpose_a():
        for c in range(0, 1024, 128):
            at[c:c + 128, :] = a[:, c:c + 128].T
        outs[AT].start()

    def load(t, c0, n, dst):
        return pltpu.make_async_copy(g.full[t].at[:, pl.ds(c0, n)], dst.at[:, pl.ds(c0, n)], load_s.at[t])

    def project(p, j):
        c = 1024 * p + 256 * j
        w = dot(a[...], bin_[:, c:c + 256])
        for i in (0, 128):
            t = w[:, i:i + 128]
            if p < 2:
                t = t * cos_ref[...] + turn(t) * sin_ref[...]
            qkv[:, c + i:c + i + 128] = t.astype(BF16)

    def attend(pair):
        for qt in range(rows // 128):
            width = 128 * (qt + 1)
            lo = pl.multiple_of(pair * 128, 128)
            q2 = two_heads(qkv[128 * qt:width, pl.ds(lo, 128)])
            p = probabilities(q2, qkv[:width, pl.ds(pl.multiple_of(1024 + lo, 128), 128)], bias_ref[:, :width])
            mixed = join_heads(dot(p.astype(BF16), qkv[:width, pl.ds(pl.multiple_of(2048 + lo, 128), 128)]))
            o[128 * qt:width, pl.ds(lo, 128)] = mixed.astype(BF16)
        ot[pl.ds(lo, 128), :] = o[:, pl.ds(lo, 128)].T

    def out_and_norm():
        for r in range(0, rows, 256):
            v = x_ref[r:r + 256, :].astype(F32) + dot(o[r:r + 256, :], bout[...])
            h[r:r + 256, :] = v
            n, _ = normed(v)
            b[r:r + 256, :] = n.astype(BF16)
        outs[H].start()
        for c in range(0, 1024, 128):
            bt[c:c + 128, :] = b[:, c:c + 128].T
        outs[BT].start()

    def gate(ct):
        lo = pl.multiple_of(ct * 256, 256)
        w = dot(b[...], bgu[:, pl.ds(lo, 256)])
        gv, uv = w[:, :128], w[:, 128:]
        sig = jax.nn.sigmoid(gv)
        silu = gv * sig
        mt[pl.ds(pl.multiple_of(ct * 128, 128), 128), :] = (silu * uv).astype(BF16).T
        slopes[:, pl.ds(lo, 128)] = (uv * sig * (1.0 + gv * (1.0 - sig))).astype(BF16)
        slopes[:, pl.ds(pl.multiple_of(lo + 128, 128), 128)] = silu.astype(BF16)

    Q, KV, O, G1, G2, D1, D2 = range(7)
    tiles = half // 256
    weight_in(0)
    g.s0(Q)
    for cp in loads[1:]:
        cp.start()
    weight_in(0, 1)
    g.s0(KV)
    ln_one(0, rows // 2)
    g.s1(Q, 1)
    ln_one(rows // 2, rows)
    g.s1(Q, 2)
    weight_in(1)
    g.s0(O)
    g.s1(KV, 1)
    g.s1(Q, 3)
    transpose_a()
    g.s2(Q)
    g.s1(KV, 2)
    weight_in(2, 0)
    g.s0(G1)
    g.s1(O, 1)
    g.s1(KV, 3)
    g.s3(Q)
    weight_in(2, 1)
    g.s0(G2)
    g.s1(O, 2)
    g.s2(KV)
    g.s1(O, 3)
    weight_in(3)
    g.s0(D1)
    g.s0(D2)
    g.s1(G1, 1)
    g.s4(Q)
    g.own(0).wait()
    ld = load(0, 0, 1024, bin_)
    ld.start()
    g.s2(O)
    g.s1(G1, 2)
    ld.wait()
    between = {
        (0, 1): lambda: g.s3(KV), (0, 3): lambda: (g.s1(G1, 3), g.s1(G2, 1)),
        (1, 1): lambda: g.s3(O), (1, 3): lambda: g.s1(G2, 2), (2, 1): lambda: (g.s2(G1), g.s1(G2, 3)), (2, 3): lambda: g.s1(D1, 1),
    }
    for p in range(3):
        if p == 1:
            g.s4(KV)
            ld = load(0, 1024, 2048, bin_)
            ld.start()
            ld.wait()
        for j in range(4):
            project(p, j)
            if (p, j) in between:
                between[p, j]()
    outs[QKV].start()
    g.s4(O)
    g.own(1).wait()
    ld = load(1, 0, 1024, bout)
    ld.start()
    steps = [lambda: g.s1(D1, 2), lambda: g.s3(G1), lambda: g.s1(D1, 3), lambda: g.s1(D2, 1), lambda: g.s2(G2), lambda: g.s1(D2, 2)]
    for i in range(8):
        attend(jnp.int32(i))
        if 0 < i < 7:
            steps[i - 1]()
    outs[OT].start()
    ld.wait()
    out_and_norm()
    g.own(2).wait()
    g.s4(G1)
    ld = load(2, 0, half, bgu)
    ld.start()
    g.s2(D1)
    g.s3(G2)
    ld.wait()
    mid = tiles // 2
    lax.fori_loop(0, mid, lambda k, _: (gate(k), 0)[1], 0)
    g.s1(D2, 3)
    g.s3(D1)
    g.s4(G2)
    ld = load(2, half, half, bgu)
    ld.start()
    lax.fori_loop(mid, tiles, lambda k, _: (gate(k), 0)[1], 0)
    outs[MT].start()
    outs[SL].start()
    ld.wait()
    lax.fori_loop(tiles, 2 * tiles, lambda k, _: (gate(k), 0)[1], 0)
    outs[MT + 1].start()
    outs[SL + 1].start()
    g.s4(D1)
    g.s4(D2)
    g.own(3).wait()
    for c in range(len(chunks)):
        g.drain(c)
    for cp in outs:
        cp.wait()


def forward_call(x, cos, sin, lengths, slot, win, wout, wgu, wdn):
    rows, d = x.shape
    r = wout.shape[0]
    ff2 = wgu.shape[0] * 128 // r
    ff = ff2 // 2
    shapes = ((r, 3 * d), (r, d), (r, ff2), wdn.shape)
    part = wdn.shape[0] // 2
    chunks = ((0, 0, r, 0, d, 1), (0, 0, r, d, 2 * d, 1), (1, 0, r, 0, d, 1), (2, 0, r, 0, ff, 0), (2, 0, r, ff, ff, 0), (3, 0, part, 0, d, 1), (3, part, part, 0, d, None))
    vm, an, sm = (pl.BlockSpec(memory_space=m) for m in (pltpu.VMEM, pl.ANY, pltpu.SMEM))
    sd = lambda s, t=BF16: jax.ShapeDtypeStruct(s, t)
    v = lambda s, t=BF16: pltpu.VMEM(s, t)
    outs = [sd((8 * s[0], s[1])) for s in shapes] + [sd((d, rows)), sd((d, rows)), sd((d, rows)), sd((ff, rows)), sd((rows, 3 * d)), sd((rows, ff2)), sd((rows, d), F32)]
    scratch = [v(win.shape, F32), v(wout.shape, F32), v(wgu.shape, F32), v(wdn.shape, F32)] + [v(s) for s in shapes]
    scratch += [v((8 * r, 3 * d)), v((8 * r, d)), v((8 * r, ff2))]
    scratch += [v((rows, d)), v((d, rows)), v((rows, 3 * d)), v((rows, d)), v((d, rows)), v((rows, d), F32), v((rows, d)), v((d, rows)), v((ff, rows)), v((rows, ff2)), v((1, rows), F32)]
    scratch += [DMA((4,)), DMA((4,)), DMA((9,))] + Gather.scratch(4, len(chunks))
    return pl.pallas_call(
        functools.partial(forward_kernel, shapes, chunks),
        out_shape=outs, in_specs=[vm] * 3 + [sm] * 2 + [an] * 4, out_specs=[an] * len(outs), scratch_shapes=scratch,
        compiler_params=pltpu.CompilerParams(collective_id=0, has_side_effects=True, vmem_limit_bytes=60 << 20),
    )(x, cos, sin, lengths, slot, win, wout, wgu, wdn)


class Reduce:
    def __init__(self, refs):
        (self.mine, self.theirs, self.held, self.sums, self.one, self.two, self.fin, self.planes, self.total,
         self.a_s, self.a_r, self.o_s, self.o_r, self.t_s, self.t_r, self.c_s, self.c_r, self.d_s, self.d_r, self.f_s, self.f_r) = refs
        self.rep, self.shard = lax.axis_index("rep"), lax.axis_index("shard")
        self.core = lax.rem(self.shard, 2)
        self.x, self.y = lax.rem(self.rep, 2), self.rep // 2
        self.sib = (self.rep, self.shard + 1 - 2 * self.core)
        self.nb = ((self.rep + 1 - 2 * self.x, self.shard), (self.rep + 2 - 4 * self.y, self.shard))

    @staticmethod
    def scratch(chunks, wide):
        v = lambda *s: pltpu.VMEM(s, BF16)
        return [
            v(RING, 8, 16, wide),
            v(RING, 8, 16, wide),
            pltpu.VMEM((2, 8, 16, wide), F32),
            v(RING_SUMS, 8, 16, wide),
            v(2, RING_ONE, 2, 16, wide),
            v(2, RING_TWO, 16, wide),
            v(RING, 2, 16, wide),
            v(chunks, 3, 2, 16, wide),
        ], [DMA((RING,)), DMA((RING,)), DMA((2, RING_ONE)), DMA((2, RING_ONE)), DMA((2, RING_TWO)), DMA((2, RING_TWO)), DMA((RING,)), DMA((chunks, 3)),
            DMA((chunks, 2)), DMA((chunks, 2)), DMA((chunks, 2)), DMA((chunks, 2))]

    def copy(self, src, dst, s, r, dev):
        return pltpu.make_async_remote_copy(src_ref=src, dst_ref=dst, send_sem=s, recv_sem=r, device_id=dev, device_id_type=MESH)

    def barrier(self):
        bar = pltpu.get_barrier_semaphore()
        for dev in (self.sib,) + self.nb + tuple((self.rep, lax.rem(self.shard + 2 * d, 8)) for d in (1, 2, 3)):
            pl.semaphore_signal(bar, inc=1, device_id=dev, device_id_type=MESH)
        pl.semaphore_wait(bar, 6)

    def first(self, u, w):
        s = lax.rem(u, RING)
        return self.copy(self.mine.at[s, :, :, pl.ds(0, w)], self.theirs.at[s, :, :, pl.ds(0, w)], self.a_s.at[s], self.a_r.at[s], self.sib)

    def hop_one(self, u, w, k):
        m, s = lax.rem(u, RING_SUMS), lax.rem(u, RING_ONE)
        at = 2 - 2 * self.x if k == 0 else 6 - 2 * self.y
        return self.copy(self.sums.at[m, pl.ds(at, 2), :, pl.ds(0, w)], self.one.at[k, s, :, :, pl.ds(0, w)], self.o_s.at[k, s], self.o_r.at[k, s], self.nb[k])

    def hop_two(self, u, w, k):
        m, s = lax.rem(u, RING_SUMS), lax.rem(u, RING_TWO)
        at = 2 * self.x + 1 - self.y if k == 0 else 4 + 2 * self.y + 1 - self.x
        return self.copy(self.sums.at[m, at, :, pl.ds(0, w)], self.two.at[k, s, :, pl.ds(0, w)], self.t_s.at[k, s], self.t_r.at[k, s], self.nb[1 - k])

    def across(self, u, w, dz):
        s = lax.rem(u, RING)
        c = u // 4
        return self.copy(self.fin.at[s, :, :, pl.ds(0, w)], self.planes.at[c, 3 - dz, :, :, pl.ds(0, w)], self.c_s.at[s], self.c_r.at[c, 3 - dz], (self.rep, lax.rem(self.shard + 2 * dz, 8)))

    def plane_in(self, c, w, j):
        return self.copy(self.fin.at[0, :, :, pl.ds(0, w)], self.planes.at[c, j, :, :, pl.ds(0, w)], self.c_s.at[0], self.c_r.at[c, j], self.sib)

    def spread(self, c, w, k, own=True):
        q = self.rep if own else self.nb[k][0]
        ref = self.total.at[c, q, :, :, pl.ds(0, w)]
        return self.copy(ref, ref, self.d_s.at[c, k], self.d_r.at[c, k], self.nb[k])

    def spread_on(self, c, w, k, own=True):
        q = self.nb[k][0] if own else self.nb[0][0] + self.nb[1][0] - self.rep
        ref = self.total.at[c, q, k, :, pl.ds(0, w)]
        return self.copy(ref, ref, self.f_s.at[c, k], self.f_r.at[c, k], self.nb[1 - k])

    def stage_two(self, u, w):
        s, m = lax.rem(u, RING), lax.rem(u, RING_SUMS)
        self.first(u, w).wait()
        self.sums[m, :, :, :w] = (self.held[lax.rem(u, 2), :, :, :w] + self.theirs[s, :, :, :w].astype(F32)).astype(BF16)
        for k in (0, 1):
            self.hop_one(u, w, k).start()

    def stage_three(self, u, w):
        m, s = lax.rem(u, RING_SUMS), lax.rem(u, RING_ONE)
        for k in (0, 1):
            self.hop_one(u, w, k).wait()
            at = 2 * self.x if k == 0 else 4 + 2 * self.y
            new = self.sums[m, pl.ds(at, 2), :, :w].astype(F32) + self.one[k, s, :, :, :w].astype(F32)
            self.sums[m, pl.ds(at, 2), :, :w] = new.astype(BF16)
            self.hop_two(u, w, k).start()

    def stage_four(self, u, w, start):
        s, m, t = lax.rem(u, RING), lax.rem(u, RING_SUMS), lax.rem(u, RING_TWO)
        c = u // 4
        dz = lax.rem(lax.rem(u, 4) + 1, 4)

        @pl.when(jnp.logical_and(u >= start + RING, dz > 0))
        def _():
            self.across(u - RING, w, dz).wait_send()

        for k in (0, 1):
            self.hop_two(u, w, k).wait()

        def plane_sum(k):
            at = 2 * self.x + self.y if k == 0 else 4 + 2 * self.y + self.x
            return self.sums[m, at, :, :w].astype(F32) + self.two[k, t, :, :w].astype(F32)

        @pl.when(dz > 0)
        def _():
            for k in (0, 1):
                self.fin[s, k, :, :w] = plane_sum(k).astype(BF16)
            self.across(u, w, dz).start()

        @pl.when(dz == 0)
        def _():
            for j in range(3):
                self.plane_in(c, w, j).wait_recv()
            for k in (0, 1):
                out = plane_sum(k)
                for j in range(3):
                    out = out + self.planes[c, j, k, :, :w].astype(F32)
                self.total[c, self.rep, k, :, :w] = out.astype(BF16)
            for k in (0, 1):
                self.spread(c, w, k).start()

    def stage_five(self, u, w):
        @pl.when(lax.rem(u, 4) == 3)
        def _():
            c = u // 4
            for k in (0, 1):
                self.spread(c, w, k, False).wait_recv()
                self.spread_on(c, w, k).start()

    def drain_across(self, units, w):
        for u in range(units - RING, units):
            if u % 4 != 3:
                self.across(u, w, u % 4 + 1).wait_send()

    def finish(self, units, width):
        self.drain_across(units, width(units - 1))
        for c in range(units // 4):
            w = width(4 * c)
            for k in (0, 1):
                self.spread(c, w, k).wait_send()
                self.spread_on(c, w, k).wait_send()
                self.spread_on(c, w, k, False).wait_recv()


def norm_back_rows(v, d):
    n, inv = normed(v)
    return inv * (d - jnp.mean(d, axis=-1, keepdims=True) - n * jnp.mean(d * n, axis=-1, keepdims=True))


def backward_kernel(
    wide,
    x_ref, cot_ref, cos_ref, sin_ref, lengths, slot, at_h, ot_h, bt_h, mt_h, qkv_h, slopes_h, h_h, fin_h, fout_h, fgu_h, fdn_h,
    total, out_h, grad_h,
    atl, bt, mt, qkv, dgu, h, wd, wb, wo, atr, do, acc, dh, dk, dv, dy, bias_ref, ld_s, wb_s, st_s, *rs,
):
    r = Reduce(rs[:8] + (total,) + rs[8:])
    rows, d = x_ref.shape
    chunk_plan = ((0, 2, wide), (1, 4, wide), (2, 4, d))
    bounds, u0 = [], 0
    for kind, n, w in chunk_plan:
        bounds.append((u0, u0 + 4 * n, kind, w))
        u0 += 4 * n
    units = u0
    names = ("mt", "wd", "gu", "bt", "qkv", "h", "wo", "ot", "at")
    pairs = ((mt_h, mt), (fdn_h, wd), (slopes_h, dgu), (bt_h, bt), (qkv_h, qkv), (h_h, h), (fout_h, wo),
             (ot_h, atl.at[pl.ds(d, d), :]), (at_h, atl.at[pl.ds(0, d), :]))
    loads = {n: pltpu.make_async_copy(s, t, ld_s.at[i]) for i, (n, (s, t)) in enumerate(zip(names, pairs))}
    for n in names[:3]:
        loads[n].start()

    def weights(j):
        src = fgu_h.at[:, pl.ds(wide * j, wide)] if j < 4 else fin_h.at[:, pl.ds(d * (j - 4), d)]
        dst = wb.at[j % 2] if j < 4 else wb.at[j % 2, :, pl.ds(0, d)]
        return pltpu.make_async_copy(src, dst, wb_s.at[j % 2])

    def width(u):
        for a, b, _, w in bounds:
            if a <= u < b:
                return w

    def start_of(w):
        return min(a for a, _, _, v in bounds if v == w)

    def product(u, kind, first, own):
        c = u // 4 - first // 4
        zt = lax.rem(r.shard // 2 + lax.rem(u, 4) + 1, 4)
        core = r.core if own else 1 - r.core

        def put(e, lo, n, val):
            if own:
                r.held[lax.rem(u, 2), e, :, lo:lo + n] = val
            else:
                r.mine[lax.rem(u, RING), e, :, lo:lo + n] = val.astype(BF16)

        if kind == 0:
            part = mt.shape[0] // 16
            left = mt[pl.ds(pl.multiple_of((2 * zt + core) * 2 * part + c * part, 16), part), :]
            for e in range(0, 8, 2):
                val = dot(left, dy[:, e * 128:e * 128 + 256])
                for i in (0, 1):
                    for j in range(part // 16):
                        put(e + i, 128 * j, 128, val[16 * j:16 * j + 16, i * 128:i * 128 + 128])
            return
        base = (2 * zt + core) * 128
        if kind == 1:
            left = bt[pl.ds(pl.multiple_of(base, 128), 128), :]
            right, n = dgu[:, pl.ds(pl.multiple_of(c * wide, 128), wide)], wide
        else:
            left = atl[pl.ds(pl.multiple_of(base + jnp.where(c == 0, d, 0), 128), 128), :]
            right, n = atr[:, pl.ds(pl.multiple_of(c * d, 128), d)], d
        put(slice(None), 0, n, dot(left, right).reshape(8, 16, n))

    def tail(u, ws):
        if ws[LAG_TWO]:
            r.stage_two(u - LAG_TWO, ws[LAG_TWO])
        if ws[LAG_THREE]:
            r.stage_three(u - LAG_THREE, ws[LAG_THREE])
        if ws[LAG_FOUR]:
            r.stage_four(u - LAG_FOUR, ws[LAG_FOUR], start_of(ws[LAG_FOUR]))
        if ws[LAG_FIVE]:
            r.stage_five(u - LAG_FIVE, ws[LAG_FIVE])

    def widths(u):
        return [width(u - k) if 0 <= u - k < units else None for k in range(LAG_FIVE + 1)]

    def step(u, kind, first, ws):
        product(u, kind, first, False)
        r.first(u, ws[0]).start()
        product(u, kind, first, True)
        tail(u, ws)

    def hidden(t):
        val = dot(dy[...], wd[pl.ds(pl.multiple_of(256 * t, 256), 256), :], 1, 1)
        for i in (0, 1):
            part = val[:, 128 * i:128 * i + 128]
            for j in (0, 1):
                at = pl.ds(pl.multiple_of(512 * t + 256 * i + 128 * j, 128), 128)
                dgu[:, at] = (part * dgu[:, at].astype(F32)).astype(BF16)

    def hidden_unit(u):
        hidden(u)
        tiles = mt.shape[0] // 256

        @pl.when(u + 8 < tiles)
        def _():
            hidden(u + 8)

    def input_two(j):
        weights(j).wait()
        val = dot(dgu[:, wide * j:wide * j + wide], wb[j % 2], 1, 1)
        acc[...] = val if j == 0 else acc[...] + val
        weights(j + 2).start()

    def norm_two(part):
        if part == 0:
            loads["h"].wait()
        for i in range(part * rows // 2, (part + 1) * rows // 2, 128):
            s = slice(i, i + 128)
            v = dy[s, :].astype(F32) + norm_back_rows(h[s, :], acc[s, :])
            dh[s, :] = v
            atr[s, :d] = v.astype(BF16)

    def mixed_grad():
        loads["wo"].wait()
        loads["qkv"].wait()
        do[...] = dot(atr[:, :d], wo[...], 1, 1).astype(BF16)

    def turn_back(t, s):
        return t * cos_ref[s, :] - turn(t) * sin_ref[s, :]

    def attend_tile(lanes, qt):
        n = 128 * (qt + 1)
        s = slice(128 * qt, n)
        keys = qkv[:n, lanes[1]]
        q2, g2 = two_heads(qkv[s, lanes[0]]), two_heads(do[s, lanes[0]])
        p = probabilities(q2, keys, bias_ref[:, :n])
        dp = dot(g2, qkv[:n, lanes[2]], 1, 1)
        ds = (p * (dp - jnp.sum(p * dp, axis=-1, keepdims=True)) * 0.125).astype(BF16)
        new_v, new_k = dot(p.astype(BF16), g2, 0, 0), dot(ds, q2, 0, 0)
        if n == rows:
            dv[...] = new_v
            dk[...] = new_k
        else:
            dv[:n, :] = dv[:n, :] + new_v
            dk[:n, :] = dk[:n, :] + new_k
        atr[s, lanes[1]] = turn_back(join_heads(dot(ds, keys)), s).astype(BF16)

    def attend_half(k):
        lo = pl.multiple_of(k // 2 * 128, 128)
        lanes = [pl.ds(pl.multiple_of(lo + d * i, 128), 128) for i in range(4)]
        tiles = rows // 128

        @pl.when(lax.rem(k, 2) == 0)
        def _():
            for qt in (tiles - 1, 0):
                attend_tile(lanes, qt)

        @pl.when(lax.rem(k, 2) == 1)
        def _():
            for qt in range(1, tiles - 1):
                attend_tile(lanes, qt)
            atr[:, lanes[2]] = turn_back(dk[...], slice(0, rows)).astype(BF16)
            atr[:, lanes[3]] = dv[...].astype(BF16)

    def input_one(j):
        weights(4 + j).wait()
        val = dot(atr[:, d * (j + 1):d * (j + 2)], wb[j % 2, :, :d], 1, 1)
        acc[...] = val if j == 0 else acc[...] + val
        if j == 0:
            weights(6).start()

    grad_out = pltpu.make_async_copy(dh, grad_h, st_s.at[0])
    result_out = pltpu.make_async_copy(do, out_h, st_s.at[1])

    def norm_one():
        for i in range(0, rows, 128):
            s = slice(i, i + 128)
            dh[s, :] = dh[s, :] + norm_back_rows(x_ref[s, :].astype(F32), acc[s, :])
        grad_out.start()

    def result(i):
        s = slice(256 * i, 256 * i + 256)
        do[s, :] = jnp.where(alive(256 * i, 256), h[s, :] + dot(mt[:, s], wd[...], 0, 0), 0.0).astype(BF16)

    before = {0: lambda: loads["mt"].wait(), 8: lambda: loads["bt"].wait(), 24: lambda: loads["ot"].wait(), 28: lambda: loads["at"].wait()}
    fill = {8 + j: functools.partial(input_two, j) for j in range(4)}
    fill[11] = lambda: (input_two(3), norm_two(0))
    fill[12] = lambda: (norm_two(1), mixed_grad())
    fill[27] = lambda: attend_half(jnp.int32(15))
    fill.update({29 + 2 * j: functools.partial(input_one, j) for j in range(3)})
    fill[35] = norm_one
    fill[36] = lambda: result(0)
    fill[37] = lambda: (result(1), result_out.start())
    fill[0] = lambda: [loads[n].start() for n in names[3:]] + [weights(j).start() for j in (0, 1)]
    fill[1] = lambda: (loads["wd"].wait(), loads["gu"].wait(), hidden_unit(jnp.int32(0)))
    fill[7] = lambda: hidden_unit(jnp.int32(7))
    ranged = [(2, 8, lambda u: hidden_unit(u - 1)), (13, 28, lambda u: attend_half(u - 13))]

    length = lengths[slot[0]]

    def alive(first, n):
        return lax.broadcasted_iota(jnp.int32, (n, d), 0) + first < length

    for i in range(0, rows, 128):
        s = slice(i, i + 128)
        dy[s, :] = jnp.where(alive(i, 128), cot_ref[s, :].astype(F32), 0.0).astype(BF16)
    key_bias(bias_ref, length)
    r.barrier()
    edges = sorted({a for a, _, _, _ in bounds} | {e for a, b, _ in ranged for e in (a, b)} | {units} | set(before))
    u = 0
    while u < units:
        if u in before:
            before[u]()
        ws = widths(u)
        first, _, kind, w = next(b for b in bounds if b[0] <= u < b[1])
        in_range = next((f for a, b, f in ranged if a <= u < b), None)
        end = min(e for e in edges if e > u)
        plain = all(x == w for x in ws) and u not in fill
        stop = u
        while plain and stop < end and stop not in fill:
            stop += 1
        if plain and stop - u > 1:
            def body(i, _, kind=kind, first=first, ws=ws, f=in_range):
                step(i, kind, first, ws)
                if f:
                    f(i)
                return 0
            lax.fori_loop(u, stop, body, 0)
            u = stop
            continue
        v = u - LAG_FOUR
        if ws[LAG_FOUR] and v == start_of(ws[LAG_FOUR]) and v > 0:
            r.drain_across(v, width(v - 1))
        step(jnp.int32(u), kind, first, ws)
        if in_range:
            in_range(jnp.int32(u))
        if u in fill:
            fill[u]()
        u += 1
    for u in range(units, units + LAG_FIVE):
        tail(jnp.int32(u), widths(u))
    r.finish(units, width)
    grad_out.wait()
    result_out.wait()


def backward_call(x, cot, cos, sin, lengths, slot, saved, full):
    rows, d = x.shape
    ff = saved[3].shape[0]
    wide = 2 * ff // 4
    chunks = 10
    vm, an, sm = (pl.BlockSpec(memory_space=m) for m in (pltpu.VMEM, pl.ANY, pltpu.SMEM))
    v = lambda s, t=BF16: pltpu.VMEM(s, t)
    bufs, sems = Reduce.scratch(chunks, wide)
    scratch = [v((2 * d, rows)), v((d, rows)), v((ff, rows)), v((rows, 3 * d)), v((rows, 2 * ff)), v((rows, d), F32), v((ff, d)), v((2, d, wide)), v((d, d)),
               v((rows, 4 * d)), v((rows, d)), v((rows, d), F32), v((rows, d), F32), v((rows, 128), F32), v((rows, 128), F32), v((rows, d)), v((1, rows), F32), DMA((9,)), DMA((2,)), DMA((2,))]
    return pl.pallas_call(
        functools.partial(backward_kernel, wide),
        out_shape=[jax.ShapeDtypeStruct((chunks, 4, 2, 16, wide), BF16), jax.ShapeDtypeStruct((rows, d), BF16), jax.ShapeDtypeStruct((rows, d), F32)],
        in_specs=[vm] * 4 + [sm] * 2 + [an] * 11, out_specs=[vm, an, an], scratch_shapes=scratch + bufs + sems,
        compiler_params=pltpu.CompilerParams(collective_id=1, has_side_effects=True, vmem_limit_bytes=63 << 20),
    )(x, cot, cos, sin, lengths, slot, *saved, *full)


def adam_kernel(scalars, total, *refs):
    masters, outs, spread = refs[:12], refs[12:28], refs[28]
    first_scale, second_scale, rate = scalars[0], scalars[1], scalars[2]
    wide = total.shape[-1]
    cols = wide // 128
    d = masters[3].shape[1]

    def update(k, at, grad):
        w, m, v = (masters[3 * k + j][at] for j in range(3))
        m = beta_first * m + (1.0 - beta_first) * grad
        v = beta_second * v + (1.0 - beta_second) * grad * grad
        outs[4 * k][at] = grad
        outs[4 * k + 1][at] = w - rate * (m * first_scale / (jnp.sqrt(v * second_scale) + adam_eps) + weight_decay * w)
        outs[4 * k + 2][at] = m
        outs[4 * k + 3][at] = v

    def piece(c, lo, n):
        return total[c, 0, 0, :, lo:lo + n].astype(F32)

    for p in range(3):
        update(0, (p,), piece(7 + p, 0, d))
    update(1, (slice(None),), piece(6, 0, d))
    stride = 4 * cols
    for c in range(4):
        for j in range(cols):
            spread[pl.ds(c * cols + j, 16, stride=stride), :] = piece(2 + c, 128 * j, 128)
    for i in range(0, 16 * stride, 176):
        s = (slice(i, i + 176),)
        update(2, s, spread[s])
    half = 16 * cols
    for c in (0, 1):
        for j in range(cols):
            update(3, (slice(c * half + 16 * j, c * half + 16 * j + 16),), piece(c, 128 * j, 128))


def adam_call(scalars, total, masters):
    chunks, _, _, _, wide = total.shape
    blocks = []
    for k, shape in enumerate((masters[0].shape, masters[3].shape, masters[6].shape, masters[9].shape)):
        if k == 0:
            blocks.append(pl.BlockSpec((3, shape[1] // 8, shape[2]), lambda i: (0, i, 0)))
        elif k < 3:
            blocks.append(pl.BlockSpec((shape[0] // 8, shape[1]), lambda i: (i, 0)))
        else:
            blocks.append(pl.BlockSpec((shape[0], shape[1] // 8), lambda i: (0, i)))

    def part(i):
        low = lax.rem(i, 2) * 2 + i // 2
        return (0, jnp.where(i < 4, low, i - 4), i // 4, 0, 0)

    shapes = [masters[3 * k].shape for k in range(4) for _ in range(4)]
    return pl.pallas_call(
        adam_kernel,
        grid=(8,),
        out_shape=[jax.ShapeDtypeStruct(s, F32) for s in shapes],
        in_specs=[pl.BlockSpec(memory_space=pltpu.SMEM), pl.BlockSpec((chunks, 1, 1, 16, wide), part)] + [blocks[k] for k in range(4) for _ in range(3)],
        out_specs=[blocks[k] for k in range(4) for _ in range(4)],
        scratch_shapes=[pltpu.VMEM((masters[6].shape[0] // 8, 128), F32)],
        compiler_params=pltpu.CompilerParams(vmem_limit_bytes=60 << 20),
    )(scalars, total, *masters)


def gather_full(local, rep_count, rep_index):
    rows = local.shape[0]
    flat = local.reshape(rows, -1)
    width = flat.shape[1] // rep_count
    piece = lax.dynamic_slice_in_dim(flat, rep_index * width, width, axis=1)
    column = lax.all_gather(piece, "shard", axis=0, tiled=True)
    return lax.all_gather(column, "rep", axis=0, tiled=False)


def reduce_full(partial):
    part = lax.psum_scatter(partial, "rep", scatter_dimension=0, tiled=False)
    part = lax.psum_scatter(part, "shard", scatter_dimension=0, tiled=True)
    pieces = lax.all_gather(part, "rep", axis=0, tiled=False)
    rows = pieces.shape[1]
    return jnp.transpose(pieces, (1, 0, 2)).reshape(rows, -1).astype(jnp.float32)


def shards_generic(
    tokens,
    cotangent,
    lengths,
    slot_sequence,
    step_count,
    learn_rate,
    attention_in,
    attention_in_first,
    attention_in_second,
    attention_out,
    attention_out_first,
    attention_out_second,
    gate_up_weight,
    gate_up_first,
    gate_up_second,
    down_weight,
    down_first,
    down_second,
):
    slot_count, position_count, feature_count = tokens.shape
    row_total = slot_count * position_count
    head_count = feature_count // HD
    shaped = (slot_count, position_count, head_count, HD)
    inputs = tokens.astype(jnp.float32).reshape(row_total, feature_count)
    matches = jnp.arange(lengths.shape[0])[None, :] == slot_sequence[:, None]
    slot_length = jnp.sum(jnp.where(matches, lengths[None, :], 0), axis=1)
    alive_rows = (
        (jnp.arange(position_count)[None, :] < slot_length[:, None])
        .astype(jnp.float32)
        .reshape(row_total, 1)
    )
    cosine_table, sine_table = rope_tables(position_count, HD)
    in_local = attention_in.astype(jnp.bfloat16)
    out_local = attention_out.astype(jnp.bfloat16)
    gate_up_local = gate_up_weight.astype(jnp.bfloat16)
    down_local = down_weight.astype(jnp.bfloat16)
    rep_count = lax.axis_size("rep")
    rep_index = lax.axis_index("rep")
    in_full = gather_full(in_local, rep_count, rep_index)
    out_full = gather_full(out_local, rep_count, rep_index)
    gate_up_full = gather_full(gate_up_local, rep_count, rep_index)
    down_full = gather_full(down_local, rep_count, rep_index)
    normed_one, inverse_one = layer_norm(inputs)
    first_input = normed_one.astype(jnp.bfloat16)
    projected = jnp.einsum(
        "rd,qde->rqe", first_input, in_full, preferred_element_type=jnp.float32
    ).reshape(row_total, 3, feature_count)
    queries = rotate(projected[:, 0].reshape(shaped), cosine_table, sine_table).astype(jnp.bfloat16)
    rotated_keys = rotate(projected[:, 1].reshape(shaped), cosine_table, sine_table).astype(
        jnp.bfloat16
    )
    values_low = projected[:, 2].reshape(shaped).astype(jnp.bfloat16)
    mixed_heads, log_total = lax.map(
        attend_forward, (queries, rotated_keys, values_low, slot_length)
    )
    mixed_low = mixed_heads.reshape(row_total, feature_count).astype(jnp.bfloat16)
    residual = inputs + jnp.einsum(
        "rd,qde->rqe", mixed_low, out_full, preferred_element_type=jnp.float32
    ).reshape(row_total, feature_count)
    normed_two, inverse_two = layer_norm(residual)
    second_input = normed_two.astype(jnp.bfloat16)
    gate_up = jnp.einsum(
        "rd,qdf->rqf", second_input, gate_up_full, preferred_element_type=jnp.float32
    ).reshape(row_total, 2, -1)
    gate_value = gate_up[:, 0]
    up_value = gate_up[:, 1]
    sigmoid_gate = jax.nn.sigmoid(gate_value)
    hidden_low = (gate_value * sigmoid_gate * up_value).astype(jnp.bfloat16)
    result = residual + jnp.einsum(
        "rf,qfe->rqe", hidden_low, down_full, preferred_element_type=jnp.float32
    ).reshape(row_total, feature_count)
    output = (result * alive_rows).astype(jnp.bfloat16).reshape(tokens.shape)
    output_grad = cotangent.astype(jnp.float32).reshape(row_total, feature_count) * alive_rows
    result_grad_low = output_grad.astype(jnp.bfloat16)
    hidden_grad = jnp.einsum(
        "rqe,qfe->rf",
        result_grad_low.reshape(row_total, rep_count, -1),
        down_full,
        preferred_element_type=jnp.float32,
    )
    gate_grad = hidden_grad * up_value * sigmoid_gate * (1.0 + gate_value * (1.0 - sigmoid_gate))
    up_grad = hidden_grad * gate_value * sigmoid_gate
    gate_up_grad_low = (
        jnp.concatenate([gate_grad, up_grad], axis=1)
        .astype(jnp.bfloat16)
        .reshape(row_total, rep_count, -1)
    )
    second_input_grad = jnp.einsum(
        "rqf,qdf->rd", gate_up_grad_low, gate_up_full, preferred_element_type=jnp.float32
    )
    residual_grad = output_grad + norm_back(normed_two, inverse_two, second_input_grad)
    down_part = reduce_full(
        jnp.einsum(
            "rc,rqe->qce",
            hidden_low,
            result_grad_low.reshape(row_total, rep_count, -1),
            preferred_element_type=jnp.float32,
        ).astype(jnp.bfloat16)
    )
    gate_up_part = reduce_full(
        jnp.einsum(
            "rc,rqf->qcf", second_input, gate_up_grad_low, preferred_element_type=jnp.float32
        ).astype(jnp.bfloat16)
    ).reshape(gate_up_weight.shape)
    branch_grad = residual_grad.astype(jnp.bfloat16)
    mixed_grad = (
        jnp.einsum(
            "rqe,qde->rd",
            branch_grad.reshape(row_total, rep_count, -1),
            out_full,
            preferred_element_type=jnp.float32,
        )
        .astype(jnp.bfloat16)
        .reshape(shaped)
    )
    query_grad, key_grad, value_grad = lax.map(
        attend_backward, (queries, rotated_keys, values_low, slot_length, log_total, mixed_grad)
    )
    query_back = rotate(query_grad, cosine_table, -sine_table).reshape(row_total, feature_count)
    key_back = rotate(key_grad, cosine_table, -sine_table).reshape(row_total, feature_count)
    projected_grad = (
        jnp.concatenate([query_back, key_back, value_grad.reshape(row_total, feature_count)], axis=1)
        .astype(jnp.bfloat16)
        .reshape(row_total, rep_count, -1)
    )
    first_input_grad = jnp.einsum(
        "rqe,qde->rd", projected_grad, in_full, preferred_element_type=jnp.float32
    )
    input_grad = (residual_grad + norm_back(normed_one, inverse_one, first_input_grad)).reshape(
        tokens.shape
    )
    in_part = reduce_full(
        jnp.einsum(
            "rc,rqe->qce", first_input, projected_grad, preferred_element_type=jnp.float32
        ).astype(jnp.bfloat16)
    ).reshape(attention_in.shape)
    out_part = reduce_full(
        jnp.einsum(
            "rc,rqe->qce",
            mixed_low,
            branch_grad.reshape(row_total, rep_count, -1),
            preferred_element_type=jnp.float32,
        ).astype(jnp.bfloat16)
    )
    in_grad, in_new, in_first, in_second = adam_update(
        attention_in,
        attention_in_first,
        attention_in_second,
        in_part,
        step_count,
        learn_rate,
    )
    out_grad, out_new, out_first, out_second = adam_update(
        attention_out,
        attention_out_first,
        attention_out_second,
        out_part,
        step_count,
        learn_rate,
    )
    gu_grad, gu_new, gu_first, gu_second = adam_update(
        gate_up_weight, gate_up_first, gate_up_second, gate_up_part, step_count, learn_rate
    )
    dn_grad, dn_new, dn_first, dn_second = adam_update(
        down_weight, down_first, down_second, down_part, step_count, learn_rate
    )
    return (
        output,
        input_grad,
        in_grad,
        in_new,
        in_first,
        in_second,
        out_grad,
        out_new,
        out_first,
        out_second,
        gu_grad,
        gu_new,
        gu_first,
        gu_second,
        dn_grad,
        dn_new,
        dn_first,
        dn_second,
    )


def shards_fast(
    tokens,
    cotangent,
    lengths,
    slot_sequence,
    step_count,
    learn_rate,
    attention_in,
    attention_in_first,
    attention_in_second,
    attention_out,
    attention_out_first,
    attention_out_second,
    gate_up_weight,
    gate_up_first,
    gate_up_second,
    down_weight,
    down_first,
    down_second,
):
    _, rows, d = tokens.shape
    x = tokens.reshape(rows, d)
    cosine, sine = half_turns(rows, HD)
    owned, _, ff = gate_up_weight.shape
    tiles = ff // 128

    def tiled(value):
        value = value.reshape(owned, 2, tiles, 128).transpose(0, 2, 1, 3)
        return with_layout_constraint(value, rowwise).reshape(-1, 128)

    def untiled(value):
        value = with_layout_constraint(value.reshape(owned, tiles, 2, 128), rowwise)
        return value.transpose(0, 2, 1, 3).reshape(owned, 2, ff)

    heads = [value.transpose(1, 0, 2) for value in (attention_in, attention_in_first, attention_in_second)]
    gates = [tiled(value) for value in (gate_up_weight, gate_up_first, gate_up_second)]
    results = forward_call(x, cosine, sine, lengths, slot_sequence, heads[0], attention_out, gates[0], down_weight)
    full, saved = results[:4], results[4:]
    total, output, input_grad = backward_call(x, cotangent.reshape(rows, d), cosine, sine, lengths, slot_sequence, saved, full)
    steps_taken = step_count[0].astype(F32)
    scalars = jnp.stack([1.0 / (1.0 - beta_first**steps_taken), 1.0 / (1.0 - beta_second**steps_taken), learn_rate[0]])
    masters = heads + [attention_out, attention_out_first, attention_out_second] + gates + [down_weight, down_first, down_second]
    new = adam_call(scalars, total, masters)
    return (
        output.reshape(tokens.shape),
        input_grad.reshape(tokens.shape),
        *[value.transpose(1, 0, 2) for value in new[:4]],
        *new[4:8],
        *[untiled(value) for value in new[8:12]],
        *new[12:],
    )


def solution(mesh):
    fast = mesh.shape["rep"] == 4 and mesh.shape["shard"] == 8
    return jax.shard_map(
        shards_fast if fast else shards_generic,
        mesh=mesh,
        in_specs=(
            P(("rep", "shard"), None, None),
            P(("rep", "shard"), None, None),
            P(),
            P(("rep", "shard")),
            P(),
            P(),
            P("shard", None, None),
            P("shard", None, None),
            P("shard", None, None),
            P("shard", None),
            P("shard", None),
            P("shard", None),
            P("shard", None, None),
            P("shard", None, None),
            P("shard", None, None),
            P("shard", None),
            P("shard", None),
            P("shard", None),
        ),
        out_specs=(
            P(("rep", "shard"), None, None),
            P(("rep", "shard"), None, None),
            P("shard", None, None),
            P("shard", None, None),
            P("shard", None, None),
            P("shard", None, None),
            P("shard", None),
            P("shard", None),
            P("shard", None),
            P("shard", None),
            P("shard", None, None),
            P("shard", None, None),
            P("shard", None, None),
            P("shard", None, None),
            P("shard", None),
            P("shard", None),
            P("shard", None),
            P("shard", None),
        ),
        check_vma=False,
    )
```

```python
import functools

import jax
import jax.numpy as jnp
import numpy as np
from jax import lax
from jax.experimental import pallas as pl
from jax.experimental.layout import Layout, with_layout_constraint
from jax.experimental.pallas import tpu as pltpu
from jax.sharding import PartitionSpec as P

MESH = pl.DeviceIdType.MESH
DMA = pltpu.SemaphoreType.DMA
RING, RING_ONE, RING_SUMS, RING_TWO = 4, 6, 5, 6
LAG_TWO, LAG_THREE, LAG_FOUR, LAG_SUM, LAG_ON = 1, 3, 5, 8, 10
FAR = 256
F32, BF16 = jnp.float32, jnp.bfloat16
rowwise = Layout(major_to_minor=(0, 1, 2, 3))

HD = 64


norm_eps = 1e-05
beta_first = 0.9
beta_second = 0.95
adam_eps = 1e-08
weight_decay = 0.1
rope_base = 10000.0
masked_score = -1e30


def layer_norm(values):
    centered = values - jnp.mean(values, axis=-1, keepdims=True)
    inverse = lax.rsqrt(jnp.mean(centered * centered, axis=-1, keepdims=True) + norm_eps)
    return (centered * inverse, inverse)


def norm_back(normed, inverse, upstream):
    mean_grad = jnp.mean(upstream, axis=-1, keepdims=True)
    mean_dot = jnp.mean(upstream * normed, axis=-1, keepdims=True)
    return inverse * (upstream - mean_grad - normed * mean_dot)


def rope_tables(position_count, head_size):
    half_size = head_size // 2
    frequency = rope_base ** (-(jnp.arange(half_size, dtype=jnp.float32) * 2.0 / head_size))
    angles = jnp.arange(position_count, dtype=jnp.float32)[:, None] * frequency[None, :]
    angles = jnp.concatenate([angles, angles], axis=1)
    return (jnp.cos(angles)[:, None, :], jnp.sin(angles)[:, None, :])


def half_turns(position_count, head_size):
    half_size = head_size // 2
    frequency = np.float32(rope_base) ** (-(np.arange(half_size, dtype=np.float32) * np.float32(2.0) / np.float32(head_size)))
    angles = np.arange(position_count, dtype=np.float32)[:, None] * frequency[None, :]
    cosine, sine = np.cos(angles), np.sin(angles)
    return (
        jnp.asarray(np.concatenate([cosine] * 4, axis=1), jnp.float32),
        jnp.asarray(np.concatenate([-sine, sine] * 2, axis=1), jnp.float32),
    )


def rotate(values, cosine_table, sine_table):
    half_size = values.shape[-1] // 2
    turned = jnp.concatenate([-values[..., half_size:], values[..., :half_size]], axis=-1)
    return values * cosine_table + turned * sine_table


def masked_scores(queries, rotated_keys, length):
    position_count, head_size = (queries.shape[0], queries.shape[-1])
    scores = jnp.einsum(
        "qhd,khd->hqk", queries, rotated_keys, preferred_element_type=jnp.float32
    ) * head_size ** (-0.5)
    position = jnp.arange(position_count)
    allowed = (position[None, :] <= position[:, None]) & (position[None, :] < length)
    return jnp.where(allowed[None], scores, masked_score)


def attend_forward(pieces):
    queries, rotated_keys, values_low, length = pieces
    scores = masked_scores(queries, rotated_keys, length)
    row_max = jnp.max(scores, axis=-1, keepdims=True)
    exponent = jnp.exp(scores - row_max)
    row_sum = jnp.sum(exponent, axis=-1, keepdims=True)
    weights = (exponent / row_sum).astype(jnp.bfloat16)
    mixed_heads = jnp.einsum(
        "hqk,khd->qhd", weights, values_low, preferred_element_type=jnp.float32
    )
    return (mixed_heads, row_max + jnp.log(row_sum))


def attend_backward(pieces):
    queries, rotated_keys, values_low, length, log_total, mixed_grad = pieces
    head_size = queries.shape[-1]
    scores = masked_scores(queries, rotated_keys, length)
    probability = jnp.exp(scores - log_total)
    value_grad = jnp.einsum(
        "hqk,qhd->khd",
        probability.astype(jnp.bfloat16),
        mixed_grad,
        preferred_element_type=jnp.float32,
    )
    probability_grad = jnp.einsum(
        "qhd,khd->hqk", mixed_grad, values_low, preferred_element_type=jnp.float32
    )
    inner_dot = jnp.sum(probability * probability_grad, axis=-1, keepdims=True)
    score_grad = (probability * (probability_grad - inner_dot) * head_size ** (-0.5)).astype(
        jnp.bfloat16
    )
    query_grad = jnp.einsum(
        "hqk,khd->qhd", score_grad, rotated_keys, preferred_element_type=jnp.float32
    )
    key_grad = jnp.einsum("hqk,qhd->khd", score_grad, queries, preferred_element_type=jnp.float32)
    return (query_grad, key_grad, value_grad)


def adam_update(weight, first, second, gradient, step_count, learn_rate):
    steps_taken = step_count[0].astype(jnp.float32)
    first_new = beta_first * first + (1.0 - beta_first) * gradient
    second_new = beta_second * second + (1.0 - beta_second) * gradient * gradient
    first_hat = first_new / (1.0 - beta_first**steps_taken)
    second_hat = second_new / (1.0 - beta_second**steps_taken)
    weight_new = weight - learn_rate[0] * (
        first_hat / (jnp.sqrt(second_hat) + adam_eps) + weight_decay * weight
    )
    return (gradient, weight_new, first_new, second_new)


class Gather:
    @staticmethod
    def scratch(tensors, chunks):
        return [DMA((tensors,)), DMA((chunks, 4)), DMA((chunks, 4)), DMA((chunks, 2, 3)), DMA((chunks, 2, 3))] + [DMA((chunks, 3, 2))] * 4

    def __init__(self, shapes, chunks, loc, full, sems):
        self.shapes, self.chunks, self.loc, self.full = shapes, chunks, loc, full
        (self.own_s, self.sib_s, self.sib_r, self.z_s, self.z_r, self.p_s, self.p_r, self.d_s, self.d_r) = sems
        self.rep, self.shard = lax.axis_index("rep"), lax.axis_index("shard")
        self.z, core = self.shard // 2, lax.rem(self.shard, 2)
        x, y = lax.rem(self.rep, 2), self.rep // 2
        self.sib = (self.rep, self.shard + 1 - 2 * core)
        self.nb = ((self.rep + 1 - 2 * x, self.shard), (self.rep + 2 - 4 * y, self.shard))
        self.diag = self.rep + (1 - 2 * x) + (2 - 4 * y)

    def barrier(self):
        bar = pltpu.get_barrier_semaphore()
        for dev in (self.sib,) + self.nb + tuple((self.rep, self.other(d)) for d in (1, 2, 3)):
            pl.semaphore_signal(bar, inc=1, device_id=dev, device_id_type=MESH)
        pl.semaphore_wait(bar, 6)

    def ref(self, c, s, q=None, half=None):
        t, r0, rows, c0, cols, axis = self.chunks[c]
        base, col, nr, nc = s * self.shapes[t][0] + r0, c0, rows, cols
        if q is not None:
            parts, i = (4, q) if half is None else (8, 2 * q + half)
            if axis == 0:
                nr = rows // parts
                base = base + i * nr
            else:
                nc = cols // parts
                col = pl.multiple_of(c0 + i * nc, 128)
        return self.full[t].at[pl.ds(pl.multiple_of(base, 16), nr), pl.ds(col, nc)]

    def loc_ref(self, c, q=None):
        t, r0, rows, c0, cols, axis = self.chunks[c]
        row, col, nr, nc = r0, c0, rows, cols
        if q is not None and axis == 0:
            nr = rows // 4
            row = pl.multiple_of(r0 + q * nr, 16)
        elif q is not None:
            nc = cols // 4
            col = pl.multiple_of(c0 + q * nc, 128)
        return self.loc[t].at[pl.ds(row, nr), pl.ds(col, nc)]

    def copy(self, src, dst, s, r, dev):
        return pltpu.make_async_remote_copy(src_ref=src, dst_ref=dst, send_sem=s, recv_sem=r, device_id=dev, device_id_type=MESH)

    def own(self, t):
        rows = self.shapes[t][0]
        return pltpu.make_async_copy(self.loc[t], self.full[t].at[pl.ds(pl.multiple_of(self.shard * rows, rows), rows), :], self.own_s.at[t])

    def other(self, dz):
        return lax.rem(self.shard + 2 * dz, 8)

    def sibling(self, c, dz):
        r = self.ref(c, self.other(dz))
        return self.copy(self.loc_ref(c) if dz == 0 else r, r, self.sib_s.at[c, dz], self.sib_r.at[c, dz], self.sib)

    def quarter(self, c):
        return None if self.chunks[c][5] is None else self.rep

    def chain(self, c, side, h):
        sgn = 1 if side == 0 else -1
        s = self.shard - sgn * 2 * (h - 1)
        q = self.quarter(c)
        src = self.loc_ref(c, q) if h == 1 else self.ref(c, s, q)
        return self.copy(src, self.ref(c, s, q), self.z_s.at[c, side, h - 1], self.z_r.at[c, side, h - 1], (self.rep, self.shard + sgn * 2))

    def chain_in(self, c, side, h):
        sgn = 1 if side == 0 else -1
        r = self.ref(c, self.shard - sgn * 2 * h, self.quarter(c))
        return self.copy(r, r, self.z_s.at[c, side, h - 1], self.z_r.at[c, side, h - 1], (self.rep, self.shard - sgn * 2))

    def chain_sends(self, side, h):
        if side == 0:
            return jnp.logical_and(self.z < 3, self.z >= h - 1)
        return jnp.logical_and(self.z > 0, self.z <= 4 - h)

    def plane(self, c, dz, k, theirs=False):
        r = self.ref(c, self.other(dz), self.nb[k][0] if theirs else self.rep)
        return self.copy(r, r, self.p_s.at[c, dz - 1, k], self.p_r.at[c, dz - 1, k], self.nb[k])

    def corner(self, c, dz, k, theirs=False):
        r = self.ref(c, self.other(dz), self.diag if theirs else self.nb[k][0], k)
        return self.copy(r, r, self.d_s.at[c, dz - 1, k], self.d_r.at[c, dz - 1, k], self.nb[1 - k])

    def s0(self, c):
        for side in (0, 1):
            @pl.when(self.chain_sends(side, 1))
            def _():
                self.chain(c, side, 1).start()
        self.sibling(c, 0).start()

    def s1(self, c, h):
        for side in (0, 1):
            @pl.when((self.z >= h) if side == 0 else (self.z <= 3 - h))
            def _():
                self.chain_in(c, side, h).wait_recv()
                if h < 3:
                    @pl.when((self.z < 3) if side == 0 else (self.z > 0))
                    def _():
                        self.chain(c, side, h + 1).start()
                dz = (4 - h) if side == 0 else h
                if self.quarter(c) is None:
                    self.sibling(c, dz).start()
                else:
                    for k in (0, 1):
                        self.plane(c, dz, k).start()

    def s2(self, c):
        for dz in (1, 3, 2):
            for k in (0, 1):
                self.plane(c, dz, k, True).wait_recv()
                self.corner(c, dz, k).start()

    def s3(self, c):
        for dz in (1, 3, 2):
            for k in (0, 1):
                self.corner(c, dz, k, True).wait_recv()
            self.sibling(c, dz).start()

    def s4(self, c):
        for dz in range(4):
            self.sibling(c, dz).wait()

    def drain(self, c):
        for side in (0, 1):
            for h in (1, 2, 3):
                @pl.when(self.chain_sends(side, h))
                def _():
                    self.chain(c, side, h).wait_send()
        for dz in (1, 2, 3) if self.quarter(c) is not None else ():
            for k in (0, 1):
                self.plane(c, dz, k).wait_send()
                self.corner(c, dz, k).wait_send()


def normed(v):
    c = v - jnp.mean(v, axis=-1, keepdims=True)
    inv = lax.rsqrt(jnp.mean(c * c, axis=-1, keepdims=True) + norm_eps)
    return c * inv, inv


def turn(w):
    lane = lax.broadcasted_iota(jnp.int32, w.shape, 1)
    return jnp.where(lax.rem(lane, 64) < 32, pltpu.roll(w, 96, 1), pltpu.roll(w, 32, 1))


def two_heads(w):
    lane = lax.broadcasted_iota(jnp.int32, w.shape, 1)
    zero = jnp.zeros_like(w)
    return jnp.concatenate([jnp.where(lane < 64, w, zero), jnp.where(lane < 64, zero, w)], axis=0)


def join_heads(w):
    n = w.shape[0] // 2
    lane = lax.broadcasted_iota(jnp.int32, (n, w.shape[1]), 1)
    return jnp.where(lane < 64, w[:n], w[n:])


def dot(a, b, da=1, db=0):
    return lax.dot_general(a, b, (((da,), (db,)), ((), ())), preferred_element_type=F32)


def key_bias(ref, length):
    ref[...] = jnp.where(lax.broadcasted_iota(jnp.int32, ref.shape, 1) < length, 0.0, -1e30)


def probabilities(q2, keys, bias):
    n, width = q2.shape[0] // 2, keys.shape[0]
    s = dot(q2, keys, 1, 1) * 0.125 + bias
    row = lax.broadcasted_iota(jnp.int32, (n, 128), 0)
    col = lax.broadcasted_iota(jnp.int32, (n, 128), 1)
    causal = jnp.where(col <= row, 0.0, -1e30)
    last = s[:, width - 128:] + jnp.concatenate([causal, causal], axis=0)
    s = last if width == 128 else jnp.concatenate([s[:, :width - 128], last], axis=1)
    e = jnp.exp(s - jnp.max(s, axis=-1, keepdims=True))
    return e * (1.0 / jnp.sum(e, axis=-1, keepdims=True))


def forward_kernel(
    shapes, chunks,
    x_ref, cos_ref, sin_ref, lengths, slot, win_h, wout_h, wgu_h, wdn_h,
    fin_h, fout_h, fgu_h, fdn_h, at_h, ot_h, bt_h, mt_h, qkv_h, slopes_h, h_h,
    win, wout, wgu, wdn, lin, lout, lgu, ldn, bin_, bout, bgu,
    a, at, qkv, o, ot, h, b, bt, mt, slopes, bias_ref, in_s, out_s, *sems,
):
    g = Gather(shapes, chunks, (lin, lout, lgu, ldn), (bin_, bout, bgu, fdn_h), sems)
    rows = x_ref.shape[0]
    loads = [pltpu.make_async_copy(s, d, in_s.at[i]) for i, (s, d) in enumerate(((win_h, win), (wout_h, wout), (wgu_h, wgu), (wdn_h, wdn)))]
    loads[0].start()
    ffh, half = mt.shape[0] // 2, slopes.shape[1] // 2
    stores = [(at, at_h), (ot, ot_h), (bt, bt_h), (qkv, qkv_h), (h, h_h)]
    stores += [(m.at[pl.ds(i * ffh, ffh), :], n.at[pl.ds(i * ffh, ffh), :]) for m, n in ((mt, mt_h),) for i in (0, 1)]
    stores += [(m.at[:, pl.ds(i * half, half)], n.at[:, pl.ds(i * half, half)]) for m, n in ((slopes, slopes_h),) for i in (0, 1)]
    stores += [(bin_, fin_h), (bout, fout_h)] + [(bgu.at[:, pl.ds(i * half, half)], fgu_h.at[:, pl.ds(i * half, half)]) for i in (0, 1)]
    outs = [pltpu.make_async_copy(s, d, out_s.at[i]) for i, (s, d) in enumerate(stores)]
    AT, OT, BT, QKV, H, MT, SL, WIN, WOUT, WGU = 0, 1, 2, 3, 4, 5, 7, 9, 10, 11
    g.barrier()
    key_bias(bias_ref, lengths[slot[0]])

    def weight_in(t, part=0):
        if part == 0:
            loads[t].wait()
        if t == 0:
            for p in (0,) if part == 0 else (1, 2):
                lin[:, 1024 * p:1024 * p + 1024] = win[p].astype(BF16)
        elif t == 1:
            lout[...] = wout[...].astype(BF16)
        elif t == 3:
            ldn[...] = wdn[...].astype(BF16)
        else:
            tiles = lgu.shape[1] // 128
            for c in range(part * tiles // 2, (part + 1) * tiles // 2):
                lgu[:, 128 * c:128 * c + 128] = wgu[pl.ds(c, lgu.shape[0], stride=tiles), :].astype(BF16)
        if t in (1, 3) or part == 1:
            g.own(t).start()

    def ln_one(first, last):
        for r in range(first, last, 128):
            n, _ = normed(x_ref[r:r + 128, :].astype(F32))
            a[r:r + 128, :] = n.astype(BF16)

    def transpose_a():
        for c in range(0, 1024, 128):
            at[c:c + 128, :] = a[:, c:c + 128].T
        outs[AT].start()

    def project(p, j):
        c = 1024 * p + 256 * j
        w = dot(a[...], bin_[:, c:c + 256])
        for i in (0, 128):
            t = w[:, i:i + 128]
            if p < 2:
                t = t * cos_ref[...] + turn(t) * sin_ref[...]
            qkv[:, c + i:c + i + 128] = t.astype(BF16)

    def attend(pair):
        for qt in range(rows // 128):
            width = 128 * (qt + 1)
            lo = pl.multiple_of(pair * 128, 128)
            q2 = two_heads(qkv[128 * qt:width, pl.ds(lo, 128)])
            p = probabilities(q2, qkv[:width, pl.ds(pl.multiple_of(1024 + lo, 128), 128)], bias_ref[:, :width])
            mixed = join_heads(dot(p.astype(BF16), qkv[:width, pl.ds(pl.multiple_of(2048 + lo, 128), 128)]))
            o[128 * qt:width, pl.ds(lo, 128)] = mixed.astype(BF16)
        ot[pl.ds(lo, 128), :] = o[:, pl.ds(lo, 128)].T

    def out_and_norm():
        for r in range(0, rows, 256):
            v = x_ref[r:r + 256, :].astype(F32) + dot(o[r:r + 256, :], bout[...])
            h[r:r + 256, :] = v
            n, _ = normed(v)
            b[r:r + 256, :] = n.astype(BF16)
        outs[H].start()
        for c in range(0, 1024, 128):
            bt[c:c + 128, :] = b[:, c:c + 128].T
        outs[BT].start()

    def gate(ct):
        lo = pl.multiple_of(ct * 256, 256)
        w = dot(b[...], bgu[:, pl.ds(lo, 256)])
        gv, uv = w[:, :128], w[:, 128:]
        sig = jax.nn.sigmoid(gv)
        silu = gv * sig
        mt[pl.ds(pl.multiple_of(ct * 128, 128), 128), :] = (silu * uv).astype(BF16).T
        slopes[:, pl.ds(lo, 128)] = (uv * sig * (1.0 + gv * (1.0 - sig))).astype(BF16)
        slopes[:, pl.ds(pl.multiple_of(lo + 128, 128), 128)] = silu.astype(BF16)

    Q, KV, O, G1, G2, D1, D2 = range(7)
    tiles = half // 256
    weight_in(0)
    g.s0(Q)
    for cp in loads[1:]:
        cp.start()
    weight_in(0, 1)
    g.s0(KV)
    ln_one(0, rows // 2)
    g.s1(Q, 1)
    ln_one(rows // 2, rows)
    g.s1(Q, 2)
    weight_in(1)
    g.s0(O)
    g.s1(KV, 1)
    g.s1(Q, 3)
    transpose_a()
    g.s2(Q)
    g.s1(KV, 2)
    weight_in(2, 0)
    g.s0(G1)
    g.s1(O, 1)
    g.s1(KV, 3)
    g.s3(Q)
    weight_in(2, 1)
    g.s0(G2)
    g.s1(O, 2)
    g.s2(KV)
    g.s1(O, 3)
    weight_in(3)
    g.s0(D1)
    g.s0(D2)
    g.s1(G1, 1)
    g.s4(Q)
    g.own(0).wait()
    g.s2(O)
    g.s1(G1, 2)
    between = {
        (0, 1): lambda: g.s3(KV), (0, 3): lambda: (g.s1(G1, 3), g.s1(G2, 1)),
        (1, 1): lambda: g.s3(O), (1, 3): lambda: g.s1(G2, 2), (2, 1): lambda: (g.s2(G1), g.s1(G2, 3)), (2, 3): lambda: g.s1(D1, 1),
    }
    for p in range(3):
        if p == 1:
            g.s4(KV)
            outs[WIN].start()
        for j in range(4):
            project(p, j)
            if (p, j) in between:
                between[p, j]()
    outs[QKV].start()
    g.s4(O)
    g.own(1).wait()
    outs[WOUT].start()
    steps = {1: lambda: g.s1(D1, 2), 3: lambda: g.s3(G1), 5: lambda: g.s1(D1, 3)}
    for i in range(8):
        attend(jnp.int32(i))
        if i in steps:
            steps[i]()
    outs[OT].start()
    out_and_norm()
    g.own(2).wait()
    g.s4(G1)
    outs[WGU].start()

    def gates(first, last):
        lax.fori_loop(first, last, lambda k, _: (gate(k), 0)[1], 0)

    third = tiles // 3
    gates(0, third)
    g.s1(D2, 1)
    gates(third, 2 * third)
    g.s2(G2)
    gates(2 * third, tiles)
    outs[MT].start()
    outs[SL].start()
    g.s1(D2, 2)
    g.s2(D1)
    g.s3(G2)
    g.s1(D2, 3)
    g.s4(G2)
    outs[WGU + 1].start()
    gates(tiles, tiles + third)
    g.s3(D1)
    gates(tiles + third, 2 * tiles)
    outs[MT + 1].start()
    outs[SL + 1].start()
    g.s4(D1)
    g.s4(D2)
    g.own(3).wait()
    for c in range(len(chunks)):
        g.drain(c)
    for cp in outs:
        cp.wait()


def forward_call(x, cos, sin, lengths, slot, win, wout, wgu, wdn):
    rows, d = x.shape
    r = wout.shape[0]
    ff2 = wgu.shape[0] * 128 // r
    ff = ff2 // 2
    shapes = ((r, 3 * d), (r, d), (r, ff2), wdn.shape)
    part = wdn.shape[0] // 2
    chunks = ((0, 0, r, 0, d, 1), (0, 0, r, d, 2 * d, 1), (1, 0, r, 0, d, 1), (2, 0, r, 0, ff, 0), (2, 0, r, ff, ff, 0), (3, 0, part, 0, d, 1), (3, part, part, 0, d, None))
    vm, an, sm = (pl.BlockSpec(memory_space=m) for m in (pltpu.VMEM, pl.ANY, pltpu.SMEM))
    sd = lambda s, t=BF16: jax.ShapeDtypeStruct(s, t)
    v = lambda s, t=BF16: pltpu.VMEM(s, t)
    outs = [sd((8 * s[0], s[1])) for s in shapes] + [sd((d, rows)), sd((d, rows)), sd((d, rows)), sd((ff, rows)), sd((rows, 3 * d)), sd((rows, ff2)), sd((rows, d), F32)]
    scratch = [v(win.shape, F32), v(wout.shape, F32), v(wgu.shape, F32), v(wdn.shape, F32)] + [v(s) for s in shapes]
    scratch += [v((8 * r, 3 * d)), v((8 * r, d)), v((8 * r, ff2))]
    scratch += [v((rows, d)), v((d, rows)), v((rows, 3 * d)), v((rows, d)), v((d, rows)), v((rows, d), F32), v((rows, d)), v((d, rows)), v((ff, rows)), v((rows, ff2)), v((1, rows), F32)]
    scratch += [DMA((4,)), DMA((13,))] + Gather.scratch(4, len(chunks))
    return pl.pallas_call(
        functools.partial(forward_kernel, shapes, chunks),
        out_shape=outs, in_specs=[vm] * 3 + [sm] * 2 + [an] * 4, out_specs=[an] * len(outs), scratch_shapes=scratch,
        compiler_params=pltpu.CompilerParams(collective_id=0, has_side_effects=True, vmem_limit_bytes=60 << 20),
    )(x, cos, sin, lengths, slot, win, wout, wgu, wdn)


class Reduce:
    def __init__(self, refs):
        (self.mine, self.theirs, self.held, self.sums, self.one, self.two, self.fin, self.planes, self.far, self.keep, self.ours, self.total,
         self.a_s, self.a_r, self.o_s, self.o_r, self.t_s, self.t_r, self.c_s, self.c_r, self.d_s, self.d_r, self.f_s, self.f_r, self.g_s, self.g_r) = refs
        self.rep, self.shard = lax.axis_index("rep"), lax.axis_index("shard")
        self.core = lax.rem(self.shard, 2)
        self.x, self.y = lax.rem(self.rep, 2), self.rep // 2
        self.sib = (self.rep, self.shard + 1 - 2 * self.core)
        self.nb = ((self.rep + 1 - 2 * self.x, self.shard), (self.rep + 2 - 4 * self.y, self.shard))

    @staticmethod
    def scratch(chunks, wide):
        v = lambda *s: pltpu.VMEM(s, BF16)
        return [
            v(RING, 8, 16, wide),
            v(RING, 8, 16, wide),
            pltpu.VMEM((2, 8, 16, wide), F32),
            v(RING_SUMS, 8, 16, wide),
            v(2, RING_ONE, 2, 16, wide),
            v(2, RING_TWO, 16, wide),
            v(RING, 2, 16, wide),
            v(chunks, 3, 2, 16, wide - FAR),
            v(chunks - 1, 3, 8, 16, FAR),
            pltpu.VMEM((8, 16, FAR), F32),
            pltpu.VMEM((2, 2, 16, wide), F32),
        ], [DMA((RING,)), DMA((RING,)), DMA((2, RING_ONE)), DMA((2, RING_ONE)), DMA((2, RING_TWO)), DMA((2, RING_TWO)), DMA((RING,)), DMA((chunks, 3)),
            DMA((chunks, 2)), DMA((chunks, 2)), DMA((chunks, 2)), DMA((chunks, 2)), DMA((RING_SUMS,)), DMA((chunks - 1, 3))]

    def copy(self, src, dst, s, r, dev):
        return pltpu.make_async_remote_copy(src_ref=src, dst_ref=dst, send_sem=s, recv_sem=r, device_id=dev, device_id_type=MESH)

    def barrier(self):
        bar = pltpu.get_barrier_semaphore()
        for dev in (self.sib,) + self.nb + tuple((self.rep, lax.rem(self.shard + 2 * d, 8)) for d in (1, 2, 3)):
            pl.semaphore_signal(bar, inc=1, device_id=dev, device_id_type=MESH)
        pl.semaphore_wait(bar, 6)

    def first(self, u, w):
        s = lax.rem(u, RING)
        return self.copy(self.mine.at[s, :, :, pl.ds(0, w)], self.theirs.at[s, :, :, pl.ds(0, w)], self.a_s.at[s], self.a_r.at[s], self.sib)

    def hop_one(self, u, w, k):
        m, s = lax.rem(u, RING_SUMS), lax.rem(u, RING_ONE)
        at = 2 - 2 * self.x if k == 0 else 6 - 2 * self.y
        return self.copy(self.sums.at[m, pl.ds(at, 2), :, pl.ds(0, w)], self.one.at[k, s, :, :, pl.ds(0, w)], self.o_s.at[k, s], self.o_r.at[k, s], self.nb[k])

    def hop_two(self, u, w, k):
        m, s = lax.rem(u, RING_SUMS), lax.rem(u, RING_TWO)
        at = 2 * self.x + 1 - self.y if k == 0 else 4 + 2 * self.y + 1 - self.x
        return self.copy(self.sums.at[m, at, :, pl.ds(0, w)], self.two.at[k, s, :, pl.ds(0, w)], self.t_s.at[k, s], self.t_r.at[k, s], self.nb[1 - k])

    def across(self, u, w, dz):
        s = lax.rem(u, RING)
        c = u // 4
        return self.copy(self.fin.at[s, :, :, pl.ds(0, w)], self.planes.at[c, 3 - dz, :, :, pl.ds(0, w)], self.c_s.at[s], self.c_r.at[c, 3 - dz], (self.rep, lax.rem(self.shard + 2 * dz, 8)))

    def plane_in(self, c, w, j):
        return self.copy(self.fin.at[0, :, :, pl.ds(0, w)], self.planes.at[c, j, :, :, pl.ds(0, w)], self.c_s.at[0], self.c_r.at[c, j], self.sib)

    def spread(self, c, w, k, own=True):
        q = self.rep if own else self.nb[k][0]
        ref = self.total.at[c, q, :, :, pl.ds(0, w)]
        return self.copy(ref, ref, self.d_s.at[c, k], self.d_r.at[c, k], self.nb[k])

    def spread_on(self, c, w, k, own=True):
        q = self.nb[k][0] if own else self.nb[0][0] + self.nb[1][0] - self.rep
        ref = self.total.at[c, q, k, :, pl.ds(0, w)]
        return self.copy(ref, ref, self.f_s.at[c, k], self.f_r.at[c, k], self.nb[1 - k])

    def away(self, u, n, dz):
        m = lax.rem(u, RING_SUMS)
        return self.copy(self.sums.at[m, :, :, pl.ds(n, FAR)], self.far.at[u // 4, 3 - dz], self.g_s.at[m], self.g_r.at[u // 4, 3 - dz], (self.rep, lax.rem(self.shard + 2 * dz, 8)))

    def away_in(self, c, j):
        return self.copy(self.far.at[c, j], self.far.at[c, j], self.g_s.at[0], self.g_r.at[c, j], self.sib)

    @staticmethod
    def offset(u):
        return lax.rem(lax.rem(u, 4) + 1, 4)

    def stage_two(self, u, w, more):
        n, o = w
        s, m, dz = lax.rem(u, RING), lax.rem(u, RING_SUMS), self.offset(u)
        self.first(u, o if more else n).wait()
        held = self.held.at[lax.rem(u, 2)]
        self.sums[m, :, :, :n] = (held[:, :, :n] + self.theirs[s, :, :, :n].astype(F32)).astype(BF16)

        @pl.when(dz > 0)
        def _():
            for k in (0, 1):
                self.hop_one(u, n, k).start()
            if more:
                self.sums[m, :, :, n:o] = (held[:, :, n:o] + self.theirs[s, :, :, n:o].astype(F32)).astype(BF16)
                self.away(u, n, dz).start()

        @pl.when(dz == 0)
        def _():
            c = u // 4

            @pl.when(c > 0)
            def _():
                out = self.keep[...]
                for j in range(3):
                    self.away_in(c - 1, j).wait_recv()
                    out = out + self.far[c - 1, j].astype(F32)
                self.sums[m, :, :, n:o] = out.astype(BF16)

            @pl.when(c == 0)
            def _():
                self.sums[m, :, :, n:o] = jnp.zeros((8, 16, FAR), BF16)

            if more:
                self.keep[...] = held[:, :, n:o] + self.theirs[s, :, :, n:o].astype(F32)
            for k in (0, 1):
                self.hop_one(u, o, k).start()

    def stage_three(self, u, w):
        m, s = lax.rem(u, RING_SUMS), lax.rem(u, RING_ONE)

        def run(n):
            for k in (0, 1):
                self.hop_one(u, n, k).wait()
                at = 2 * self.x if k == 0 else 4 + 2 * self.y
                new = self.sums[m, pl.ds(at, 2), :, :n].astype(F32) + self.one[k, s, :, :, :n].astype(F32)
                self.sums[m, pl.ds(at, 2), :, :n] = new.astype(BF16)
                self.hop_two(u, n, k).start()

        pl.when(self.offset(u) > 0)(lambda: run(w[0]))
        pl.when(self.offset(u) == 0)(lambda: run(w[1]))

    def stage_four(self, u, w, start, more):
        s, m, t = lax.rem(u, RING), lax.rem(u, RING_SUMS), lax.rem(u, RING_TWO)
        n, o = w
        dz = self.offset(u)

        def plane_sum(k, n):
            self.hop_two(u, n, k).wait()
            at = 2 * self.x + self.y if k == 0 else 4 + 2 * self.y + self.x
            return self.sums[m, at, :, :n].astype(F32) + self.two[k, t, :, :n].astype(F32)

        @pl.when(dz > 0)
        def _():
            @pl.when(u >= start + RING)
            def _():
                self.across(u - RING, n, dz).wait_send()

            for k in (0, 1):
                self.fin[s, k, :, :n] = plane_sum(k, n).astype(BF16)
            self.across(u, n, dz).start()
            if more:
                self.away(u, n, dz).wait_send()

        @pl.when(dz == 0)
        def _():
            for k in (0, 1):
                self.ours[lax.rem(u // 4, 2), k, :, :o] = plane_sum(k, o)

    def stage_sum(self, u, w):
        n, o = w

        @pl.when(self.offset(u) == 0)
        def _():
            c = u // 4
            for j in range(3):
                self.plane_in(c, n, j).wait_recv()
            for k in (0, 1):
                ours = self.ours.at[lax.rem(c, 2), k]
                out = ours[:, :n]
                for j in range(3):
                    out = out + self.planes[c, j, k, :, :n].astype(F32)
                self.total[c, self.rep, k, :, :n] = out.astype(BF16)
                self.total[c, self.rep, k, :, n:o] = ours[:, n:o].astype(BF16)
            for k in (0, 1):
                self.spread(c, o, k).start()

    def stage_on(self, u, w):
        @pl.when(self.offset(u) == 0)
        def _():
            for k in (0, 1):
                self.spread(u // 4, w[1], k, False).wait_recv()
                self.spread_on(u // 4, w[1], k).start()

    def drain_across(self, units, w):
        for u in range(units - RING, units):
            if u % 4 != 3:
                self.across(u, w[0], u % 4 + 1).wait_send()

    def finish(self, units, width):
        self.drain_across(units, width(units - 1))
        for c in range(units // 4):
            w = width(4 * c)[1]
            for k in (0, 1):
                self.spread(c, w, k).wait_send()
                self.spread_on(c, w, k).wait_send()
                self.spread_on(c, w, k, False).wait_recv()


def norm_back_rows(v, d):
    n, inv = normed(v)
    return inv * (d - jnp.mean(d, axis=-1, keepdims=True) - n * jnp.mean(d * n, axis=-1, keepdims=True))


def backward_kernel(
    wide,
    x_ref, cot_ref, cos_ref, sin_ref, lengths, slot, at_h, ot_h, bt_h, mt_h, qkv_h, slopes_h, h_h, fin_h, fout_h, fgu_h, fdn_h,
    total, out_h, grad_h,
    atl, bt, mt, qkv, dgu, h, wd, wb, wo, atr, do, acc, dh, dk, dv, dy, bias_ref, ld_s, wb_s, st_s, *rs,
):
    r = Reduce(rs[:11] + (total,) + rs[11:])
    rows, d = x_ref.shape
    bounds = ((0, 8, 0), (8, 24, 1), (24, 40, 2))
    units = 40
    names = ("mt", "wd", "gu", "bt", "qkv", "h", "wo", "ot", "at")
    pairs = ((mt_h, mt), (fdn_h, wd), (slopes_h, dgu), (bt_h, bt), (qkv_h, qkv), (h_h, h), (fout_h, wo),
             (ot_h, atl.at[pl.ds(d, d), :]), (at_h, atl.at[pl.ds(0, d), :]))
    loads = {n: pltpu.make_async_copy(s, t, ld_s.at[i]) for i, (n, (s, t)) in enumerate(zip(names, pairs))}
    for n in names[:3]:
        loads[n].start()

    def weights(j):
        src = fgu_h.at[:, pl.ds(wide * j, wide)] if j < 4 else fin_h.at[:, pl.ds(d * (j - 4), d)]
        dst = wb.at[j % 2] if j < 4 else wb.at[j % 2, :, pl.ds(0, d)]
        return pltpu.make_async_copy(src, dst, wb_s.at[j % 2])

    def width(u):
        if u >= units - 4:
            return (d, d + FAR, d)
        w = wide if u < 24 else d
        return (w - FAR, w, w)

    def start_of(w):
        return next(u for u in range(units) if width(u) == w)

    def product(u, kind, first, own):
        c = u // 4 - first // 4
        zt = lax.rem(r.shard // 2 + lax.rem(u, 4) + 1, 4)
        core = r.core if own else 1 - r.core

        def put(e, lo, n, val):
            if own:
                r.held[lax.rem(u, 2), e, :, lo:lo + n] = val
            else:
                r.mine[lax.rem(u, RING), e, :, lo:lo + n] = val.astype(BF16)

        if kind == 0:
            part = mt.shape[0] // 16
            left = mt[pl.ds(pl.multiple_of((2 * zt + core) * 2 * part + c * part, 16), part), :]
            for e in range(0, 8, 2):
                val = dot(left, dy[:, e * 128:e * 128 + 256])
                for i in (0, 1):
                    for j in range(part // 16):
                        put(e + i, 128 * j, 128, val[16 * j:16 * j + 16, i * 128:i * 128 + 128])
            return
        base = (2 * zt + core) * 128
        if kind == 1:
            left = bt[pl.ds(pl.multiple_of(base, 128), 128), :]
            right, n = dgu[:, pl.ds(pl.multiple_of(c * wide, 128), wide)], wide
        else:
            left = atl[pl.ds(pl.multiple_of(base + jnp.where(c == 0, d, 0), 128), 128), :]
            right, n = atr[:, pl.ds(pl.multiple_of(c * d, 128), d)], d
        put(slice(None), 0, n, dot(left, right).reshape(8, 16, n))

    def tail(u, ws):
        for lag, stage in ((LAG_TWO, r.stage_two), (LAG_THREE, r.stage_three), (LAG_FOUR, r.stage_four), (LAG_SUM, r.stage_sum), (LAG_ON, r.stage_on)):
            w = ws[lag]
            if not w:
                continue
            more = () if lag not in (LAG_TWO, LAG_FOUR) else (w[0] < w[2],)
            start = (start_of(w),) if lag == LAG_FOUR else ()
            stage(u - lag, w[:2], *start, *more)

    def drain(u, ws):
        v = u - LAG_FOUR
        if ws[LAG_FOUR] and v == start_of(ws[LAG_FOUR]) and v > 0:
            r.drain_across(v, width(v - 1))

    def widths(u):
        return [width(u - k) if 0 <= u - k < units else None for k in range(LAG_ON + 1)]

    def step(u, kind, first, ws):
        product(u, kind, first, False)
        r.first(u, ws[0][2]).start()
        product(u, kind, first, True)
        tail(u, ws)

    def hidden(t):
        val = dot(dy[...], wd[pl.ds(pl.multiple_of(256 * t, 256), 256), :], 1, 1)
        for i in (0, 1):
            part = val[:, 128 * i:128 * i + 128]
            for j in (0, 1):
                at = pl.ds(pl.multiple_of(512 * t + 256 * i + 128 * j, 128), 128)
                dgu[:, at] = (part * dgu[:, at].astype(F32)).astype(BF16)

    def hidden_unit(u):
        hidden(u)
        tiles = mt.shape[0] // 256

        @pl.when(u + 8 < tiles)
        def _():
            hidden(u + 8)

    def input_two(j):
        weights(j).wait()
        val = dot(dgu[:, wide * j:wide * j + wide], wb[j % 2], 1, 1)
        acc[...] = val if j == 0 else acc[...] + val
        weights(j + 2).start()

    def norm_two(part):
        if part == 0:
            loads["h"].wait()
        for i in range(part * rows // 2, (part + 1) * rows // 2, 128):
            s = slice(i, i + 128)
            v = dy[s, :].astype(F32) + norm_back_rows(h[s, :], acc[s, :])
            dh[s, :] = v
            atr[s, :d] = v.astype(BF16)

    def mixed_grad():
        loads["wo"].wait()
        loads["qkv"].wait()
        do[...] = dot(atr[:, :d], wo[...], 1, 1).astype(BF16)

    def turn_back(t, s):
        return t * cos_ref[s, :] - turn(t) * sin_ref[s, :]

    def attend_tile(lanes, qt):
        n = 128 * (qt + 1)
        s = slice(128 * qt, n)
        keys = qkv[:n, lanes[1]]
        q2, g2 = two_heads(qkv[s, lanes[0]]), two_heads(do[s, lanes[0]])
        p = probabilities(q2, keys, bias_ref[:, :n])
        dp = dot(g2, qkv[:n, lanes[2]], 1, 1)
        ds = (p * (dp - jnp.sum(p * dp, axis=-1, keepdims=True)) * 0.125).astype(BF16)
        new_v, new_k = dot(p.astype(BF16), g2, 0, 0), dot(ds, q2, 0, 0)
        if n == rows:
            dv[...] = new_v
            dk[...] = new_k
        else:
            dv[:n, :] = dv[:n, :] + new_v
            dk[:n, :] = dk[:n, :] + new_k
        atr[s, lanes[1]] = turn_back(join_heads(dot(ds, keys)), s).astype(BF16)

    def attend_half(k):
        lo = pl.multiple_of(k // 2 * 128, 128)
        lanes = [pl.ds(pl.multiple_of(lo + d * i, 128), 128) for i in range(4)]
        tiles = rows // 128

        @pl.when(lax.rem(k, 2) == 0)
        def _():
            for qt in (tiles - 1, 0):
                attend_tile(lanes, qt)

        @pl.when(lax.rem(k, 2) == 1)
        def _():
            for qt in range(1, tiles - 1):
                attend_tile(lanes, qt)
            atr[:, lanes[2]] = turn_back(dk[...], slice(0, rows)).astype(BF16)
            atr[:, lanes[3]] = dv[...].astype(BF16)

    def input_one(j):
        weights(4 + j).wait()
        val = dot(atr[:, d * (j + 1):d * (j + 2)], wb[j % 2, :, :d], 1, 1)
        acc[...] = val if j == 0 else acc[...] + val
        if j == 0:
            weights(6).start()

    grad_out = pltpu.make_async_copy(dh, grad_h, st_s.at[0])
    result_out = pltpu.make_async_copy(do, out_h, st_s.at[1])

    def norm_one():
        for i in range(0, rows, 128):
            s = slice(i, i + 128)
            dh[s, :] = dh[s, :] + norm_back_rows(x_ref[s, :].astype(F32), acc[s, :])
        grad_out.start()

    def result(i):
        s = slice(256 * i, 256 * i + 256)
        do[s, :] = jnp.where(alive(256 * i, 256), h[s, :] + dot(mt[:, s], wd[...], 0, 0), 0.0).astype(BF16)

    before = {0: lambda: loads["mt"].wait(), 8: lambda: loads["bt"].wait(), 24: lambda: loads["ot"].wait(), 28: lambda: loads["at"].wait()}
    fill = {8 + j: functools.partial(input_two, j) for j in range(4)}
    fill[11] = lambda: (input_two(3), norm_two(0))
    fill[12] = lambda: (norm_two(1), mixed_grad())
    fill[27] = lambda: attend_half(jnp.int32(15))
    fill.update({29 + 2 * j: functools.partial(input_one, j) for j in range(3)})
    fill[35] = norm_one
    fill[36] = lambda: result(0)
    fill[37] = lambda: (result(1), result_out.start())
    fill[0] = lambda: [loads[n].start() for n in names[3:]] + [weights(j).start() for j in (0, 1)]
    fill[1] = lambda: (loads["wd"].wait(), loads["gu"].wait(), hidden_unit(jnp.int32(0)))
    fill[7] = lambda: hidden_unit(jnp.int32(7))
    ranged = [(2, 8, lambda u: hidden_unit(u - 1)), (13, 28, lambda u: attend_half(u - 13))]

    length = lengths[slot[0]]

    def alive(first, n):
        return lax.broadcasted_iota(jnp.int32, (n, d), 0) + first < length

    for i in range(0, rows, 128):
        s = slice(i, i + 128)
        dy[s, :] = jnp.where(alive(i, 128), cot_ref[s, :].astype(F32), 0.0).astype(BF16)
    key_bias(bias_ref, length)
    r.barrier()
    edges = sorted({a for a, _, _ in bounds} | {e for a, b, _ in ranged for e in (a, b)} | {units, units - 4} | set(before))
    u = 0
    while u < units:
        if u in before:
            before[u]()
        ws = widths(u)
        first, _, kind = next(b for b in bounds if b[0] <= u < b[1])
        w = width(u)
        in_range = next((f for a, b, f in ranged if a <= u < b), None)
        end = min(e for e in edges if e > u)
        plain = all(x == w for x in ws) and u not in fill
        stop = u
        while plain and stop < end and stop not in fill:
            stop += 1
        if plain and stop - u > 1:
            def body(i, _, kind=kind, first=first, ws=ws, f=in_range):
                step(i, kind, first, ws)
                if f:
                    f(i)
                return 0
            lax.fori_loop(u, stop, body, 0)
            u = stop
            continue
        drain(u, ws)
        step(jnp.int32(u), kind, first, ws)
        if in_range:
            in_range(jnp.int32(u))
        if u in fill:
            fill[u]()
        u += 1
    for u in range(units, units + LAG_ON + 1):
        drain(u, widths(u))
        tail(jnp.int32(u), widths(u))
    r.finish(units, width)
    grad_out.wait()
    result_out.wait()


def backward_call(x, cot, cos, sin, lengths, slot, saved, full):
    rows, d = x.shape
    ff = saved[3].shape[0]
    wide = 2 * ff // 4
    chunks = 10
    vm, an, sm = (pl.BlockSpec(memory_space=m) for m in (pltpu.VMEM, pl.ANY, pltpu.SMEM))
    v = lambda s, t=BF16: pltpu.VMEM(s, t)
    bufs, sems = Reduce.scratch(chunks, wide)
    scratch = [v((2 * d, rows)), v((d, rows)), v((ff, rows)), v((rows, 3 * d)), v((rows, 2 * ff)), v((rows, d), F32), v((ff, d)), v((2, d, wide)), v((d, d)),
               v((rows, 4 * d)), v((rows, d)), v((rows, d), F32), v((rows, d), F32), v((rows, 128), F32), v((rows, 128), F32), v((rows, d)), v((1, rows), F32), DMA((9,)), DMA((2,)), DMA((2,))]
    return pl.pallas_call(
        functools.partial(backward_kernel, wide),
        out_shape=[jax.ShapeDtypeStruct((chunks, 4, 2, 16, wide), BF16), jax.ShapeDtypeStruct((rows, d), BF16), jax.ShapeDtypeStruct((rows, d), F32)],
        in_specs=[vm] * 4 + [sm] * 2 + [an] * 11, out_specs=[vm, an, an], scratch_shapes=scratch + bufs + sems,
        compiler_params=pltpu.CompilerParams(collective_id=1, has_side_effects=True, vmem_limit_bytes=63 << 20),
    )(x, cot, cos, sin, lengths, slot, *saved, *full)


def adam_kernel(scalars, total, *refs):
    masters, outs, spread = refs[:12], refs[12:28], refs[28]
    first_scale, second_scale, rate = scalars[0], scalars[1], scalars[2]
    wide = total.shape[-1]
    cols = wide // 128
    d = masters[3].shape[1]

    def update(k, at, grad):
        w, m, v = (masters[3 * k + j][at] for j in range(3))
        m = beta_first * m + (1.0 - beta_first) * grad
        v = beta_second * v + (1.0 - beta_second) * grad * grad
        outs[4 * k][at] = grad
        outs[4 * k + 1][at] = w - rate * (m * first_scale / (jnp.sqrt(v * second_scale) + adam_eps) + weight_decay * w)
        outs[4 * k + 2][at] = m
        outs[4 * k + 3][at] = v

    def piece(c, lo, n):
        w = (wide if c < 6 else d) - FAR
        if c < 9 and lo >= w:
            lo = lo - w + (wide - FAR if c < 5 else d - FAR if c < 8 else d)
            c += 1
        return total[c, 0, 0, :, lo:lo + n].astype(F32)

    for lo, hi in ((0, d - FAR), (d - FAR, d)):
        for p in range(3):
            update(0, (p, slice(None), slice(lo, hi)), piece(7 + p, lo, hi - lo))
        update(1, (slice(None), slice(lo, hi)), piece(6, lo, hi - lo))
    stride = 4 * cols
    for c in range(4):
        for j in range(cols):
            spread[pl.ds(c * cols + j, 16, stride=stride), :] = piece(2 + c, 128 * j, 128)
    for i in range(0, 16 * stride, 176):
        s = (slice(i, i + 176),)
        update(2, s, spread[s])
    half = 16 * cols
    for c in (0, 1):
        for j in range(cols):
            update(3, (slice(c * half + 16 * j, c * half + 16 * j + 16),), piece(c, 128 * j, 128))


def adam_call(scalars, total, masters):
    chunks, _, _, _, wide = total.shape
    blocks = []
    for k, shape in enumerate((masters[0].shape, masters[3].shape, masters[6].shape, masters[9].shape)):
        if k == 0:
            blocks.append(pl.BlockSpec((3, shape[1] // 8, shape[2]), lambda i: (0, i, 0)))
        elif k < 3:
            blocks.append(pl.BlockSpec((shape[0] // 8, shape[1]), lambda i: (i, 0)))
        else:
            blocks.append(pl.BlockSpec((shape[0], shape[1] // 8), lambda i: (0, i)))

    def part(i):
        low = lax.rem(i, 2) * 2 + i // 2
        return (0, jnp.where(i < 4, low, i - 4), i // 4, 0, 0)

    shapes = [masters[3 * k].shape for k in range(4) for _ in range(4)]
    return pl.pallas_call(
        adam_kernel,
        grid=(8,),
        out_shape=[jax.ShapeDtypeStruct(s, F32) for s in shapes],
        in_specs=[pl.BlockSpec(memory_space=pltpu.SMEM), pl.BlockSpec((chunks, 1, 1, 16, wide), part)] + [blocks[k] for k in range(4) for _ in range(3)],
        out_specs=[blocks[k] for k in range(4) for _ in range(4)],
        scratch_shapes=[pltpu.VMEM((masters[6].shape[0] // 8, 128), F32)],
        compiler_params=pltpu.CompilerParams(vmem_limit_bytes=60 << 20),
    )(scalars, total, *masters)


def gather_full(local, rep_count, rep_index):
    rows = local.shape[0]
    flat = local.reshape(rows, -1)
    width = flat.shape[1] // rep_count
    piece = lax.dynamic_slice_in_dim(flat, rep_index * width, width, axis=1)
    column = lax.all_gather(piece, "shard", axis=0, tiled=True)
    return lax.all_gather(column, "rep", axis=0, tiled=False)


def reduce_full(partial):
    part = lax.psum_scatter(partial, "rep", scatter_dimension=0, tiled=False)
    part = lax.psum_scatter(part, "shard", scatter_dimension=0, tiled=True)
    pieces = lax.all_gather(part, "rep", axis=0, tiled=False)
    rows = pieces.shape[1]
    return jnp.transpose(pieces, (1, 0, 2)).reshape(rows, -1).astype(jnp.float32)


def shards_generic(
    tokens,
    cotangent,
    lengths,
    slot_sequence,
    step_count,
    learn_rate,
    attention_in,
    attention_in_first,
    attention_in_second,
    attention_out,
    attention_out_first,
    attention_out_second,
    gate_up_weight,
    gate_up_first,
    gate_up_second,
    down_weight,
    down_first,
    down_second,
):
    slot_count, position_count, feature_count = tokens.shape
    row_total = slot_count * position_count
    head_count = feature_count // HD
    shaped = (slot_count, position_count, head_count, HD)
    inputs = tokens.astype(jnp.float32).reshape(row_total, feature_count)
    matches = jnp.arange(lengths.shape[0])[None, :] == slot_sequence[:, None]
    slot_length = jnp.sum(jnp.where(matches, lengths[None, :], 0), axis=1)
    alive_rows = (
        (jnp.arange(position_count)[None, :] < slot_length[:, None])
        .astype(jnp.float32)
        .reshape(row_total, 1)
    )
    cosine_table, sine_table = rope_tables(position_count, HD)
    in_local = attention_in.astype(jnp.bfloat16)
    out_local = attention_out.astype(jnp.bfloat16)
    gate_up_local = gate_up_weight.astype(jnp.bfloat16)
    down_local = down_weight.astype(jnp.bfloat16)
    rep_count = lax.axis_size("rep")
    rep_index = lax.axis_index("rep")
    in_full = gather_full(in_local, rep_count, rep_index)
    out_full = gather_full(out_local, rep_count, rep_index)
    gate_up_full = gather_full(gate_up_local, rep_count, rep_index)
    down_full = gather_full(down_local, rep_count, rep_index)
    normed_one, inverse_one = layer_norm(inputs)
    first_input = normed_one.astype(jnp.bfloat16)
    projected = jnp.einsum(
        "rd,qde->rqe", first_input, in_full, preferred_element_type=jnp.float32
    ).reshape(row_total, 3, feature_count)
    queries = rotate(projected[:, 0].reshape(shaped), cosine_table, sine_table).astype(jnp.bfloat16)
    rotated_keys = rotate(projected[:, 1].reshape(shaped), cosine_table, sine_table).astype(
        jnp.bfloat16
    )
    values_low = projected[:, 2].reshape(shaped).astype(jnp.bfloat16)
    mixed_heads, log_total = lax.map(
        attend_forward, (queries, rotated_keys, values_low, slot_length)
    )
    mixed_low = mixed_heads.reshape(row_total, feature_count).astype(jnp.bfloat16)
    residual = inputs + jnp.einsum(
        "rd,qde->rqe", mixed_low, out_full, preferred_element_type=jnp.float32
    ).reshape(row_total, feature_count)
    normed_two, inverse_two = layer_norm(residual)
    second_input = normed_two.astype(jnp.bfloat16)
    gate_up = jnp.einsum(
        "rd,qdf->rqf", second_input, gate_up_full, preferred_element_type=jnp.float32
    ).reshape(row_total, 2, -1)
    gate_value = gate_up[:, 0]
    up_value = gate_up[:, 1]
    sigmoid_gate = jax.nn.sigmoid(gate_value)
    hidden_low = (gate_value * sigmoid_gate * up_value).astype(jnp.bfloat16)
    result = residual + jnp.einsum(
        "rf,qfe->rqe", hidden_low, down_full, preferred_element_type=jnp.float32
    ).reshape(row_total, feature_count)
    output = (result * alive_rows).astype(jnp.bfloat16).reshape(tokens.shape)
    output_grad = cotangent.astype(jnp.float32).reshape(row_total, feature_count) * alive_rows
    result_grad_low = output_grad.astype(jnp.bfloat16)
    hidden_grad = jnp.einsum(
        "rqe,qfe->rf",
        result_grad_low.reshape(row_total, rep_count, -1),
        down_full,
        preferred_element_type=jnp.float32,
    )
    gate_grad = hidden_grad * up_value * sigmoid_gate * (1.0 + gate_value * (1.0 - sigmoid_gate))
    up_grad = hidden_grad * gate_value * sigmoid_gate
    gate_up_grad_low = (
        jnp.concatenate([gate_grad, up_grad], axis=1)
        .astype(jnp.bfloat16)
        .reshape(row_total, rep_count, -1)
    )
    second_input_grad = jnp.einsum(
        "rqf,qdf->rd", gate_up_grad_low, gate_up_full, preferred_element_type=jnp.float32
    )
    residual_grad = output_grad + norm_back(normed_two, inverse_two, second_input_grad)
    down_part = reduce_full(
        jnp.einsum(
            "rc,rqe->qce",
            hidden_low,
            result_grad_low.reshape(row_total, rep_count, -1),
            preferred_element_type=jnp.float32,
        ).astype(jnp.bfloat16)
    )
    gate_up_part = reduce_full(
        jnp.einsum(
            "rc,rqf->qcf", second_input, gate_up_grad_low, preferred_element_type=jnp.float32
        ).astype(jnp.bfloat16)
    ).reshape(gate_up_weight.shape)
    branch_grad = residual_grad.astype(jnp.bfloat16)
    mixed_grad = (
        jnp.einsum(
            "rqe,qde->rd",
            branch_grad.reshape(row_total, rep_count, -1),
            out_full,
            preferred_element_type=jnp.float32,
        )
        .astype(jnp.bfloat16)
        .reshape(shaped)
    )
    query_grad, key_grad, value_grad = lax.map(
        attend_backward, (queries, rotated_keys, values_low, slot_length, log_total, mixed_grad)
    )
    query_back = rotate(query_grad, cosine_table, -sine_table).reshape(row_total, feature_count)
    key_back = rotate(key_grad, cosine_table, -sine_table).reshape(row_total, feature_count)
    projected_grad = (
        jnp.concatenate([query_back, key_back, value_grad.reshape(row_total, feature_count)], axis=1)
        .astype(jnp.bfloat16)
        .reshape(row_total, rep_count, -1)
    )
    first_input_grad = jnp.einsum(
        "rqe,qde->rd", projected_grad, in_full, preferred_element_type=jnp.float32
    )
    input_grad = (residual_grad + norm_back(normed_one, inverse_one, first_input_grad)).reshape(
        tokens.shape
    )
    in_part = reduce_full(
        jnp.einsum(
            "rc,rqe->qce", first_input, projected_grad, preferred_element_type=jnp.float32
        ).astype(jnp.bfloat16)
    ).reshape(attention_in.shape)
    out_part = reduce_full(
        jnp.einsum(
            "rc,rqe->qce",
            mixed_low,
            branch_grad.reshape(row_total, rep_count, -1),
            preferred_element_type=jnp.float32,
        ).astype(jnp.bfloat16)
    )
    in_grad, in_new, in_first, in_second = adam_update(
        attention_in,
        attention_in_first,
        attention_in_second,
        in_part,
        step_count,
        learn_rate,
    )
    out_grad, out_new, out_first, out_second = adam_update(
        attention_out,
        attention_out_first,
        attention_out_second,
        out_part,
        step_count,
        learn_rate,
    )
    gu_grad, gu_new, gu_first, gu_second = adam_update(
        gate_up_weight, gate_up_first, gate_up_second, gate_up_part, step_count, learn_rate
    )
    dn_grad, dn_new, dn_first, dn_second = adam_update(
        down_weight, down_first, down_second, down_part, step_count, learn_rate
    )
    return (
        output,
        input_grad,
        in_grad,
        in_new,
        in_first,
        in_second,
        out_grad,
        out_new,
        out_first,
        out_second,
        gu_grad,
        gu_new,
        gu_first,
        gu_second,
        dn_grad,
        dn_new,
        dn_first,
        dn_second,
    )


def shards_fast(
    tokens,
    cotangent,
    lengths,
    slot_sequence,
    step_count,
    learn_rate,
    attention_in,
    attention_in_first,
    attention_in_second,
    attention_out,
    attention_out_first,
    attention_out_second,
    gate_up_weight,
    gate_up_first,
    gate_up_second,
    down_weight,
    down_first,
    down_second,
):
    _, rows, d = tokens.shape
    x = tokens.reshape(rows, d)
    cosine, sine = half_turns(rows, HD)
    owned, _, ff = gate_up_weight.shape
    tiles = ff // 128

    def tiled(value):
        value = value.reshape(owned, 2, tiles, 128).transpose(0, 2, 1, 3)
        return with_layout_constraint(value, rowwise).reshape(-1, 128)

    def untiled(value):
        value = with_layout_constraint(value.reshape(owned, tiles, 2, 128), rowwise)
        return value.transpose(0, 2, 1, 3).reshape(owned, 2, ff)

    heads = [value.transpose(1, 0, 2) for value in (attention_in, attention_in_first, attention_in_second)]
    gates = [tiled(value) for value in (gate_up_weight, gate_up_first, gate_up_second)]
    results = forward_call(x, cosine, sine, lengths, slot_sequence, heads[0], attention_out, gates[0], down_weight)
    full, saved = results[:4], results[4:]
    total, output, input_grad = backward_call(x, cotangent.reshape(rows, d), cosine, sine, lengths, slot_sequence, saved, full)
    steps_taken = step_count[0].astype(F32)
    scalars = jnp.stack([1.0 / (1.0 - beta_first**steps_taken), 1.0 / (1.0 - beta_second**steps_taken), learn_rate[0]])
    masters = heads + [attention_out, attention_out_first, attention_out_second] + gates + [down_weight, down_first, down_second]
    new = adam_call(scalars, total, masters)
    return (
        output.reshape(tokens.shape),
        input_grad.reshape(tokens.shape),
        *[value.transpose(1, 0, 2) for value in new[:4]],
        *new[4:8],
        *[untiled(value) for value in new[8:12]],
        *new[12:],
    )


def solution(mesh):
    fast = mesh.shape["rep"] == 4 and mesh.shape["shard"] == 8
    return jax.shard_map(
        shards_fast if fast else shards_generic,
        mesh=mesh,
        in_specs=(
            P(("rep", "shard"), None, None),
            P(("rep", "shard"), None, None),
            P(),
            P(("rep", "shard")),
            P(),
            P(),
            P("shard", None, None),
            P("shard", None, None),
            P("shard", None, None),
            P("shard", None),
            P("shard", None),
            P("shard", None),
            P("shard", None, None),
            P("shard", None, None),
            P("shard", None, None),
            P("shard", None),
            P("shard", None),
            P("shard", None),
        ),
        out_specs=(
            P(("rep", "shard"), None, None),
            P(("rep", "shard"), None, None),
            P("shard", None, None),
            P("shard", None, None),
            P("shard", None, None),
            P("shard", None, None),
            P("shard", None),
            P("shard", None),
            P("shard", None),
            P("shard", None),
            P("shard", None, None),
            P("shard", None, None),
            P("shard", None, None),
            P("shard", None, None),
            P("shard", None),
            P("shard", None),
            P("shard", None),
            P("shard", None),
        ),
        check_vma=False,
    )
```

```python
import functools

import jax
import jax.numpy as jnp
import numpy as np
from jax import lax
from jax.experimental import pallas as pl
from jax.experimental.layout import Layout, with_layout_constraint
from jax.experimental.pallas import tpu as pltpu
from jax.sharding import PartitionSpec as P

MESH = pl.DeviceIdType.MESH
DMA = pltpu.SemaphoreType.DMA
RING, RING_ONE, RING_SUMS, RING_TWO = 4, 6, 5, 6
LAG_TWO, LAG_THREE, LAG_FOUR, LAG_SUM, LAG_ON = 1, 3, 5, 8, 10
FAR = 256
F32, BF16 = jnp.float32, jnp.bfloat16
rowwise = Layout(major_to_minor=(0, 1, 2, 3))

HD = 64


norm_eps = 1e-05
beta_first = 0.9
beta_second = 0.95
adam_eps = 1e-08
weight_decay = 0.1
rope_base = 10000.0
masked_score = -1e30


def layer_norm(values):
    centered = values - jnp.mean(values, axis=-1, keepdims=True)
    inverse = lax.rsqrt(jnp.mean(centered * centered, axis=-1, keepdims=True) + norm_eps)
    return (centered * inverse, inverse)


def norm_back(normed, inverse, upstream):
    mean_grad = jnp.mean(upstream, axis=-1, keepdims=True)
    mean_dot = jnp.mean(upstream * normed, axis=-1, keepdims=True)
    return inverse * (upstream - mean_grad - normed * mean_dot)


def rope_tables(position_count, head_size):
    half_size = head_size // 2
    frequency = rope_base ** (-(jnp.arange(half_size, dtype=jnp.float32) * 2.0 / head_size))
    angles = jnp.arange(position_count, dtype=jnp.float32)[:, None] * frequency[None, :]
    angles = jnp.concatenate([angles, angles], axis=1)
    return (jnp.cos(angles)[:, None, :], jnp.sin(angles)[:, None, :])


def half_turns(position_count, head_size):
    half_size = head_size // 2
    frequency = np.float32(rope_base) ** (-(np.arange(half_size, dtype=np.float32) * np.float32(2.0) / np.float32(head_size)))
    angles = np.arange(position_count, dtype=np.float32)[:, None] * frequency[None, :]
    cosine, sine = np.cos(angles), np.sin(angles)
    return (
        jnp.asarray(np.concatenate([cosine] * 4, axis=1), jnp.float32),
        jnp.asarray(np.concatenate([-sine, sine] * 2, axis=1), jnp.float32),
    )


def rotate(values, cosine_table, sine_table):
    half_size = values.shape[-1] // 2
    turned = jnp.concatenate([-values[..., half_size:], values[..., :half_size]], axis=-1)
    return values * cosine_table + turned * sine_table


def masked_scores(queries, rotated_keys, length):
    position_count, head_size = (queries.shape[0], queries.shape[-1])
    scores = jnp.einsum(
        "qhd,khd->hqk", queries, rotated_keys, preferred_element_type=jnp.float32
    ) * head_size ** (-0.5)
    position = jnp.arange(position_count)
    allowed = (position[None, :] <= position[:, None]) & (position[None, :] < length)
    return jnp.where(allowed[None], scores, masked_score)


def attend_forward(pieces):
    queries, rotated_keys, values_low, length = pieces
    scores = masked_scores(queries, rotated_keys, length)
    row_max = jnp.max(scores, axis=-1, keepdims=True)
    exponent = jnp.exp(scores - row_max)
    row_sum = jnp.sum(exponent, axis=-1, keepdims=True)
    weights = (exponent / row_sum).astype(jnp.bfloat16)
    mixed_heads = jnp.einsum(
        "hqk,khd->qhd", weights, values_low, preferred_element_type=jnp.float32
    )
    return (mixed_heads, row_max + jnp.log(row_sum))


def attend_backward(pieces):
    queries, rotated_keys, values_low, length, log_total, mixed_grad = pieces
    head_size = queries.shape[-1]
    scores = masked_scores(queries, rotated_keys, length)
    probability = jnp.exp(scores - log_total)
    value_grad = jnp.einsum(
        "hqk,qhd->khd",
        probability.astype(jnp.bfloat16),
        mixed_grad,
        preferred_element_type=jnp.float32,
    )
    probability_grad = jnp.einsum(
        "qhd,khd->hqk", mixed_grad, values_low, preferred_element_type=jnp.float32
    )
    inner_dot = jnp.sum(probability * probability_grad, axis=-1, keepdims=True)
    score_grad = (probability * (probability_grad - inner_dot) * head_size ** (-0.5)).astype(
        jnp.bfloat16
    )
    query_grad = jnp.einsum(
        "hqk,khd->qhd", score_grad, rotated_keys, preferred_element_type=jnp.float32
    )
    key_grad = jnp.einsum("hqk,qhd->khd", score_grad, queries, preferred_element_type=jnp.float32)
    return (query_grad, key_grad, value_grad)


def adam_update(weight, first, second, gradient, step_count, learn_rate):
    steps_taken = step_count[0].astype(jnp.float32)
    first_new = beta_first * first + (1.0 - beta_first) * gradient
    second_new = beta_second * second + (1.0 - beta_second) * gradient * gradient
    first_hat = first_new / (1.0 - beta_first**steps_taken)
    second_hat = second_new / (1.0 - beta_second**steps_taken)
    weight_new = weight - learn_rate[0] * (
        first_hat / (jnp.sqrt(second_hat) + adam_eps) + weight_decay * weight
    )
    return (gradient, weight_new, first_new, second_new)


class Gather:
    @staticmethod
    def scratch(tensors, chunks):
        return [DMA((tensors,)), DMA((chunks, 4)), DMA((chunks, 4)), DMA((chunks, 2, 3)), DMA((chunks, 2, 3))] + [DMA((chunks, 3, 2))] * 4

    def __init__(self, shapes, chunks, loc, full, sems):
        self.shapes, self.chunks, self.loc, self.full = shapes, chunks, loc, full
        (self.own_s, self.sib_s, self.sib_r, self.z_s, self.z_r, self.p_s, self.p_r, self.d_s, self.d_r) = sems
        self.rep, self.shard = lax.axis_index("rep"), lax.axis_index("shard")
        self.z, core = self.shard // 2, lax.rem(self.shard, 2)
        x, y = lax.rem(self.rep, 2), self.rep // 2
        self.sib = (self.rep, self.shard + 1 - 2 * core)
        self.nb = ((self.rep + 1 - 2 * x, self.shard), (self.rep + 2 - 4 * y, self.shard))
        self.diag = self.rep + (1 - 2 * x) + (2 - 4 * y)

    def barrier(self):
        bar = pltpu.get_barrier_semaphore()
        for dev in (self.sib,) + self.nb + tuple((self.rep, self.other(d)) for d in (1, 2, 3)):
            pl.semaphore_signal(bar, inc=1, device_id=dev, device_id_type=MESH)
        pl.semaphore_wait(bar, 6)

    def ref(self, c, s, q=None, half=None):
        t, r0, rows, c0, cols, axis = self.chunks[c]
        base, col, nr, nc = s * self.shapes[t][0] + r0, c0, rows, cols
        if q is not None:
            parts, i = (4, q) if half is None else (8, 2 * q + half)
            if axis == 0:
                nr = rows // parts
                base = base + i * nr
            else:
                nc = cols // parts
                col = pl.multiple_of(c0 + i * nc, 128)
        return self.full[t].at[pl.ds(pl.multiple_of(base, 16), nr), pl.ds(col, nc)]

    def loc_ref(self, c, q=None):
        t, r0, rows, c0, cols, axis = self.chunks[c]
        row, col, nr, nc = r0, c0, rows, cols
        if q is not None and axis == 0:
            nr = rows // 4
            row = pl.multiple_of(r0 + q * nr, 16)
        elif q is not None:
            nc = cols // 4
            col = pl.multiple_of(c0 + q * nc, 128)
        return self.loc[t].at[pl.ds(row, nr), pl.ds(col, nc)]

    def copy(self, src, dst, s, r, dev):
        return pltpu.make_async_remote_copy(src_ref=src, dst_ref=dst, send_sem=s, recv_sem=r, device_id=dev, device_id_type=MESH)

    def own(self, t):
        rows = self.shapes[t][0]
        return pltpu.make_async_copy(self.loc[t], self.full[t].at[pl.ds(pl.multiple_of(self.shard * rows, rows), rows), :], self.own_s.at[t])

    def other(self, dz):
        return lax.rem(self.shard + 2 * dz, 8)

    def sibling(self, c, dz):
        r = self.ref(c, self.other(dz))
        return self.copy(self.loc_ref(c) if dz == 0 else r, r, self.sib_s.at[c, dz], self.sib_r.at[c, dz], self.sib)

    def quarter(self, c):
        return None if self.chunks[c][5] is None else self.rep

    def chain(self, c, side, h):
        sgn = 1 if side == 0 else -1
        s = self.shard - sgn * 2 * (h - 1)
        q = self.quarter(c)
        src = self.loc_ref(c, q) if h == 1 else self.ref(c, s, q)
        return self.copy(src, self.ref(c, s, q), self.z_s.at[c, side, h - 1], self.z_r.at[c, side, h - 1], (self.rep, self.shard + sgn * 2))

    def chain_in(self, c, side, h):
        sgn = 1 if side == 0 else -1
        r = self.ref(c, self.shard - sgn * 2 * h, self.quarter(c))
        return self.copy(r, r, self.z_s.at[c, side, h - 1], self.z_r.at[c, side, h - 1], (self.rep, self.shard - sgn * 2))

    def chain_sends(self, side, h):
        if side == 0:
            return jnp.logical_and(self.z < 3, self.z >= h - 1)
        return jnp.logical_and(self.z > 0, self.z <= 4 - h)

    def plane(self, c, dz, k, theirs=False):
        r = self.ref(c, self.other(dz), self.nb[k][0] if theirs else self.rep)
        return self.copy(r, r, self.p_s.at[c, dz - 1, k], self.p_r.at[c, dz - 1, k], self.nb[k])

    def corner(self, c, dz, k, theirs=False):
        r = self.ref(c, self.other(dz), self.diag if theirs else self.nb[k][0], k)
        return self.copy(r, r, self.d_s.at[c, dz - 1, k], self.d_r.at[c, dz - 1, k], self.nb[1 - k])

    def s0(self, c):
        for side in (0, 1):
            @pl.when(self.chain_sends(side, 1))
            def _():
                self.chain(c, side, 1).start()
        self.sibling(c, 0).start()

    def s1(self, c, h):
        for side in (0, 1):
            @pl.when((self.z >= h) if side == 0 else (self.z <= 3 - h))
            def _():
                self.chain_in(c, side, h).wait_recv()
                if h < 3:
                    @pl.when((self.z < 3) if side == 0 else (self.z > 0))
                    def _():
                        self.chain(c, side, h + 1).start()
                dz = (4 - h) if side == 0 else h
                if self.quarter(c) is None:
                    self.sibling(c, dz).start()
                else:
                    for k in (0, 1):
                        self.plane(c, dz, k).start()

    def s2(self, c):
        for dz in (1, 3, 2):
            for k in (0, 1):
                self.plane(c, dz, k, True).wait_recv()
                self.corner(c, dz, k).start()

    def s3(self, c):
        for dz in (1, 3, 2):
            for k in (0, 1):
                self.corner(c, dz, k, True).wait_recv()
            self.sibling(c, dz).start()

    def s4(self, c):
        for dz in range(4):
            self.sibling(c, dz).wait()

    def drain(self, c):
        for side in (0, 1):
            for h in (1, 2, 3):
                @pl.when(self.chain_sends(side, h))
                def _():
                    self.chain(c, side, h).wait_send()
        for dz in (1, 2, 3) if self.quarter(c) is not None else ():
            for k in (0, 1):
                self.plane(c, dz, k).wait_send()
                self.corner(c, dz, k).wait_send()


def normed(v):
    c = v - jnp.mean(v, axis=-1, keepdims=True)
    inv = lax.rsqrt(jnp.mean(c * c, axis=-1, keepdims=True) + norm_eps)
    return c * inv, inv


def turn(w):
    lane = lax.broadcasted_iota(jnp.int32, w.shape, 1)
    return jnp.where(lax.rem(lane, 64) < 32, pltpu.roll(w, 96, 1), pltpu.roll(w, 32, 1))


def two_heads(w):
    lane = lax.broadcasted_iota(jnp.int32, w.shape, 1)
    zero = jnp.zeros_like(w)
    return jnp.concatenate([jnp.where(lane < 64, w, zero), jnp.where(lane < 64, zero, w)], axis=0)


def join_heads(w):
    n = w.shape[0] // 2
    lane = lax.broadcasted_iota(jnp.int32, (n, w.shape[1]), 1)
    return jnp.where(lane < 64, w[:n], w[n:])


def dot(a, b, da=1, db=0):
    return lax.dot_general(a, b, (((da,), (db,)), ((), ())), preferred_element_type=F32)


def key_bias(ref, length):
    ref[...] = jnp.where(lax.broadcasted_iota(jnp.int32, ref.shape, 1) < length, 0.0, -1e30)


def probabilities(q2, keys, bias):
    n, width = q2.shape[0] // 2, keys.shape[0]
    s = dot(q2, keys, 1, 1) * 0.125 + bias
    row = lax.broadcasted_iota(jnp.int32, (n, 128), 0)
    col = lax.broadcasted_iota(jnp.int32, (n, 128), 1)
    causal = jnp.where(col <= row, 0.0, -1e30)
    last = s[:, width - 128:] + jnp.concatenate([causal, causal], axis=0)
    s = last if width == 128 else jnp.concatenate([s[:, :width - 128], last], axis=1)
    e = jnp.exp(s - jnp.max(s, axis=-1, keepdims=True))
    return e * (1.0 / jnp.sum(e, axis=-1, keepdims=True))


def forward_kernel(
    shapes, chunks,
    x_ref, cos_ref, sin_ref, lengths, slot, win_h, wout_h, wgu_h, wdn_h,
    fin_h, fout_h, fgu_h, fdn_h, at_h, ot_h, bt_h, mt_h, qkv_h, slopes_h, h_h,
    win, wout, wgu, wdn, lin, lout, lgu, ldn, bin_, bout, bgu,
    a, at, qkv, o, ot, h, b, bt, mt, slopes, bias_ref, in_s, out_s, *sems,
):
    g = Gather(shapes, chunks, (lin, lout, lgu, ldn), (bin_, bout, bgu, fdn_h), sems)
    rows = x_ref.shape[0]
    loads = [pltpu.make_async_copy(s, d, in_s.at[i]) for i, (s, d) in enumerate(((win_h, win), (wout_h, wout), (wgu_h, wgu), (wdn_h, wdn)))]
    loads[0].start()
    ffh, half = mt.shape[0] // 2, slopes.shape[1] // 2
    stores = [(at, at_h), (ot, ot_h), (bt, bt_h), (qkv, qkv_h), (h, h_h)]
    stores += [(m.at[pl.ds(i * ffh, ffh), :], n.at[pl.ds(i * ffh, ffh), :]) for m, n in ((mt, mt_h),) for i in (0, 1)]
    stores += [(m.at[:, pl.ds(i * half, half)], n.at[:, pl.ds(i * half, half)]) for m, n in ((slopes, slopes_h),) for i in (0, 1)]
    stores += [(bin_, fin_h), (bout, fout_h)] + [(bgu.at[:, pl.ds(i * half, half)], fgu_h.at[:, pl.ds(i * half, half)]) for i in (0, 1)]
    outs = [pltpu.make_async_copy(s, d, out_s.at[i]) for i, (s, d) in enumerate(stores)]
    AT, OT, BT, QKV, H, MT, SL, WIN, WOUT, WGU = 0, 1, 2, 3, 4, 5, 7, 9, 10, 11
    g.barrier()
    key_bias(bias_ref, lengths[slot[0]])

    def weight_in(t, part=0):
        if part == 0:
            loads[t].wait()
        if t == 0:
            for p in (0,) if part == 0 else (1, 2):
                lin[:, 1024 * p:1024 * p + 1024] = win[p].astype(BF16)
        elif t == 1:
            lout[...] = wout[...].astype(BF16)
        elif t == 3:
            ldn[...] = wdn[...].astype(BF16)
        else:
            tiles = lgu.shape[1] // 128
            for c in range(part * tiles // 2, (part + 1) * tiles // 2):
                lgu[:, 128 * c:128 * c + 128] = wgu[pl.ds(c, lgu.shape[0], stride=tiles), :].astype(BF16)
        if t in (1, 3) or part == 1:
            g.own(t).start()

    def ln_one(first, last):
        for r in range(first, last, 128):
            n, _ = normed(x_ref[r:r + 128, :].astype(F32))
            a[r:r + 128, :] = n.astype(BF16)

    def transpose_a():
        for c in range(0, 1024, 128):
            at[c:c + 128, :] = a[:, c:c + 128].T
        outs[AT].start()

    def project(p, j):
        c = 1024 * p + 256 * j
        w = dot(a[...], bin_[:, c:c + 256])
        for i in (0, 128):
            t = w[:, i:i + 128]
            if p < 2:
                t = t * cos_ref[...] + turn(t) * sin_ref[...]
            qkv[:, c + i:c + i + 128] = t.astype(BF16)

    def attend(pair):
        for qt in range(rows // 128):
            width = 128 * (qt + 1)
            lo = pl.multiple_of(pair * 128, 128)
            q2 = two_heads(qkv[128 * qt:width, pl.ds(lo, 128)])
            p = probabilities(q2, qkv[:width, pl.ds(pl.multiple_of(1024 + lo, 128), 128)], bias_ref[:, :width])
            mixed = join_heads(dot(p.astype(BF16), qkv[:width, pl.ds(pl.multiple_of(2048 + lo, 128), 128)]))
            o[128 * qt:width, pl.ds(lo, 128)] = mixed.astype(BF16)
        ot[pl.ds(lo, 128), :] = o[:, pl.ds(lo, 128)].T

    def out_and_norm():
        for r in range(0, rows, 256):
            v = x_ref[r:r + 256, :].astype(F32) + dot(o[r:r + 256, :], bout[...])
            h[r:r + 256, :] = v
            n, _ = normed(v)
            b[r:r + 256, :] = n.astype(BF16)
        outs[H].start()
        for c in range(0, 1024, 128):
            bt[c:c + 128, :] = b[:, c:c + 128].T
        outs[BT].start()

    def gate(ct):
        lo = pl.multiple_of(ct * 256, 256)
        w = dot(b[...], bgu[:, pl.ds(lo, 256)])
        gv, uv = w[:, :128], w[:, 128:]
        sig = jax.nn.sigmoid(gv)
        silu = gv * sig
        mt[pl.ds(pl.multiple_of(ct * 128, 128), 128), :] = (silu * uv).astype(BF16).T
        slopes[:, pl.ds(lo, 128)] = (uv * sig * (1.0 + gv * (1.0 - sig))).astype(BF16)
        slopes[:, pl.ds(pl.multiple_of(lo + 128, 128), 128)] = silu.astype(BF16)

    Q, KV, O, G1, G2, D1, D2 = range(7)
    tiles = half // 256
    weight_in(0)
    g.s0(Q)
    for cp in loads[1:]:
        cp.start()
    weight_in(0, 1)
    g.s0(KV)
    ln_one(0, rows // 2)
    g.s1(Q, 1)
    ln_one(rows // 2, rows)
    g.s1(Q, 2)
    weight_in(1)
    g.s0(O)
    g.s1(KV, 1)
    g.s1(Q, 3)
    transpose_a()
    g.s2(Q)
    g.s1(KV, 2)
    weight_in(2, 0)
    g.s0(G1)
    g.s1(O, 1)
    g.s1(KV, 3)
    g.s3(Q)
    weight_in(2, 1)
    g.s0(G2)
    g.s1(O, 2)
    g.s2(KV)
    g.s1(O, 3)
    weight_in(3)
    g.s0(D1)
    g.s0(D2)
    g.s1(G1, 1)
    g.s4(Q)
    g.own(0).wait()
    g.s2(O)
    g.s1(G1, 2)
    between = {
        (0, 1): lambda: g.s3(KV), (0, 3): lambda: (g.s1(G1, 3), g.s1(G2, 1)),
        (1, 1): lambda: g.s3(O), (1, 3): lambda: g.s1(G2, 2), (2, 1): lambda: (g.s2(G1), g.s1(G2, 3)), (2, 3): lambda: g.s1(D1, 1),
    }
    for p in range(3):
        if p == 1:
            g.s4(KV)
            outs[WIN].start()
        for j in range(4):
            project(p, j)
            if (p, j) in between:
                between[p, j]()
    outs[QKV].start()
    g.s4(O)
    g.own(1).wait()
    outs[WOUT].start()
    steps = {1: lambda: g.s1(D1, 2), 3: lambda: g.s3(G1), 5: lambda: g.s1(D1, 3)}
    for i in range(8):
        attend(jnp.int32(i))
        if i in steps:
            steps[i]()
    outs[OT].start()
    out_and_norm()
    g.own(2).wait()
    g.s4(G1)
    outs[WGU].start()

    def gates(first, last):
        lax.fori_loop(first, last, lambda k, _: (gate(k), 0)[1], 0)

    third = tiles // 3
    gates(0, third)
    g.s1(D2, 1)
    gates(third, 2 * third)
    g.s2(G2)
    gates(2 * third, tiles)
    outs[MT].start()
    outs[SL].start()
    g.s1(D2, 2)
    g.s2(D1)
    g.s3(G2)
    g.s1(D2, 3)
    g.s4(G2)
    outs[WGU + 1].start()
    gates(tiles, tiles + third)
    g.s3(D1)
    gates(tiles + third, 2 * tiles)
    outs[MT + 1].start()
    outs[SL + 1].start()
    g.s4(D1)
    g.s4(D2)
    g.own(3).wait()
    for c in range(len(chunks)):
        g.drain(c)
    for cp in outs:
        cp.wait()


def forward_call(x, cos, sin, lengths, slot, win, wout, wgu, wdn):
    rows, d = x.shape
    r = wout.shape[0]
    ff2 = wgu.shape[0] * 128 // r
    ff = ff2 // 2
    shapes = ((r, 3 * d), (r, d), (r, ff2), wdn.shape)
    part = wdn.shape[0] // 2
    chunks = ((0, 0, r, 0, d, 1), (0, 0, r, d, 2 * d, 1), (1, 0, r, 0, d, 1), (2, 0, r, 0, ff, 0), (2, 0, r, ff, ff, 0), (3, 0, part, 0, d, 1), (3, part, part, 0, d, None))
    vm, an, sm = (pl.BlockSpec(memory_space=m) for m in (pltpu.VMEM, pl.ANY, pltpu.SMEM))
    sd = lambda s, t=BF16: jax.ShapeDtypeStruct(s, t)
    v = lambda s, t=BF16: pltpu.VMEM(s, t)
    outs = [sd((8 * s[0], s[1])) for s in shapes] + [sd((d, rows)), sd((d, rows)), sd((d, rows)), sd((ff, rows)), sd((rows, 3 * d)), sd((rows, ff2)), sd((rows, d), F32)]
    scratch = [v(win.shape, F32), v(wout.shape, F32), v(wgu.shape, F32), v(wdn.shape, F32)] + [v(s) for s in shapes]
    scratch += [v((8 * r, 3 * d)), v((8 * r, d)), v((8 * r, ff2))]
    scratch += [v((rows, d)), v((d, rows)), v((rows, 3 * d)), v((rows, d)), v((d, rows)), v((rows, d), F32), v((rows, d)), v((d, rows)), v((ff, rows)), v((rows, ff2)), v((1, rows), F32)]
    scratch += [DMA((4,)), DMA((13,))] + Gather.scratch(4, len(chunks))
    return pl.pallas_call(
        functools.partial(forward_kernel, shapes, chunks),
        out_shape=outs, in_specs=[vm] * 3 + [sm] * 2 + [an] * 4, out_specs=[an] * len(outs), scratch_shapes=scratch,
        compiler_params=pltpu.CompilerParams(collective_id=0, has_side_effects=True, vmem_limit_bytes=60 << 20),
    )(x, cos, sin, lengths, slot, win, wout, wgu, wdn)


class Reduce:
    def __init__(self, refs):
        (self.mine, self.theirs, self.held, self.sums, self.one, self.two, self.fin, self.planes, self.far, self.keep, self.ours, self.total,
         self.a_s, self.a_r, self.o_s, self.o_r, self.t_s, self.t_r, self.c_s, self.c_r, self.d_s, self.d_r, self.f_s, self.f_r, self.g_s, self.g_r) = refs
        self.rep, self.shard = lax.axis_index("rep"), lax.axis_index("shard")
        self.core = lax.rem(self.shard, 2)
        self.x, self.y = lax.rem(self.rep, 2), self.rep // 2
        self.sib = (self.rep, self.shard + 1 - 2 * self.core)
        self.nb = ((self.rep + 1 - 2 * self.x, self.shard), (self.rep + 2 - 4 * self.y, self.shard))

    @staticmethod
    def scratch(chunks, wide):
        v = lambda *s: pltpu.VMEM(s, BF16)
        return [
            v(RING, 8, 16, wide),
            v(RING, 8, 16, wide),
            pltpu.VMEM((2, 8, 16, wide), F32),
            v(RING_SUMS, 8, 16, wide),
            v(2, RING_ONE, 2, 16, wide),
            v(2, RING_TWO, 16, wide),
            v(RING, 2, 16, wide),
            v(chunks, 3, 2, 16, wide - FAR),
            v(chunks - 1, 3, 8, 16, FAR),
            pltpu.VMEM((8, 16, FAR), F32),
            pltpu.VMEM((2, 2, 16, wide), F32),
        ], [DMA((RING,)), DMA((RING,)), DMA((2, RING_ONE)), DMA((2, RING_ONE)), DMA((2, RING_TWO)), DMA((2, RING_TWO)), DMA((RING,)), DMA((chunks, 3)),
            DMA((chunks, 2)), DMA((chunks, 2)), DMA((chunks, 2)), DMA((chunks, 2)), DMA((RING_SUMS,)), DMA((chunks - 1, 3))]

    def copy(self, src, dst, s, r, dev):
        return pltpu.make_async_remote_copy(src_ref=src, dst_ref=dst, send_sem=s, recv_sem=r, device_id=dev, device_id_type=MESH)

    def barrier(self):
        bar = pltpu.get_barrier_semaphore()
        for dev in (self.sib,) + self.nb + tuple((self.rep, lax.rem(self.shard + 2 * d, 8)) for d in (1, 2, 3)):
            pl.semaphore_signal(bar, inc=1, device_id=dev, device_id_type=MESH)
        pl.semaphore_wait(bar, 6)

    def first(self, u, w):
        s = lax.rem(u, RING)
        return self.copy(self.mine.at[s, :, :, pl.ds(0, w)], self.theirs.at[s, :, :, pl.ds(0, w)], self.a_s.at[s], self.a_r.at[s], self.sib)

    def hop_one(self, u, w, k):
        m, s = lax.rem(u, RING_SUMS), lax.rem(u, RING_ONE)
        at = 2 - 2 * self.x if k == 0 else 6 - 2 * self.y
        return self.copy(self.sums.at[m, pl.ds(at, 2), :, pl.ds(0, w)], self.one.at[k, s, :, :, pl.ds(0, w)], self.o_s.at[k, s], self.o_r.at[k, s], self.nb[k])

    def hop_two(self, u, w, k):
        m, s = lax.rem(u, RING_SUMS), lax.rem(u, RING_TWO)
        at = 2 * self.x + 1 - self.y if k == 0 else 4 + 2 * self.y + 1 - self.x
        return self.copy(self.sums.at[m, at, :, pl.ds(0, w)], self.two.at[k, s, :, pl.ds(0, w)], self.t_s.at[k, s], self.t_r.at[k, s], self.nb[1 - k])

    def across(self, u, w, dz):
        s = lax.rem(u, RING)
        c = u // 4
        return self.copy(self.fin.at[s, :, :, pl.ds(0, w)], self.planes.at[c, 3 - dz, :, :, pl.ds(0, w)], self.c_s.at[s], self.c_r.at[c, 3 - dz], (self.rep, lax.rem(self.shard + 2 * dz, 8)))

    def plane_in(self, c, w, j):
        return self.copy(self.fin.at[0, :, :, pl.ds(0, w)], self.planes.at[c, j, :, :, pl.ds(0, w)], self.c_s.at[0], self.c_r.at[c, j], self.sib)

    def spread(self, c, w, k, own=True):
        q = self.rep if own else self.nb[k][0]
        ref = self.total.at[c, q, :, :, pl.ds(0, w)]
        return self.copy(ref, ref, self.d_s.at[c, k], self.d_r.at[c, k], self.nb[k])

    def spread_on(self, c, w, k, own=True):
        q = self.nb[k][0] if own else self.nb[0][0] + self.nb[1][0] - self.rep
        ref = self.total.at[c, q, k, :, pl.ds(0, w)]
        return self.copy(ref, ref, self.f_s.at[c, k], self.f_r.at[c, k], self.nb[1 - k])

    def away(self, u, n, dz):
        m = lax.rem(u, RING_SUMS)
        return self.copy(self.sums.at[m, :, :, pl.ds(n, FAR)], self.far.at[u // 4, 3 - dz], self.g_s.at[m], self.g_r.at[u // 4, 3 - dz], (self.rep, lax.rem(self.shard + 2 * dz, 8)))

    def away_in(self, c, j):
        return self.copy(self.far.at[c, j], self.far.at[c, j], self.g_s.at[0], self.g_r.at[c, j], self.sib)

    @staticmethod
    def offset(u):
        return lax.rem(lax.rem(u, 4) + 1, 4)

    def stage_two(self, u, w, more):
        n, o = w
        s, m, dz = lax.rem(u, RING), lax.rem(u, RING_SUMS), self.offset(u)
        self.first(u, o if more else n).wait()
        held = self.held.at[lax.rem(u, 2)]
        self.sums[m, :, :, :n] = (held[:, :, :n] + self.theirs[s, :, :, :n].astype(F32)).astype(BF16)

        @pl.when(dz > 0)
        def _():
            for k in (0, 1):
                self.hop_one(u, n, k).start()
            if more:
                self.sums[m, :, :, n:o] = (held[:, :, n:o] + self.theirs[s, :, :, n:o].astype(F32)).astype(BF16)
                self.away(u, n, dz).start()

        @pl.when(dz == 0)
        def _():
            c = u // 4

            @pl.when(c > 0)
            def _():
                out = self.keep[...]
                for j in range(3):
                    self.away_in(c - 1, j).wait_recv()
                    out = out + self.far[c - 1, j].astype(F32)
                self.sums[m, :, :, n:o] = out.astype(BF16)

            @pl.when(c == 0)
            def _():
                self.sums[m, :, :, n:o] = jnp.zeros((8, 16, FAR), BF16)

            if more:
                self.keep[...] = held[:, :, n:o] + self.theirs[s, :, :, n:o].astype(F32)
            for k in (0, 1):
                self.hop_one(u, o, k).start()

    def stage_three(self, u, w):
        m, s = lax.rem(u, RING_SUMS), lax.rem(u, RING_ONE)

        def run(n):
            for k in (0, 1):
                self.hop_one(u, n, k).wait()
                at = 2 * self.x if k == 0 else 4 + 2 * self.y
                new = self.sums[m, pl.ds(at, 2), :, :n].astype(F32) + self.one[k, s, :, :, :n].astype(F32)
                self.sums[m, pl.ds(at, 2), :, :n] = new.astype(BF16)
                self.hop_two(u, n, k).start()

        pl.when(self.offset(u) > 0)(lambda: run(w[0]))
        pl.when(self.offset(u) == 0)(lambda: run(w[1]))

    def stage_four(self, u, w, start, more):
        s, m, t = lax.rem(u, RING), lax.rem(u, RING_SUMS), lax.rem(u, RING_TWO)
        n, o = w
        dz = self.offset(u)

        def plane_sum(k, n):
            self.hop_two(u, n, k).wait()
            at = 2 * self.x + self.y if k == 0 else 4 + 2 * self.y + self.x
            return self.sums[m, at, :, :n].astype(F32) + self.two[k, t, :, :n].astype(F32)

        @pl.when(dz > 0)
        def _():
            @pl.when(u >= start + RING)
            def _():
                self.across(u - RING, n, dz).wait_send()

            for k in (0, 1):
                self.fin[s, k, :, :n] = plane_sum(k, n).astype(BF16)
            self.across(u, n, dz).start()
            if more:
                self.away(u, n, dz).wait_send()

        @pl.when(dz == 0)
        def _():
            for k in (0, 1):
                self.ours[lax.rem(u // 4, 2), k, :, :o] = plane_sum(k, o)

    def stage_sum(self, u, w):
        n, o = w

        @pl.when(self.offset(u) == 0)
        def _():
            c = u // 4
            for j in range(3):
                self.plane_in(c, n, j).wait_recv()
            for k in (0, 1):
                ours = self.ours.at[lax.rem(c, 2), k]
                out = ours[:, :n]
                for j in range(3):
                    out = out + self.planes[c, j, k, :, :n].astype(F32)
                self.total[c, self.rep, k, :, :n] = out.astype(BF16)
                self.total[c, self.rep, k, :, n:o] = ours[:, n:o].astype(BF16)
            for k in (0, 1):
                self.spread(c, o, k).start()

    def stage_on(self, u, w):
        @pl.when(self.offset(u) == 0)
        def _():
            for k in (0, 1):
                self.spread(u // 4, w[1], k, False).wait_recv()
                self.spread_on(u // 4, w[1], k).start()

    def drain_across(self, units, w):
        for u in range(units - RING, units):
            if u % 4 != 3:
                self.across(u, w[0], u % 4 + 1).wait_send()

    def finish(self, units, width):
        self.drain_across(units, width(units - 1))
        for c in range(units // 4):
            w = width(4 * c)[1]
            for k in (0, 1):
                self.spread(c, w, k).wait_send()
                self.spread_on(c, w, k).wait_send()
                self.spread_on(c, w, k, False).wait_recv()


def norm_back_rows(v, d):
    n, inv = normed(v)
    return inv * (d - jnp.mean(d, axis=-1, keepdims=True) - n * jnp.mean(d * n, axis=-1, keepdims=True))


def backward_kernel(
    wide,
    x_ref, cot_ref, cos_ref, sin_ref, lengths, slot, at_h, ot_h, bt_h, mt_h, qkv_h, slopes_h, h_h, fin_h, fout_h, fgu_h, fdn_h,
    total, out_h, grad_h,
    atl, bt, mt, qkv, dgu, h, wd, wb, wo, atr, do, acc, dh, dk, dv, dy, bias_ref, ld_s, wb_s, st_s, *rs,
):
    r = Reduce(rs[:11] + (total,) + rs[11:])
    rows, d = x_ref.shape
    bounds = ((0, 8, 0), (8, 24, 1), (24, 40, 2))
    units = 40
    names = ("mt", "wd", "gu", "bt", "qkv", "h", "wo", "ot", "at")
    pairs = ((mt_h, mt), (fdn_h, wd), (slopes_h, dgu), (bt_h, bt), (qkv_h, qkv), (h_h, h), (fout_h, wo),
             (ot_h, atl.at[pl.ds(d, d), :]), (at_h, atl.at[pl.ds(0, d), :]))
    loads = {n: pltpu.make_async_copy(s, t, ld_s.at[i]) for i, (n, (s, t)) in enumerate(zip(names, pairs))}
    for n in names[:3]:
        loads[n].start()

    def weights(j):
        src = fgu_h.at[:, pl.ds(wide * j, wide)] if j < 4 else fin_h.at[:, pl.ds(d * (j - 4), d)]
        dst = wb.at[j % 2] if j < 4 else wb.at[j % 2, :, pl.ds(0, d)]
        return pltpu.make_async_copy(src, dst, wb_s.at[j % 2])

    def width(u):
        if u >= units - 4:
            return (d, d + FAR, d)
        w = wide if u < 24 else d
        return (w - FAR, w, w)

    def start_of(w):
        return next(u for u in range(units) if width(u) == w)

    def product(u, kind, first, own):
        c = u // 4 - first // 4
        zt = lax.rem(r.shard // 2 + lax.rem(u, 4) + 1, 4)
        core = r.core if own else 1 - r.core

        def put(e, lo, n, val):
            if own:
                r.held[lax.rem(u, 2), e, :, lo:lo + n] = val
            else:
                r.mine[lax.rem(u, RING), e, :, lo:lo + n] = val.astype(BF16)

        if kind == 0:
            part = mt.shape[0] // 16
            left = mt[pl.ds(pl.multiple_of((2 * zt + core) * 2 * part + c * part, 16), part), :]
            for e in range(0, 8, 2):
                val = dot(left, dy[:, e * 128:e * 128 + 256])
                for i in (0, 1):
                    for j in range(part // 16):
                        put(e + i, 128 * j, 128, val[16 * j:16 * j + 16, i * 128:i * 128 + 128])
            return
        base = (2 * zt + core) * 128
        if kind == 1:
            left = bt[pl.ds(pl.multiple_of(base, 128), 128), :]
            right, n = dgu[:, pl.ds(pl.multiple_of(c * wide, 128), wide)], wide
        else:
            left = atl[pl.ds(pl.multiple_of(base + jnp.where(c == 0, d, 0), 128), 128), :]
            right, n = atr[:, pl.ds(pl.multiple_of(c * d, 128), d)], d
        put(slice(None), 0, n, dot(left, right).reshape(8, 16, n))

    def tail(u, ws):
        for lag, stage in ((LAG_TWO, r.stage_two), (LAG_THREE, r.stage_three), (LAG_FOUR, r.stage_four), (LAG_SUM, r.stage_sum), (LAG_ON, r.stage_on)):
            w = ws[lag]
            if not w:
                continue
            more = () if lag not in (LAG_TWO, LAG_FOUR) else (w[0] < w[2],)
            start = (start_of(w),) if lag == LAG_FOUR else ()
            stage(u - lag, w[:2], *start, *more)

    def drain(u, ws):
        v = u - LAG_FOUR
        if ws[LAG_FOUR] and v == start_of(ws[LAG_FOUR]) and v > 0:
            r.drain_across(v, width(v - 1))

    def widths(u):
        return [width(u - k) if 0 <= u - k < units else None for k in range(LAG_ON + 1)]

    def step(u, kind, first, ws):
        product(u, kind, first, False)
        r.first(u, ws[0][2]).start()
        product(u, kind, first, True)
        tail(u, ws)

    def hidden(t):
        val = dot(dy[...], wd[pl.ds(pl.multiple_of(256 * t, 256), 256), :], 1, 1)
        for i in (0, 1):
            part = val[:, 128 * i:128 * i + 128]
            for j in (0, 1):
                at = pl.ds(pl.multiple_of(512 * t + 256 * i + 128 * j, 128), 128)
                dgu[:, at] = (part * dgu[:, at].astype(F32)).astype(BF16)

    def hidden_unit(u):
        hidden(u)
        tiles = mt.shape[0] // 256

        @pl.when(u + 8 < tiles)
        def _():
            hidden(u + 8)

    def input_two(j):
        weights(j).wait()
        val = dot(dgu[:, wide * j:wide * j + wide], wb[j % 2], 1, 1)
        acc[...] = val if j == 0 else acc[...] + val
        weights(j + 2).start()

    def norm_two(part):
        if part == 0:
            loads["h"].wait()
        for i in range(part * rows // 2, (part + 1) * rows // 2, 128):
            s = slice(i, i + 128)
            v = dy[s, :].astype(F32) + norm_back_rows(h[s, :], acc[s, :])
            dh[s, :] = v
            atr[s, :d] = v.astype(BF16)

    def mixed_grad():
        loads["wo"].wait()
        loads["qkv"].wait()
        do[...] = dot(atr[:, :d], wo[...], 1, 1).astype(BF16)

    def turn_back(t, s):
        return t * cos_ref[s, :] - turn(t) * sin_ref[s, :]

    def attend_tile(lanes, qt):
        n = 128 * (qt + 1)
        s = slice(128 * qt, n)
        keys = qkv[:n, lanes[1]]
        q2, g2 = two_heads(qkv[s, lanes[0]]), two_heads(do[s, lanes[0]])
        p = probabilities(q2, keys, bias_ref[:, :n])
        dp = dot(g2, qkv[:n, lanes[2]], 1, 1)
        ds = (p * (dp - jnp.sum(p * dp, axis=-1, keepdims=True)) * 0.125).astype(BF16)
        new_v, new_k = dot(p.astype(BF16), g2, 0, 0), dot(ds, q2, 0, 0)
        if n == rows:
            dv[...] = new_v
            dk[...] = new_k
        else:
            dv[:n, :] = dv[:n, :] + new_v
            dk[:n, :] = dk[:n, :] + new_k
        atr[s, lanes[1]] = turn_back(join_heads(dot(ds, keys)), s).astype(BF16)

    def attend_half(k):
        lo = pl.multiple_of(k // 2 * 128, 128)
        lanes = [pl.ds(pl.multiple_of(lo + d * i, 128), 128) for i in range(4)]
        tiles = rows // 128

        @pl.when(lax.rem(k, 2) == 0)
        def _():
            for qt in (tiles - 1, 0):
                attend_tile(lanes, qt)

        @pl.when(lax.rem(k, 2) == 1)
        def _():
            for qt in range(1, tiles - 1):
                attend_tile(lanes, qt)
            atr[:, lanes[2]] = turn_back(dk[...], slice(0, rows)).astype(BF16)
            atr[:, lanes[3]] = dv[...].astype(BF16)

    def input_one(j):
        weights(4 + j).wait()
        val = dot(atr[:, d * (j + 1):d * (j + 2)], wb[j % 2, :, :d], 1, 1)
        acc[...] = val if j == 0 else acc[...] + val
        if j == 0:
            weights(6).start()

    grad_out = pltpu.make_async_copy(dh, grad_h, st_s.at[0])
    result_out = pltpu.make_async_copy(do, out_h, st_s.at[1])

    def norm_one():
        for i in range(0, rows, 128):
            s = slice(i, i + 128)
            dh[s, :] = dh[s, :] + norm_back_rows(x_ref[s, :].astype(F32), acc[s, :])
        grad_out.start()

    def result(i):
        s = slice(256 * i, 256 * i + 256)
        do[s, :] = jnp.where(alive(256 * i, 256), h[s, :] + dot(mt[:, s], wd[...], 0, 0), 0.0).astype(BF16)

    before = {0: lambda: loads["mt"].wait(), 8: lambda: loads["bt"].wait(), 24: lambda: loads["ot"].wait(), 28: lambda: loads["at"].wait()}
    fill = {8 + j: functools.partial(input_two, j) for j in range(4)}
    fill[11] = lambda: (input_two(3), norm_two(0))
    fill[12] = lambda: (norm_two(1), mixed_grad())
    fill[27] = lambda: attend_half(jnp.int32(15))
    fill.update({29 + 2 * j: functools.partial(input_one, j) for j in range(3)})
    fill[35] = norm_one
    fill[36] = lambda: result(0)
    fill[37] = lambda: (result(1), result_out.start())
    fill[0] = lambda: [loads[n].start() for n in names[3:]] + [weights(j).start() for j in (0, 1)]
    fill[1] = lambda: (loads["wd"].wait(), loads["gu"].wait(), hidden_unit(jnp.int32(0)))
    fill[7] = lambda: hidden_unit(jnp.int32(7))
    ranged = [(2, 8, lambda u: hidden_unit(u - 1)), (13, 28, lambda u: attend_half(u - 13))]

    length = lengths[slot[0]]

    def alive(first, n):
        return lax.broadcasted_iota(jnp.int32, (n, d), 0) + first < length

    for i in range(0, rows, 128):
        s = slice(i, i + 128)
        dy[s, :] = jnp.where(alive(i, 128), cot_ref[s, :].astype(F32), 0.0).astype(BF16)
    key_bias(bias_ref, length)
    r.barrier()
    edges = sorted({a for a, _, _ in bounds} | {e for a, b, _ in ranged for e in (a, b)} | {units, units - 4} | set(before))
    u = 0
    while u < units:
        if u in before:
            before[u]()
        ws = widths(u)
        first, _, kind = next(b for b in bounds if b[0] <= u < b[1])
        w = width(u)
        in_range = next((f for a, b, f in ranged if a <= u < b), None)
        end = min(e for e in edges if e > u)
        plain = all(x == w for x in ws) and u not in fill
        stop = u
        while plain and stop < end and stop not in fill:
            stop += 1
        if plain and stop - u > 1:
            def body(i, _, kind=kind, first=first, ws=ws, f=in_range):
                step(i, kind, first, ws)
                if f:
                    f(i)
                return 0
            lax.fori_loop(u, stop, body, 0)
            u = stop
            continue
        drain(u, ws)
        step(jnp.int32(u), kind, first, ws)
        if in_range:
            in_range(jnp.int32(u))
        if u in fill:
            fill[u]()
        u += 1
    for u in range(units, units + LAG_ON + 1):
        drain(u, widths(u))
        tail(jnp.int32(u), widths(u))
    r.finish(units, width)
    grad_out.wait()
    result_out.wait()


def backward_call(x, cot, cos, sin, lengths, slot, saved, full):
    rows, d = x.shape
    ff = saved[3].shape[0]
    wide = 2 * ff // 4
    chunks = 10
    vm, an, sm = (pl.BlockSpec(memory_space=m) for m in (pltpu.VMEM, pl.ANY, pltpu.SMEM))
    v = lambda s, t=BF16: pltpu.VMEM(s, t)
    bufs, sems = Reduce.scratch(chunks, wide)
    scratch = [v((2 * d, rows)), v((d, rows)), v((ff, rows)), v((rows, 3 * d)), v((rows, 2 * ff)), v((rows, d), F32), v((ff, d)), v((2, d, wide)), v((d, d)),
               v((rows, 4 * d)), v((rows, d)), v((rows, d), F32), v((rows, d), F32), v((rows, 128), F32), v((rows, 128), F32), v((rows, d)), v((1, rows), F32), DMA((9,)), DMA((2,)), DMA((2,))]
    return pl.pallas_call(
        functools.partial(backward_kernel, wide),
        out_shape=[jax.ShapeDtypeStruct((chunks, 4, 2, 16, wide), BF16), jax.ShapeDtypeStruct((rows, d), BF16), jax.ShapeDtypeStruct((rows, d), F32)],
        in_specs=[vm] * 4 + [sm] * 2 + [an] * 11, out_specs=[vm, an, an], scratch_shapes=scratch + bufs + sems,
        compiler_params=pltpu.CompilerParams(collective_id=1, has_side_effects=True, vmem_limit_bytes=63 << 20),
    )(x, cot, cos, sin, lengths, slot, *saved, *full)


def adam_kernel(scalars, first, second, *refs):
    masters, outs, spread = refs[:12], refs[12:28], refs[28]
    first_scale, second_scale, rate = scalars[0], scalars[1], scalars[2]
    wide = first.shape[-1]
    cols = wide // 128
    d = masters[3].shape[1]

    def update(k, at, grad):
        w, m, v = (masters[3 * k + j][at] for j in range(3))
        m = beta_first * m + (1.0 - beta_first) * grad
        v = beta_second * v + (1.0 - beta_second) * grad * grad
        outs[4 * k][at] = grad
        outs[4 * k + 1][at] = w - rate * (m * first_scale / (jnp.sqrt(v * second_scale) + adam_eps) + weight_decay * w)
        outs[4 * k + 2][at] = m
        outs[4 * k + 3][at] = v

    def piece(e, c, lo, n):
        w = (wide if c < 6 else d) - FAR
        if c < 9 and lo >= w:
            lo = lo - w + (wide - FAR if c < 5 else d - FAR if c < 8 else d)
            c += 1
        return (first, second)[e][c, 0, 0, :, lo:lo + n].astype(F32)

    stride = 4 * cols
    half = 16 * cols
    for e in (0, 1):
        own = slice(16 * e, 16 * e + 16)
        for lo, hi in ((0, d - FAR), (d - FAR, d)):
            for p in range(3):
                update(0, (p, own, slice(lo, hi)), piece(e, 7 + p, lo, hi - lo))
            update(1, (own, slice(lo, hi)), piece(e, 6, lo, hi - lo))
        for c in range(4):
            for j in range(cols):
                spread[pl.ds(16 * stride * e + c * cols + j, 16, stride=stride), :] = piece(e, 2 + c, 128 * j, 128)
        for c in (0, 1):
            for j in range(cols):
                at = (slice(c * half + 16 * j, c * half + 16 * j + 16), slice(128 * e, 128 * e + 128))
                update(3, at, piece(e, c, 128 * j, 128))
    for i in range(0, 32 * stride, 176):
        s = (slice(i, i + 176),)
        update(2, s, spread[s])


def adam_call(scalars, total, masters):
    chunks, _, _, _, wide = total.shape
    blocks = []
    for k, shape in enumerate((masters[0].shape, masters[3].shape, masters[6].shape, masters[9].shape)):
        if k == 0:
            blocks.append(pl.BlockSpec((3, shape[1] // 4, shape[2]), lambda i: (0, i, 0)))
        elif k < 3:
            blocks.append(pl.BlockSpec((shape[0] // 4, shape[1]), lambda i: (i, 0)))
        else:
            blocks.append(pl.BlockSpec((shape[0], shape[1] // 4), lambda i: (0, i)))

    def part(e):
        low = lax.rem(e, 2) * 2 + e // 2
        return (0, jnp.where(e < 4, low, e - 4), e // 4, 0, 0)

    shapes = [masters[3 * k].shape for k in range(4) for _ in range(4)]
    return pl.pallas_call(
        adam_kernel,
        grid=(4,),
        out_shape=[jax.ShapeDtypeStruct(s, F32) for s in shapes],
        in_specs=[pl.BlockSpec(memory_space=pltpu.SMEM), pl.BlockSpec((chunks, 1, 1, 16, wide), lambda i: part(2 * i)), pl.BlockSpec((chunks, 1, 1, 16, wide), lambda i: part(2 * i + 1))] + [blocks[k] for k in range(4) for _ in range(3)],
        out_specs=[blocks[k] for k in range(4) for _ in range(4)],
        scratch_shapes=[pltpu.VMEM((masters[6].shape[0] // 4, 128), F32)],
        compiler_params=pltpu.CompilerParams(vmem_limit_bytes=60 << 20),
    )(scalars, total, total, *masters)


def gather_full(local, rep_count, rep_index):
    rows = local.shape[0]
    flat = local.reshape(rows, -1)
    width = flat.shape[1] // rep_count
    piece = lax.dynamic_slice_in_dim(flat, rep_index * width, width, axis=1)
    column = lax.all_gather(piece, "shard", axis=0, tiled=True)
    return lax.all_gather(column, "rep", axis=0, tiled=False)


def reduce_full(partial):
    part = lax.psum_scatter(partial, "rep", scatter_dimension=0, tiled=False)
    part = lax.psum_scatter(part, "shard", scatter_dimension=0, tiled=True)
    pieces = lax.all_gather(part, "rep", axis=0, tiled=False)
    rows = pieces.shape[1]
    return jnp.transpose(pieces, (1, 0, 2)).reshape(rows, -1).astype(jnp.float32)


def shards_generic(
    tokens,
    cotangent,
    lengths,
    slot_sequence,
    step_count,
    learn_rate,
    attention_in,
    attention_in_first,
    attention_in_second,
    attention_out,
    attention_out_first,
    attention_out_second,
    gate_up_weight,
    gate_up_first,
    gate_up_second,
    down_weight,
    down_first,
    down_second,
):
    slot_count, position_count, feature_count = tokens.shape
    row_total = slot_count * position_count
    head_count = feature_count // HD
    shaped = (slot_count, position_count, head_count, HD)
    inputs = tokens.astype(jnp.float32).reshape(row_total, feature_count)
    matches = jnp.arange(lengths.shape[0])[None, :] == slot_sequence[:, None]
    slot_length = jnp.sum(jnp.where(matches, lengths[None, :], 0), axis=1)
    alive_rows = (
        (jnp.arange(position_count)[None, :] < slot_length[:, None])
        .astype(jnp.float32)
        .reshape(row_total, 1)
    )
    cosine_table, sine_table = rope_tables(position_count, HD)
    in_local = attention_in.astype(jnp.bfloat16)
    out_local = attention_out.astype(jnp.bfloat16)
    gate_up_local = gate_up_weight.astype(jnp.bfloat16)
    down_local = down_weight.astype(jnp.bfloat16)
    rep_count = lax.axis_size("rep")
    rep_index = lax.axis_index("rep")
    in_full = gather_full(in_local, rep_count, rep_index)
    out_full = gather_full(out_local, rep_count, rep_index)
    gate_up_full = gather_full(gate_up_local, rep_count, rep_index)
    down_full = gather_full(down_local, rep_count, rep_index)
    normed_one, inverse_one = layer_norm(inputs)
    first_input = normed_one.astype(jnp.bfloat16)
    projected = jnp.einsum(
        "rd,qde->rqe", first_input, in_full, preferred_element_type=jnp.float32
    ).reshape(row_total, 3, feature_count)
    queries = rotate(projected[:, 0].reshape(shaped), cosine_table, sine_table).astype(jnp.bfloat16)
    rotated_keys = rotate(projected[:, 1].reshape(shaped), cosine_table, sine_table).astype(
        jnp.bfloat16
    )
    values_low = projected[:, 2].reshape(shaped).astype(jnp.bfloat16)
    mixed_heads, log_total = lax.map(
        attend_forward, (queries, rotated_keys, values_low, slot_length)
    )
    mixed_low = mixed_heads.reshape(row_total, feature_count).astype(jnp.bfloat16)
    residual = inputs + jnp.einsum(
        "rd,qde->rqe", mixed_low, out_full, preferred_element_type=jnp.float32
    ).reshape(row_total, feature_count)
    normed_two, inverse_two = layer_norm(residual)
    second_input = normed_two.astype(jnp.bfloat16)
    gate_up = jnp.einsum(
        "rd,qdf->rqf", second_input, gate_up_full, preferred_element_type=jnp.float32
    ).reshape(row_total, 2, -1)
    gate_value = gate_up[:, 0]
    up_value = gate_up[:, 1]
    sigmoid_gate = jax.nn.sigmoid(gate_value)
    hidden_low = (gate_value * sigmoid_gate * up_value).astype(jnp.bfloat16)
    result = residual + jnp.einsum(
        "rf,qfe->rqe", hidden_low, down_full, preferred_element_type=jnp.float32
    ).reshape(row_total, feature_count)
    output = (result * alive_rows).astype(jnp.bfloat16).reshape(tokens.shape)
    output_grad = cotangent.astype(jnp.float32).reshape(row_total, feature_count) * alive_rows
    result_grad_low = output_grad.astype(jnp.bfloat16)
    hidden_grad = jnp.einsum(
        "rqe,qfe->rf",
        result_grad_low.reshape(row_total, rep_count, -1),
        down_full,
        preferred_element_type=jnp.float32,
    )
    gate_grad = hidden_grad * up_value * sigmoid_gate * (1.0 + gate_value * (1.0 - sigmoid_gate))
    up_grad = hidden_grad * gate_value * sigmoid_gate
    gate_up_grad_low = (
        jnp.concatenate([gate_grad, up_grad], axis=1)
        .astype(jnp.bfloat16)
        .reshape(row_total, rep_count, -1)
    )
    second_input_grad = jnp.einsum(
        "rqf,qdf->rd", gate_up_grad_low, gate_up_full, preferred_element_type=jnp.float32
    )
    residual_grad = output_grad + norm_back(normed_two, inverse_two, second_input_grad)
    down_part = reduce_full(
        jnp.einsum(
            "rc,rqe->qce",
            hidden_low,
            result_grad_low.reshape(row_total, rep_count, -1),
            preferred_element_type=jnp.float32,
        ).astype(jnp.bfloat16)
    )
    gate_up_part = reduce_full(
        jnp.einsum(
            "rc,rqf->qcf", second_input, gate_up_grad_low, preferred_element_type=jnp.float32
        ).astype(jnp.bfloat16)
    ).reshape(gate_up_weight.shape)
    branch_grad = residual_grad.astype(jnp.bfloat16)
    mixed_grad = (
        jnp.einsum(
            "rqe,qde->rd",
            branch_grad.reshape(row_total, rep_count, -1),
            out_full,
            preferred_element_type=jnp.float32,
        )
        .astype(jnp.bfloat16)
        .reshape(shaped)
    )
    query_grad, key_grad, value_grad = lax.map(
        attend_backward, (queries, rotated_keys, values_low, slot_length, log_total, mixed_grad)
    )
    query_back = rotate(query_grad, cosine_table, -sine_table).reshape(row_total, feature_count)
    key_back = rotate(key_grad, cosine_table, -sine_table).reshape(row_total, feature_count)
    projected_grad = (
        jnp.concatenate([query_back, key_back, value_grad.reshape(row_total, feature_count)], axis=1)
        .astype(jnp.bfloat16)
        .reshape(row_total, rep_count, -1)
    )
    first_input_grad = jnp.einsum(
        "rqe,qde->rd", projected_grad, in_full, preferred_element_type=jnp.float32
    )
    input_grad = (residual_grad + norm_back(normed_one, inverse_one, first_input_grad)).reshape(
        tokens.shape
    )
    in_part = reduce_full(
        jnp.einsum(
            "rc,rqe->qce", first_input, projected_grad, preferred_element_type=jnp.float32
        ).astype(jnp.bfloat16)
    ).reshape(attention_in.shape)
    out_part = reduce_full(
        jnp.einsum(
            "rc,rqe->qce",
            mixed_low,
            branch_grad.reshape(row_total, rep_count, -1),
            preferred_element_type=jnp.float32,
        ).astype(jnp.bfloat16)
    )
    in_grad, in_new, in_first, in_second = adam_update(
        attention_in,
        attention_in_first,
        attention_in_second,
        in_part,
        step_count,
        learn_rate,
    )
    out_grad, out_new, out_first, out_second = adam_update(
        attention_out,
        attention_out_first,
        attention_out_second,
        out_part,
        step_count,
        learn_rate,
    )
    gu_grad, gu_new, gu_first, gu_second = adam_update(
        gate_up_weight, gate_up_first, gate_up_second, gate_up_part, step_count, learn_rate
    )
    dn_grad, dn_new, dn_first, dn_second = adam_update(
        down_weight, down_first, down_second, down_part, step_count, learn_rate
    )
    return (
        output,
        input_grad,
        in_grad,
        in_new,
        in_first,
        in_second,
        out_grad,
        out_new,
        out_first,
        out_second,
        gu_grad,
        gu_new,
        gu_first,
        gu_second,
        dn_grad,
        dn_new,
        dn_first,
        dn_second,
    )


def shards_fast(
    tokens,
    cotangent,
    lengths,
    slot_sequence,
    step_count,
    learn_rate,
    attention_in,
    attention_in_first,
    attention_in_second,
    attention_out,
    attention_out_first,
    attention_out_second,
    gate_up_weight,
    gate_up_first,
    gate_up_second,
    down_weight,
    down_first,
    down_second,
):
    _, rows, d = tokens.shape
    x = tokens.reshape(rows, d)
    cosine, sine = half_turns(rows, HD)
    owned, _, ff = gate_up_weight.shape
    tiles = ff // 128

    def tiled(value):
        value = value.reshape(owned, 2, tiles, 128).transpose(0, 2, 1, 3)
        return with_layout_constraint(value, rowwise).reshape(-1, 128)

    def untiled(value):
        value = with_layout_constraint(value.reshape(owned, tiles, 2, 128), rowwise)
        return value.transpose(0, 2, 1, 3).reshape(owned, 2, ff)

    heads = [value.transpose(1, 0, 2) for value in (attention_in, attention_in_first, attention_in_second)]
    gates = [tiled(value) for value in (gate_up_weight, gate_up_first, gate_up_second)]
    results = forward_call(x, cosine, sine, lengths, slot_sequence, heads[0], attention_out, gates[0], down_weight)
    full, saved = results[:4], results[4:]
    total, output, input_grad = backward_call(x, cotangent.reshape(rows, d), cosine, sine, lengths, slot_sequence, saved, full)
    steps_taken = step_count[0].astype(F32)
    scalars = jnp.stack([1.0 / (1.0 - beta_first**steps_taken), 1.0 / (1.0 - beta_second**steps_taken), learn_rate[0]])
    masters = heads + [attention_out, attention_out_first, attention_out_second] + gates + [down_weight, down_first, down_second]
    new = adam_call(scalars, total, masters)
    return (
        output.reshape(tokens.shape),
        input_grad.reshape(tokens.shape),
        *[value.transpose(1, 0, 2) for value in new[:4]],
        *new[4:8],
        *[untiled(value) for value in new[8:12]],
        *new[12:],
    )


def solution(mesh):
    fast = mesh.shape["rep"] == 4 and mesh.shape["shard"] == 8
    return jax.shard_map(
        shards_fast if fast else shards_generic,
        mesh=mesh,
        in_specs=(
            P(("rep", "shard"), None, None),
            P(("rep", "shard"), None, None),
            P(),
            P(("rep", "shard")),
            P(),
            P(),
            P("shard", None, None),
            P("shard", None, None),
            P("shard", None, None),
            P("shard", None),
            P("shard", None),
            P("shard", None),
            P("shard", None, None),
            P("shard", None, None),
            P("shard", None, None),
            P("shard", None),
            P("shard", None),
            P("shard", None),
        ),
        out_specs=(
            P(("rep", "shard"), None, None),
            P(("rep", "shard"), None, None),
            P("shard", None, None),
            P("shard", None, None),
            P("shard", None, None),
            P("shard", None, None),
            P("shard", None),
            P("shard", None),
            P("shard", None),
            P("shard", None),
            P("shard", None, None),
            P("shard", None, None),
            P("shard", None, None),
            P("shard", None, None),
            P("shard", None),
            P("shard", None),
            P("shard", None),
            P("shard", None),
        ),
        check_vma=False,
    )
```
